128 devices in a mesh: col: 16 (over z_lo, y, core), row: 8 (over z_hi, x).
Axes of the slice: x: 4, y: 4, z: 4 (z_hi: 2, z_lo: 2; z = z_hi * 2 + z_lo), core: 2. Of those that a mesh axis runs over, the one named last changes fastest.
Arguments:
- trace_start: float32 [32, 131072], P(None, ('col', 'row')), may hold values from -6 to 6
- surface_load: float32 [32, 131072], P(None, ('col', 'row')), may hold values from -6 to 6
- panel_tiles: bfloat16 [5504, 512, 512], P(('col', 'row')), may hold values from -0.015625 to 0.015625
- tile_list: int32 [5504], P(('col', 'row')), may hold values from -1 to 65535, as said below
- surf_map: int32 [32], replicated, may hold values from 0 to 31, as said below
- coef_index: int32 [4, 4, 32768], P(None, None, 'row'), may hold values from 0 to 15
- coef_table: float32 [16], replicated, may hold values from 0.2 to 2
- vol_source: float32 [4, 4, 32768], P(None, None, 'row'), may hold values from -6 to 6
Outputs:
- traces: float32 [32, 131072], P(None, ('col', 'row'))
- response: float32 [32, 131072], P(None, ('col', 'row'))
The draws below stay inside these ranges and needn't reach their ends.
Inputs may be any that keep to these rules, and one draw needn't show every extreme that they name: `tile_list`: each device has 43 slots, ordered by col index, then row index, then slot. A value i * 256 + j names the tile of rows i * 512 to (i + 1) * 512 - 1 and columns j * 512 to (j + 1) * 512 - 1 of the boundary matrix, with j <= i and j < 16; each such tile is named exactly once. A device of col index c and row index r names only tiles whose rows lie in shards of row index r (i * 512 // 1024 leaves remainder r modulo 8), and none if c >= 12; its named tiles fill its first slots and the rest hold -1. Some device names 43 tiles. surf_map[r * 4 + q] leaves remainder r modulo 8; each volume tile lies under exactly one surface tile.
All inputs are finite; a program needn't handle non-finite values.
Results may differ from the reference program's by a relative error of at most 0.0041.
Values may be sent and summed in bfloat16 or wider, within the bound.
No kernel may reach another device: no remote copies, remote signals or barrier semaphores. Data moves between devices by JAX's collectives and lax.ppermute only.
A program may use at most 128 MiB of HBM per device.

```python
import math
import jax
import jax.numpy as jnp
import numpy as np
from jax import lax

RHS = 32
NODES = 4096
TILE = 512
LAYERS = 4
ITERS = 2
SWEEPS = 4
COEFS = 16
VOL_COLS = 4
DENSE_COLS = 12
SURFACE = 131072
SHARD = 1024
WIN_TILES = 16
SIDE = 256
SLOTS_DEV = 43
SLOTS = 5504
SURF_TILES = 32
LINE = 32768
N_COL = 16
N_ROW = 8


def draw_tile_list(key, part):
    per_shard = SHARD // TILE
    slot_table = jnp.full((N_COL, N_ROW, SLOTS_DEV), -1, jnp.int32)
    for row_block in range(N_ROW):
        tile_names = []
        for tile_row in range(SIDE):
            if tile_row // per_shard % N_ROW == row_block:
                for tile_col in range(min(tile_row + 1, WIN_TILES)):
                    tile_names.append(tile_row * SIDE + tile_col)
        name_table = jnp.asarray(np.array(tile_names, dtype=np.int32))
        name_count = len(tile_names)
        key_order = jax.random.fold_in(key, 2 * row_block + 11)
        key_columns = jax.random.fold_in(key, 2 * row_block + 12)
        tile_order = jax.random.permutation(key_order, name_count)
        column_order = jax.random.permutation(key_columns, DENSE_COLS)
        placing = np.arange(name_count)
        slot_table = slot_table.at[column_order[placing % DENSE_COLS], row_block, placing // DENSE_COLS].set(name_table[tile_order])
    return slot_table.reshape(-1)


def draw_surf_map(key, part):
    pieces = []
    for row_block in range(N_ROW):
        order = jax.random.permutation(jax.random.fold_in(key, 101 + row_block), VOL_COLS).astype(jnp.int32)
        pieces.append(order * N_ROW + row_block)
    return jnp.concatenate(pieces)


def plant(values, rng, smallest, largest):
    spot = [jax.random.randint(jax.random.fold_in(rng, axis), (), 0, length) for axis, length in enumerate(values.shape)]
    longest = values.shape.index(max(values.shape))
    neighbour = spot[:longest] + [(spot[longest] + 1) % values.shape[longest]] + spot[longest + 1:]
    return values.at[tuple(spot)].set(smallest).at[tuple(neighbour)].set(largest)


def level_of(own_key, extent, split, low, high):
    def one(dim, parts):
        steps = jax.random.uniform(jax.random.fold_in(jax.random.fold_in(own_key, 6), dim), (parts,), jnp.float32, low / len(split), high / len(split))
        return jnp.repeat(jnp.exp(steps), extent[dim] // parts).reshape((-1,) + (1,) * (len(extent) - dim - 1))

    gain = one(*split[0])
    for cut in split[1:]:
        gain = gain * one(*cut)
    return gain


def scatter_about(own_key, extent, scale, bound, shards=(), held_as=jnp.bfloat16):
    factor_of = level_of(own_key, extent, shards, -0.22, 0.18) if shards else 1.0
    values = jax.random.normal(own_key, extent, jnp.float32) * scale * factor_of
    return jnp.minimum(jnp.maximum(values, -bound), bound).astype(held_as)


def setup_inputs(seed: int = 0) -> dict:
    key_list = jax.random.split(jax.random.key(seed), 9)
    trace_start = scatter_about(key_list[0], (RHS, SURFACE), 1.0, 6.0, ((1, 128),), jnp.float32)
    surface_load = scatter_about(key_list[1], (RHS, SURFACE), 1.0, 6.0, ((1, 128),), jnp.float32)
    panel_tiles = scatter_about(key_list[2], (SLOTS, TILE, TILE), SURFACE ** -0.5, 0.015625, ((0, 128),))
    tile_list = draw_tile_list(jax.random.fold_in(key_list[8], 71), 0)
    surf_map = draw_surf_map(jax.random.fold_in(key_list[8], 71), 0)
    coef_index = plant(jax.random.randint(key_list[5], (VOL_COLS, LAYERS, LINE), 0, COEFS), jax.random.fold_in(key_list[5], 1), 0, COEFS - 1).astype(jnp.int32)
    coef_table = jnp.clip(jnp.exp(jax.random.uniform(key_list[6], (COEFS,), jnp.float32, math.log(0.2), math.log(2.0))), 0.2, 2.0)
    vol_source = scatter_about(key_list[7], (VOL_COLS, LAYERS, LINE), 1.0, 6.0, ((2, 8),), jnp.float32)
    return {"trace_start": trace_start, "surface_load": surface_load, "panel_tiles": panel_tiles, "tile_list": tile_list, "surf_map": surf_map, "coef_index": coef_index, "coef_table": coef_table, "vol_source": vol_source}


COUPLING_STEP = 0.3
JACOBI_WEIGHT = 0.8
CELL_MASS = 0.05


def lookup_coefs(indices, coef_values):
    levels = jnp.arange(coef_values.shape[0], dtype=jnp.int32)
    return jnp.sum(jnp.where(indices[..., None] == levels, coef_values, 0.0), axis=-1)


def relax_line(padded_values, coefs_pad, source, top_trace):
    centre_coef = coefs_pad[:, 1:-1]
    left_weight = 0.5 * (centre_coef + coefs_pad[:, :-2])
    right_weight = 0.5 * (centre_coef + coefs_pad[:, 2:])
    layer_weight = 0.5 * (centre_coef[:-1] + centre_coef[1:])
    upper_weight = jnp.concatenate([centre_coef[:1], layer_weight], 0)
    lower_weight = jnp.concatenate([layer_weight, jnp.zeros_like(centre_coef[:1])], 0)
    centre = padded_values[:, :, 1:-1]
    upper_values = jnp.concatenate([top_trace[:, None, :], centre[:, :-1]], 1)
    lower_values = jnp.concatenate([centre[:, 1:], jnp.zeros_like(centre[:, :1])], 1)
    gathered = (left_weight * padded_values[:, :, :-2] + right_weight * padded_values[:, :, 2:]
                + upper_weight * upper_values + lower_weight * lower_values + source)
    diagonal = left_weight + right_weight + upper_weight + lower_weight + CELL_MASS
    return (1.0 - JACOBI_WEIGHT) * centre + JACOBI_WEIGHT * gathered / diagonal


def add_block(partial_value, block_sum, block_start):
    current = lax.dynamic_slice_in_dim(partial_value, block_start, TILE, 1)
    return lax.dynamic_update_slice_in_dim(partial_value, current + block_sum, block_start, 1)


def to_bands(values):
    return values.reshape(RHS, N_COL, N_ROW, SHARD).transpose(0, 2, 1, 3).reshape(RHS, SURFACE)


def from_bands(values):
    return values.reshape(RHS, N_ROW, N_COL, SHARD).transpose(0, 2, 1, 3).reshape(RHS, SURFACE)


def panel_product(whole_traces, panel_tiles, tile_list):
    def advance(partial_value, item):
        panel_block, tile_ident = item

        def accumulate(current):
            row_start = ((tile_ident // SIDE) * TILE).astype(jnp.int32)
            col_start = ((tile_ident % SIDE) * TILE).astype(jnp.int32)
            row_part = lax.dynamic_slice_in_dim(whole_traces, row_start, TILE, 1)
            col_part = lax.dynamic_slice_in_dim(whole_traces, col_start, TILE, 1)
            into_rows = lax.dot_general(col_part, panel_block, (((1,), (1,)), ((), ())),
                                        preferred_element_type=jnp.float32)
            into_cols = jnp.dot(row_part, panel_block, preferred_element_type=jnp.float32)
            current = add_block(current, into_rows, row_start)
            return add_block(current, into_cols, col_start)

        partial_value = lax.cond(tile_ident >= 0, accumulate, lambda current: current, partial_value)
        return partial_value, None

    start_sum = jnp.zeros((RHS, SURFACE), jnp.float32)
    result, _ = lax.scan(advance, start_sum, (panel_tiles, tile_list))
    return result


def reference(trace_start, surface_load, panel_tiles, tile_list, surf_map, coef_index, coef_table, vol_source):
    coef_lines = lookup_coefs(coef_index, coef_table)
    coef_padded = jnp.pad(coef_lines, ((0, 0), (0, 0), (1, 1)))
    inverse_map = jnp.zeros((SURF_TILES,), jnp.int32).at[surf_map].set(jnp.arange(SURF_TILES, dtype=jnp.int32))
    volume_states = [jnp.zeros((RHS, LAYERS, LINE), jnp.float32) for line_index in range(VOL_COLS)]
    traces = trace_start
    response = trace_start
    for iteration in range(ITERS):
        whole_traces = traces.astype(jnp.bfloat16)
        products = panel_product(whole_traces, panel_tiles, tile_list)
        surface_tiles = to_bands(whole_traces.astype(jnp.float32)).reshape(RHS, SURF_TILES, NODES)
        line_traces = surface_tiles[:, inverse_map].reshape(RHS, VOL_COLS, LINE)
        fluxes = []
        for line_index in range(VOL_COLS):
            top_trace = line_traces[:, line_index]
            volume_state = volume_states[line_index]
            for sweep_index in range(SWEEPS):
                padded_state = jnp.pad(volume_state, ((0, 0), (0, 0), (1, 1)))
                volume_state = relax_line(padded_state, coef_padded[line_index], vol_source[line_index], top_trace)
            volume_states[line_index] = volume_state
            fluxes.append(coef_lines[line_index, 0] * (top_trace - volume_state[:, 0]))
        flux_lines = jnp.stack(fluxes, 1).reshape(RHS, SURF_TILES, NODES)
        flux_surface = from_bands(flux_lines[:, surf_map].reshape(RHS, SURFACE))
        response = products + flux_surface
        traces = traces + COUPLING_STEP * (surface_load - traces - response)
    return traces, response
```

```python
import functools

import jax
import jax.numpy as jnp
from jax import lax
from jax.experimental import pallas as pl
from jax.experimental.pallas import tpu as pltpu
from jax.sharding import PartitionSpec as P

ITERS = 2
SWEEPS = 4
COUPLING_STEP = 0.3
JACOBI_WEIGHT = 0.8
CELL_MASS = 0.05

RHS = 32
TILE = 512
LANES = 128
N_COL = 16
N_ROW = 8
DENSE_COLS = 12
LAYERS = 4
SLOTS = 43
BAND_TILES = 32
WIN_TILES = 16
MID = 32
EXT = MID + 2
MIB = 1 << 20

VMEM = pl.BlockSpec(memory_space=pltpu.VMEM)
SMEM = pl.BlockSpec(memory_space=pltpu.SMEM)
ANY = pl.BlockSpec(memory_space=pl.ANY)
f32 = jnp.float32
bf16 = jnp.bfloat16


def exchange(x, axis):
    return lax.all_to_all(x, axis, 0, 0, tiled=True)


def put_everywhere(half_pair, out_ref, copies):
    for copy in range(copies):
        for half in range(2):
            out_ref[copy, half] = half_pair[half]


def start_body(trace_ref, out_ref):
    halves = [trace_ref[:, h * TILE : (h + 1) * TILE].astype(bf16) for h in range(2)]
    put_everywhere(halves, out_ref, N_COL)


def spread_start(trace_start):
    return pl.pallas_call(
        start_body,
        out_shape=jax.ShapeDtypeStruct((N_COL, 2, RHS, TILE), bf16),
        in_specs=[VMEM],
        out_specs=VMEM,
        name="spread_start",
    )(trace_start)


def row_body(scal_ref, band_ref, out_ref):
    halves = [band_ref[scal_ref[1]], band_ref[scal_ref[2]]]
    put_everywhere(halves, out_ref, N_ROW)


def spread_row(scal, band):
    return pl.pallas_call(
        row_body,
        out_shape=jax.ShapeDtypeStruct((N_ROW, 2, RHS, TILE), bf16),
        in_specs=[SMEM, VMEM],
        out_specs=VMEM,
        name="spread_row",
    )(scal, band)


def relax(scal_ref, band_ref, win_ref, coef_ref, state_ref, top_ref):
    first = scal_ref[3]
    row = scal_ref[4]
    before = jnp.maximum(row - 1, 0)
    after = jnp.minimum(row + 1, N_ROW - 1)
    top_ref[0] = win_ref[2 * before + 1, :, TILE - LANES :].astype(f32)
    top_ref[EXT - 1] = win_ref[2 * after, :, :LANES].astype(f32)
    for chunk in range(MID):
        lane = chunk % 4 * LANES
        top_ref[chunk + 1] = band_ref[first + chunk // 4, :, lane : lane + LANES].astype(f32)
    lane_id = lax.broadcasted_iota(jnp.int32, (RHS, LANES), 1)
    is_first = lane_id == 0
    is_last = lane_id == LANES - 1

    def sweep(source, target):
        def one_chunk(chunk, carry):
            top = top_ref[chunk]
            centre = [state_ref[source, chunk + 1, l] for l in range(LAYERS)]
            for l in range(LAYERS):
                prev = state_ref[source, chunk, l]
                nxt = state_ref[source, chunk + 2, l]
                left = pltpu.roll(jnp.where(is_last, prev, centre[l]), 1, 1)
                right = pltpu.roll(jnp.where(is_first, nxt, centre[l]), LANES - 1, 1)
                upper = top if l == 0 else centre[l - 1]
                value = (
                    (1.0 - JACOBI_WEIGHT) * centre[l]
                    + coef_ref[chunk, l : l + 1, :] * left
                    + coef_ref[chunk, 4 + l : 5 + l, :] * right
                    + coef_ref[chunk, 8 + l : 9 + l, :] * upper
                    + coef_ref[chunk, 16 + l : 17 + l, :]
                )
                if l + 1 < LAYERS:
                    value = value + coef_ref[chunk, 12 + l : 13 + l, :] * centre[l + 1]
                state_ref[target, chunk + 1, l] = value
            return carry

        lax.fori_loop(0, EXT, one_chunk, 0)

    for step in range(SWEEPS):
        sweep(step % 2, 1 - step % 2)


def work_body(
    first_iteration,
    ident_ref,
    scal_ref,
    band_ref,
    win_ref,
    coef_ref,
    panel_ref,
    *refs,
):
    if first_iteration:
        band_out, head_out, win_out, saved_ref = refs[:4]
        scratch = refs[4:]
    else:
        saved_ref, band_out, head_out, win_out = refs[:4]
        scratch = refs[4:]
    buffer_ref, band_acc, win_acc, state_ref, top_ref, panel_sems, state_sem = scratch
    is_volume = scal_ref[0] == 1

    def fetch(slot):
        return pltpu.make_async_copy(panel_ref.at[slot], buffer_ref.at[slot], panel_sems.at[slot])

    @pl.when(jnp.logical_not(is_volume))
    def _():
        def start(slot, carry):
            fetch(slot).start()
            return carry

        lax.fori_loop(0, SLOTS, start, 0)
        band_acc[...] = jnp.zeros_like(band_acc)
        win_acc[...] = jnp.zeros_like(win_acc)

        def one_tile(slot, carry):
            ident = ident_ref[slot]
            named = ident >= 0
            safe = jnp.maximum(ident, 0)
            row_tile = lax.shift_right_logical(safe, 8)
            col_tile = jnp.bitwise_and(safe, 15)
            band_tile = lax.shift_right_logical(row_tile, 4) * 2 + jnp.bitwise_and(row_tile, 1)
            band_to = jnp.where(named, band_tile, BAND_TILES)
            win_to = jnp.where(named, col_tile, WIN_TILES)
            fetch(slot).wait()
            panel = buffer_ref[slot]
            win_acc[win_to] += jnp.dot(band_ref[band_tile], panel, preferred_element_type=f32)
            band_acc[band_to] += lax.dot_general(
                win_ref[col_tile], panel, (((1,), (1,)), ((), ())), preferred_element_type=f32
            )
            return carry

        lax.fori_loop(0, SLOTS, one_tile, 0)
        band_out[...] = band_acc[:BAND_TILES].astype(bf16)
        head_out[...] = band_acc[:2]
        win_out[...] = win_acc[:WIN_TILES].astype(bf16)

    @pl.when(is_volume)
    def _():
        if first_iteration:
            state_ref[...] = jnp.zeros_like(state_ref)
        else:
            load = pltpu.make_async_copy(saved_ref, state_ref.at[0], state_sem)
            load.start()
            for guard in (0, EXT + 1):
                state_ref[1, guard] = jnp.zeros((LAYERS, RHS, LANES), f32)
            load.wait()
        relax(scal_ref, band_ref, win_ref, coef_ref, state_ref, top_ref)
        band_out[...] = jnp.zeros_like(band_out)
        head_out[...] = jnp.zeros_like(head_out)
        win_out[...] = jnp.zeros_like(win_out)
        first = scal_ref[3]
        for chunk in range(MID):
            lane = chunk % 4 * LANES
            flux = coef_ref[chunk + 1, 20:21, :] * (top_ref[chunk + 1] - state_ref[0, chunk + 2, 0])
            band_out[first + chunk // 4, :, lane : lane + LANES] = flux.astype(bf16)

            @pl.when(first + chunk // 4 < 2)
            def _():
                head_out[first + chunk // 4, :, lane : lane + LANES] = flux

        if first_iteration:
            save = pltpu.make_async_copy(state_ref.at[0], saved_ref, state_sem)
            save.start()
            save.wait()


def work(ident, scal, band, win, coefs, panel, saved):
    first_iteration = saved is None
    outs = [
        jax.ShapeDtypeStruct((BAND_TILES, RHS, TILE), bf16),
        jax.ShapeDtypeStruct((2, RHS, TILE), f32),
        jax.ShapeDtypeStruct((WIN_TILES, RHS, TILE), bf16),
    ]
    out_specs = [VMEM, VMEM, VMEM]
    in_specs = [SMEM, SMEM, VMEM, VMEM, VMEM, ANY]
    args = [ident, scal, band, win, coefs, panel]
    state = jax.ShapeDtypeStruct((EXT + 2, LAYERS, RHS, LANES), f32)
    if first_iteration:
        outs.append(state)
        out_specs.append(ANY)
    else:
        in_specs.append(ANY)
        args.append(saved)
    return pl.pallas_call(
        functools.partial(work_body, first_iteration),
        out_shape=outs,
        in_specs=in_specs,
        out_specs=out_specs,
        scratch_shapes=[
            pltpu.VMEM((SLOTS, TILE, TILE), bf16),
            pltpu.VMEM((BAND_TILES + 1, RHS, TILE), f32),
            pltpu.VMEM((WIN_TILES + 1, RHS, TILE), f32),
            pltpu.VMEM((2, EXT + 2, LAYERS, RHS, LANES), f32),
            pltpu.VMEM((EXT, RHS, LANES), f32),
            pltpu.SemaphoreType.DMA((SLOTS,)),
            pltpu.SemaphoreType.DMA(()),
        ],
        compiler_params=pltpu.CompilerParams(vmem_limit_bytes=46 * MIB),
        name="work_first" if first_iteration else "work_next",
    )(*args)


def head_body(parts_ref, head_ref, band_ref, out_ref):
    total = head_ref[...]
    for peer in range(N_ROW):
        total = total + parts_ref[peer].astype(f32)
    out_ref[0] = total.astype(bf16)


def add_head(parts, head, band):
    return pl.pallas_call(
        head_body,
        grid=(1,),
        out_shape=jax.ShapeDtypeStruct((N_COL, 2, RHS, TILE), bf16),
        in_specs=[
            pl.BlockSpec((N_ROW, 2, RHS, TILE), lambda i: (0, 0, 0, 0)),
            pl.BlockSpec((2, RHS, TILE), lambda i: (0, 0, 0)),
            ANY,
        ],
        out_specs=pl.BlockSpec((1, 2, RHS, TILE), lambda i: (0, 0, 0, 0)),
        input_output_aliases={2: 0},
        name="add_head",
    )(parts, head, band)


def update_body(last, parts_ref, trace_ref, load_ref, *outs):
    for half in range(2):
        lanes = slice(half * TILE, (half + 1) * TILE)
        total = parts_ref[0, half].astype(f32)
        for peer in range(1, N_COL):
            total = total + parts_ref[peer, half].astype(f32)
        trace = trace_ref[:, lanes]
        trace = trace + COUPLING_STEP * (load_ref[:, lanes] - trace - total)
        outs[0][:, lanes] = trace
        if last:
            outs[1][:, lanes] = total
        else:
            rounded = trace.astype(bf16)
            for copy in range(N_COL):
                outs[1][copy, half] = rounded


def update(parts, traces, load, last):
    whole = jax.ShapeDtypeStruct(traces.shape, f32)
    return pl.pallas_call(
        functools.partial(update_body, last),
        out_shape=[whole, whole if last else jax.ShapeDtypeStruct(parts.shape, bf16)],
        in_specs=[VMEM, VMEM, VMEM],
        out_specs=[VMEM, VMEM],
        name="update_last" if last else "update_next",
    )(parts, traces, load)


def volume_weights(coef_index, coef_table, vol_source, volume_line, row_index):
    indices = lax.dynamic_index_in_dim(coef_index, volume_line, 0, keepdims=False)
    source = lax.dynamic_index_in_dim(vol_source, volume_line, 0, keepdims=False)
    levels = jnp.arange(coef_table.shape[0], dtype=jnp.int32)
    k = jnp.sum(jnp.where(indices[..., None] == levels, coef_table, 0.0), axis=-1)
    both = jnp.concatenate([k, source], 0)
    up = [(i, i + 1) for i in range(N_ROW - 1)]
    down = [(i + 1, i) for i in range(N_ROW - 1)]
    before = lax.ppermute(both[:, -LANES:], "row", up)
    after = lax.ppermute(both[:, :LANES], "row", down)
    both = jnp.concatenate([before, both, after], 1)
    k, source = both[:LAYERS], both[LAYERS:]
    wide = jnp.pad(k, ((0, 0), (1, 1)))
    left = 0.5 * (k + wide[:, :-2])
    right = 0.5 * (k + wide[:, 2:])
    between = 0.5 * (k[:-1] + k[1:])
    upper = jnp.concatenate([k[:1], between], 0)
    lower = jnp.concatenate([between, jnp.zeros_like(k[:1])], 0)
    node = jnp.arange(k.shape[1], dtype=jnp.int32) - LANES
    inside = ((node >= 0) | (row_index > 0)) & ((node < MID * LANES) | (row_index < N_ROW - 1))
    scale = jnp.where(inside, JACOBI_WEIGHT / (left + right + upper + lower + CELL_MASS), 0.0)
    rows = jnp.concatenate(
        [left * scale, right * scale, upper * scale, lower * scale, source * scale, k], 0
    )
    return rows.reshape(24, EXT, LANES).transpose(1, 0, 2)


def local(
    trace_start, surface_load, panel_tiles, tile_list, surf_map, coef_index, coef_table, vol_source
):
    col_index = lax.axis_index("col")
    row_index = lax.axis_index("row")
    volume_line = jnp.maximum(col_index - DENSE_COLS, 0)
    is_volume = col_index >= DENSE_COLS
    volume_tile = volume_line * N_ROW + row_index
    tile_numbers = jnp.arange(surf_map.shape[0], dtype=jnp.int32)
    quarter = jnp.sum(jnp.where(surf_map == volume_tile, tile_numbers, 0)) % 4
    first = quarter * 8
    scal = jnp.stack(
        [
            is_volume.astype(jnp.int32),
            jnp.where(is_volume, first, 0),
            jnp.where(is_volume, first + 7, 1),
            first,
            row_index,
        ]
    ).astype(jnp.int32)
    traces = trace_start
    spread = spread_start(traces)
    coefs = volume_weights(coef_index, coef_table, vol_source, volume_line, row_index)
    saved = None
    for iteration in range(ITERS):
        last = iteration == ITERS - 1
        band = exchange(spread, "col").reshape(BAND_TILES, RHS, TILE)
        win = exchange(spread_row(scal, band), "row").reshape(WIN_TILES, RHS, TILE)
        made = work(tile_list, scal, band, win, coefs, panel_tiles, saved)
        band_part, head, win_part = made[:3]
        saved = None if last else made[3]
        win_parts = exchange(win_part.reshape(N_ROW, 2, RHS, TILE), "row")
        band_part = add_head(win_parts, head, band_part.reshape(N_COL, 2, RHS, TILE))
        traces, spread = update(exchange(band_part, "col"), traces, surface_load, last)
    return (traces, spread)


def solution(mesh):
    return jax.shard_map(
        local,
        mesh=mesh,
        in_specs=(
            P(None, ("col", "row")),
            P(None, ("col", "row")),
            P(("col", "row"), None, None),
            P(("col", "row")),
            P(),
            P(None, None, "row"),
            P(),
            P(None, None, "row"),
        ),
        out_specs=(P(None, ("col", "row")), P(None, ("col", "row"))),
        check_vma=False,
    )
```

```python
import functools

import jax
import jax.numpy as jnp
from jax import lax
from jax.experimental import pallas as pl
from jax.experimental.pallas import tpu as pltpu
from jax.sharding import PartitionSpec as P

ITERS = 2
SWEEPS = 4
COUPLING_STEP = 0.3
JACOBI_WEIGHT = 0.8
CELL_MASS = 0.05

RHS = 32
TILE = 512
LANES = 128
N_COL = 16
N_ROW = 8
DENSE_COLS = 12
LAYERS = 4
SLOTS = 43
GROUP = 4
COEFS = 16
BAND_TILES = 32
WIN_TILES = 16
MID = 32
EXT = MID + 2
MIB = 1 << 20

VMEM = pl.BlockSpec(memory_space=pltpu.VMEM)
SMEM = pl.BlockSpec(memory_space=pltpu.SMEM)
ANY = pl.BlockSpec(memory_space=pl.ANY)
f32 = jnp.float32
bf16 = jnp.bfloat16


def exchange(x, axis):
    return lax.all_to_all(x, axis, 0, 0, tiled=True)


def put_everywhere(half_pair, out_ref, copies):
    for copy in range(copies):
        for half in range(2):
            out_ref[copy, half] = half_pair[half]


def start_body(trace_ref, out_ref):
    halves = [trace_ref[:, h * TILE : (h + 1) * TILE].astype(bf16) for h in range(2)]
    put_everywhere(halves, out_ref, N_COL)


def spread_start(trace_start):
    return pl.pallas_call(
        start_body,
        out_shape=jax.ShapeDtypeStruct((N_COL, 2, RHS, TILE), bf16),
        in_specs=[VMEM],
        out_specs=VMEM,
        compiler_params=pltpu.CompilerParams(vmem_limit_bytes=6 * MIB),
        name="spread_start",
    )(trace_start)


def row_body(first_iteration, scal_ref, band_ref, *refs):
    out_ref = refs[-1]
    halves = [band_ref[scal_ref[1]], band_ref[scal_ref[2]]]
    put_everywhere(halves, out_ref, N_ROW)
    if first_iteration:

        @pl.when(scal_ref[0] == 1)
        def _():
            for peer in range(N_ROW):
                out_ref[peer, 0, :, LANES : 3 * LANES] = refs[0][...]


def spread_row(scal, band, edges):
    first_iteration = edges is not None
    args = [scal, band] + ([edges] if first_iteration else [])
    return pl.pallas_call(
        functools.partial(row_body, first_iteration),
        out_shape=jax.ShapeDtypeStruct((N_ROW, 2, RHS, TILE), bf16),
        in_specs=[SMEM] + [VMEM] * (len(args) - 1),
        out_specs=VMEM,
        compiler_params=pltpu.CompilerParams(vmem_limit_bytes=6 * MIB),
        name="spread_row",
    )(*args)


def for_slots(ident_ref, panel_ref, buffer_ref, sems, do_slot):
    def fetch(slot):
        return pltpu.make_async_copy(panel_ref.at[slot], buffer_ref.at[slot], sems.at[slot])

    def start(slot, carry):
        fetch(slot).start()
        return carry

    lax.fori_loop(0, SLOTS, start, 0)

    def place(slot):
        ident = ident_ref[slot]
        named = ident >= 0
        safe = jnp.maximum(ident, 0)
        row_tile = lax.shift_right_logical(safe, 8)
        col_tile = jnp.bitwise_and(safe, 15)
        band_tile = lax.shift_right_logical(row_tile, 4) * 2 + jnp.bitwise_and(row_tile, 1)
        do_slot(slot, named, band_tile, col_tile)

    def group(index, carry):
        for extra in range(GROUP):
            fetch(index * GROUP + extra).wait()
        for extra in range(GROUP):
            place(index * GROUP + extra)
        return carry

    lax.fori_loop(0, SLOTS // GROUP, group, 0)
    for slot in range(SLOTS // GROUP * GROUP, SLOTS):
        fetch(slot).wait()
        place(slot)


def window_body(ident_ref, scal_ref, band_ref, panel_ref, win_out, win_acc, buffer_ref, sems):
    win_acc[...] = jnp.zeros_like(win_acc)

    @pl.when(scal_ref[0] == 0)
    def _():
        def one_slot(slot, named, band_tile, col_tile):
            win_acc[jnp.where(named, col_tile, WIN_TILES)] += jnp.dot(
                band_ref[band_tile], buffer_ref[slot], preferred_element_type=f32
            )

        for_slots(ident_ref, panel_ref, buffer_ref, sems, one_slot)

    win_out[...] = win_acc[:WIN_TILES].astype(bf16)


def into_window(ident, scal, band, panel):
    return pl.pallas_call(
        window_body,
        out_shape=jax.ShapeDtypeStruct((WIN_TILES, RHS, TILE), bf16),
        in_specs=[SMEM, SMEM, VMEM, ANY],
        out_specs=VMEM,
        scratch_shapes=[
            pltpu.VMEM((WIN_TILES + 1, RHS, TILE), f32),
            pltpu.VMEM((SLOTS, TILE, TILE), bf16),
            pltpu.SemaphoreType.DMA((SLOTS,)),
        ],
        compiler_params=pltpu.CompilerParams(vmem_limit_bytes=44 * MIB),
        cost_estimate=pl.CostEstimate(flops=7 * 10**8, transcendentals=0, bytes_accessed=25 * 10**6),
        name="into_window",
    )(ident, scal, band, panel)


def weigh(scal_ref, table_ref, cells_ref, win_ref, cell_ref, coef_ref):
    row = scal_ref[4]
    before = jnp.maximum(row - 1, 0)
    after = jnp.minimum(row + 1, N_ROW - 1)
    layer = lax.broadcasted_iota(jnp.int32, (8, LANES), 0)
    lane = lax.broadcasted_iota(jnp.int32, (8, LANES), 1)
    nothing = jnp.zeros((8, LANES), f32)
    for chunk, source, start, here in (
        (0, 2 * before, 2 * LANES, row > 0),
        (EXT - 1, 2 * after, LANES, row < N_ROW - 1),
    ):
        sent = win_ref[source, :, start : start + LANES].astype(f32)
        k = nothing
        for level in range(COEFS):
            k = jnp.where(sent[0:8] == float(level), table_ref[level], k)
        cell_ref[chunk + 1, 0] = jnp.where((layer < LAYERS) & here, k, 0.0)
        cell_ref[chunk + 1, 1] = jnp.where(here, sent[8:16] + sent[16:24], 0.0)
    cell_ref[0, 0] = nothing
    cell_ref[EXT + 1, 0] = nothing

    for chunk in range(MID):
        cell_ref[chunk + 2] = cells_ref[chunk]

    def one_chunk(chunk, carry):
        k = cell_ref[chunk + 1, 0]
        left = pltpu.roll(jnp.where(lane == LANES - 1, cell_ref[chunk, 0], k), 1, 1)
        right = pltpu.roll(jnp.where(lane == 0, cell_ref[chunk + 2, 0], k), LANES - 1, 1)
        left = 0.5 * (k + left)
        right = 0.5 * (k + right)
        lower = jnp.where(layer < LAYERS - 1, 0.5 * (k + pltpu.roll(k, 7, 0)), 0.0)
        upper = jnp.where(layer == 0, k, pltpu.roll(lower, 1, 0))
        inside = ((chunk > 0) | (row > 0)) & ((chunk < EXT - 1) | (row < N_ROW - 1))
        scale = jnp.where(inside, JACOBI_WEIGHT / (left + right + upper + lower + CELL_MASS), 0.0)
        coef_ref[chunk, 0:8] = left * scale
        coef_ref[chunk, 8:16] = right * scale
        coef_ref[chunk, 16:24] = upper * scale
        coef_ref[chunk, 24:32] = lower * scale
        coef_ref[chunk, 32:40] = cell_ref[chunk + 1, 1] * scale
        coef_ref[chunk, 40:48] = k
        return carry

    lax.fori_loop(0, EXT, one_chunk, 0, unroll=2)


def relax(scal_ref, band_ref, win_ref, coef_ref, states, top_ref):
    first = scal_ref[3]
    row = scal_ref[4]
    before = jnp.maximum(row - 1, 0)
    after = jnp.minimum(row + 1, N_ROW - 1)
    top_ref[0] = win_ref[2 * before + 1, :, TILE - LANES :].astype(f32)
    top_ref[EXT - 1] = win_ref[2 * after, :, :LANES].astype(f32)
    for chunk in range(MID):
        start = chunk % 4 * LANES
        top_ref[chunk + 1] = band_ref[first + chunk // 4, :, start : start + LANES].astype(f32)
    lane = lax.broadcasted_iota(jnp.int32, (RHS, LANES), 1)
    is_first = lane == 0
    is_last = lane == LANES - 1

    def sweep(source_ref, target_ref):
        def one_chunk(chunk, carry):
            upper = top_ref[chunk]
            centre = source_ref[chunk + 1, 0]
            for l in range(LAYERS):
                left = pltpu.roll(jnp.where(is_last, source_ref[chunk, l], centre), 1, 1)
                right = pltpu.roll(jnp.where(is_first, source_ref[chunk + 2, l], centre), LANES - 1, 1)
                value = (
                    (1.0 - JACOBI_WEIGHT) * centre
                    + coef_ref[chunk, l : l + 1, :] * left
                    + coef_ref[chunk, 8 + l : 9 + l, :] * right
                    + coef_ref[chunk, 16 + l : 17 + l, :] * upper
                    + coef_ref[chunk, 32 + l : 33 + l, :]
                )
                if l + 1 < LAYERS:
                    below = source_ref[chunk + 1, l + 1]
                    value = value + coef_ref[chunk, 24 + l : 25 + l, :] * below
                    upper, centre = centre, below
                target_ref[chunk + 1, l] = value
            return carry

        lax.fori_loop(0, EXT, one_chunk, 0, unroll=2)

    for step in range(SWEEPS):
        sweep(states[step % 2], states[1 - step % 2])


def rows_body(first_iteration, ident_ref, scal_ref, band_ref, win_ref, panel_ref, *refs):
    if first_iteration:
        table_ref, cells_ref, band_out, head_out, state_out, coef_out = refs[:6]
        refs = refs[6:]
    else:
        state_in, coef_in, band_out, head_out = refs[:4]
        refs = refs[4:]
    band_acc, state_a, state_b, coef_ref, cell_ref, top_ref, sems, buffer_ref, panel_sems = refs
    is_volume = scal_ref[0] == 1

    @pl.when(jnp.logical_not(is_volume))
    def _():
        band_acc[...] = jnp.zeros_like(band_acc)

        def one_slot(slot, named, band_tile, col_tile):
            band_acc[jnp.where(named, band_tile, BAND_TILES)] += lax.dot_general(
                win_ref[col_tile],
                buffer_ref[slot],
                (((1,), (1,)), ((), ())),
                preferred_element_type=f32,
            )

        for_slots(ident_ref, panel_ref, buffer_ref, panel_sems, one_slot)
        band_out[...] = band_acc[:BAND_TILES].astype(bf16)
        head_out[...] = band_acc[:2]

    @pl.when(is_volume)
    def _():
        guard = jnp.zeros((LAYERS, RHS, LANES), f32)
        state_b[0] = guard
        state_b[EXT + 1] = guard
        if first_iteration:
            state_a[...] = jnp.zeros_like(state_a)
            weigh(scal_ref, table_ref, cells_ref, win_ref, cell_ref, coef_ref)
        else:
            loads = [
                pltpu.make_async_copy(state_in, state_a, sems.at[0]),
                pltpu.make_async_copy(coef_in, coef_ref, sems.at[1]),
            ]
            for load in loads:
                load.start()
            for load in loads:
                load.wait()
        relax(scal_ref, band_ref, win_ref, coef_ref, (state_a, state_b), top_ref)
        if first_iteration:
            saves = [
                pltpu.make_async_copy(state_a, state_out, sems.at[0]),
                pltpu.make_async_copy(coef_ref, coef_out, sems.at[1]),
            ]
            for save in saves:
                save.start()
        band_out[...] = jnp.zeros_like(band_out)
        head_out[...] = jnp.zeros_like(head_out)
        first = scal_ref[3]
        for chunk in range(MID):
            start = chunk % 4 * LANES
            flux = coef_ref[chunk + 1, 40:41, :] * (top_ref[chunk + 1] - state_a[chunk + 2, 0])
            band_out[first + chunk // 4, :, start : start + LANES] = flux.astype(bf16)
            if chunk < 8:

                @pl.when(first == 0)
                def _():
                    head_out[chunk // 4, :, start : start + LANES] = flux

        if first_iteration:
            for save in saves:
                save.wait()


def into_rows(ident, scal, band, win, panel, table, cells, saved):
    first_iteration = saved is None
    outs = [
        jax.ShapeDtypeStruct((BAND_TILES, RHS, TILE), bf16),
        jax.ShapeDtypeStruct((2, RHS, TILE), f32),
    ]
    out_specs = [VMEM, VMEM]
    in_specs = [SMEM, SMEM, VMEM, VMEM, ANY]
    args = [ident, scal, band, win, panel]
    state = (EXT + 2, LAYERS, RHS, LANES)
    coefs = (EXT, 48, LANES)
    if first_iteration:
        outs += [jax.ShapeDtypeStruct(state, f32), jax.ShapeDtypeStruct(coefs, f32)]
        out_specs += [ANY, ANY]
        in_specs += [SMEM, VMEM]
        args += [table, cells]
    else:
        in_specs += [ANY, ANY]
        args += saved
    return pl.pallas_call(
        functools.partial(rows_body, first_iteration),
        out_shape=outs,
        in_specs=in_specs,
        out_specs=out_specs,
        scratch_shapes=[
            pltpu.VMEM((BAND_TILES + 1, RHS, TILE), f32),
            pltpu.VMEM(state, f32),
            pltpu.VMEM(state, f32),
            pltpu.VMEM(coefs, f32),
            pltpu.VMEM((EXT + 2, 2, 8, LANES), f32),
            pltpu.VMEM((EXT, RHS, LANES), f32),
            pltpu.SemaphoreType.DMA((2,)),
            pltpu.VMEM((SLOTS, TILE, TILE), bf16),
            pltpu.SemaphoreType.DMA((SLOTS,)),
        ],
        compiler_params=pltpu.CompilerParams(vmem_limit_bytes=44 * MIB),
        cost_estimate=pl.CostEstimate(flops=7 * 10**8, transcendentals=0, bytes_accessed=30 * 10**6),
        name="into_rows_first" if first_iteration else "into_rows_next",
    )(*args)


def head_body(parts_ref, head_ref, band_ref, out_ref):
    total = head_ref[...]
    for peer in range(N_ROW):
        total = total + parts_ref[peer].astype(f32)
    out_ref[0] = total.astype(bf16)


def add_head(parts, head, band):
    return pl.pallas_call(
        head_body,
        grid=(1,),
        out_shape=jax.ShapeDtypeStruct((N_COL, 2, RHS, TILE), bf16),
        in_specs=[
            pl.BlockSpec((N_ROW, 2, RHS, TILE), lambda i: (0, 0, 0, 0)),
            pl.BlockSpec((2, RHS, TILE), lambda i: (0, 0, 0)),
            ANY,
        ],
        out_specs=pl.BlockSpec((1, 2, RHS, TILE), lambda i: (0, 0, 0, 0)),
        input_output_aliases={2: 0},
        compiler_params=pltpu.CompilerParams(vmem_limit_bytes=6 * MIB),
        name="add_head",
    )(parts, head, band)


def update_body(last, parts_ref, trace_ref, load_ref, *outs):
    for half in range(2):
        lanes = slice(half * TILE, (half + 1) * TILE)
        total = parts_ref[0, half].astype(f32)
        for peer in range(1, N_COL):
            total = total + parts_ref[peer, half].astype(f32)
        trace = trace_ref[:, lanes]
        trace = trace + COUPLING_STEP * (load_ref[:, lanes] - trace - total)
        outs[0][:, lanes] = trace
        if last:
            outs[1][:, lanes] = total
        else:
            rounded = trace.astype(bf16)
            for copy in range(N_COL):
                outs[1][copy, half] = rounded


def update(parts, traces, load, last):
    whole = jax.ShapeDtypeStruct(traces.shape, f32)
    return pl.pallas_call(
        functools.partial(update_body, last),
        out_shape=[whole, whole if last else jax.ShapeDtypeStruct(parts.shape, bf16)],
        in_specs=[VMEM, VMEM, VMEM],
        out_specs=[VMEM, VMEM],
        compiler_params=pltpu.CompilerParams(vmem_limit_bytes=8 * MIB),
        name="update_last" if last else "update_next",
    )(parts, traces, load)


def lookup(indices, table):
    levels = jnp.arange(table.shape[0], dtype=jnp.int32)
    return jnp.sum(jnp.where(indices[..., None] == levels, table, 0.0), axis=-1)


def volume_cells(coef_index, coef_table, vol_source, volume_line):
    indices = lax.dynamic_index_in_dim(coef_index, volume_line, 0, keepdims=False)
    source = lax.dynamic_index_in_dim(vol_source, volume_line, 0, keepdims=False)
    spare = ((0, 0), (0, 8 - LAYERS), (0, 0), (0, 0))
    cells = jnp.stack([lookup(indices, coef_table), source]).reshape(2, LAYERS, MID, LANES)
    cells = jnp.pad(cells, spare).transpose(2, 0, 1, 3)

    def ends(x):
        return jnp.concatenate([x[:, :LANES], x[:, -LANES:]], 1)

    high = ends(source).astype(bf16)
    low = (ends(source) - high.astype(f32)).astype(bf16)
    edges = [jnp.pad(e, ((0, 4), (0, 0))) for e in (ends(indices).astype(bf16), high, low)]
    return cells, jnp.pad(jnp.concatenate(edges, 0), ((0, 8), (0, 0)))


def local(
    trace_start, surface_load, panel_tiles, tile_list, surf_map, coef_index, coef_table, vol_source
):
    col_index = lax.axis_index("col")
    row_index = lax.axis_index("row")
    volume_line = jnp.maximum(col_index - DENSE_COLS, 0)
    is_volume = col_index >= DENSE_COLS
    volume_tile = volume_line * N_ROW + row_index
    tile_numbers = jnp.arange(surf_map.shape[0], dtype=jnp.int32)
    quarter = jnp.sum(jnp.where(surf_map == volume_tile, tile_numbers, 0)) % 4
    first = quarter * 8
    scal = jnp.stack(
        [
            is_volume.astype(jnp.int32),
            jnp.where(is_volume, first, 0),
            jnp.where(is_volume, first + 7, 1),
            first,
            row_index,
        ]
    ).astype(jnp.int32)
    traces = trace_start
    spread = spread_start(traces)
    cells, edges = volume_cells(coef_index, coef_table, vol_source, volume_line)
    panel = panel_tiles
    saved = None
    for iteration in range(ITERS):
        last = iteration == ITERS - 1
        band = exchange(spread, "col").reshape(BAND_TILES, RHS, TILE)
        row_spread = spread_row(scal, band, edges if iteration == 0 else None)
        win = exchange(row_spread, "row").reshape(WIN_TILES, RHS, TILE)
        win_part = into_window(tile_list, scal, band, panel)
        win_parts = exchange(win_part.reshape(N_ROW, 2, RHS, TILE), "row")
        made = into_rows(tile_list, scal, band, win, panel, coef_table, cells, saved)
        band_part, head = made[:2]
        saved = made[2:]
        band_part = add_head(win_parts, head, band_part.reshape(N_COL, 2, RHS, TILE))
        traces, spread = update(exchange(band_part, "col"), traces, surface_load, last)
    return (traces, spread)


def solution(mesh):
    return jax.shard_map(
        local,
        mesh=mesh,
        in_specs=(
            P(None, ("col", "row")),
            P(None, ("col", "row")),
            P(("col", "row"), None, None),
            P(("col", "row")),
            P(),
            P(None, None, "row"),
            P(),
            P(None, None, "row"),
        ),
        out_specs=(P(None, ("col", "row")), P(None, ("col", "row"))),
        check_vma=False,
    )
```

```python
import functools

import jax
import jax.numpy as jnp
from jax import lax
from jax.experimental import pallas as pl
from jax.experimental.pallas import tpu as pltpu
from jax.sharding import PartitionSpec as P

ITERS = 2
SWEEPS = 4
COUPLING_STEP = 0.3
JACOBI_WEIGHT = 0.8
CELL_MASS = 0.05

RHS = 32
TILE = 512
LANES = 128
N_COL = 16
N_ROW = 8
DENSE_COLS = 12
LAYERS = 4
SLOTS = 43
GROUP = 4
UNROLL = 17
COEFS = 16
BAND_TILES = 32
WIN_TILES = 16
MID = 32
EXT = MID + 2
MIB = 1 << 20

VMEM = pl.BlockSpec(memory_space=pltpu.VMEM)
SMEM = pl.BlockSpec(memory_space=pltpu.SMEM)
ANY = pl.BlockSpec(memory_space=pl.ANY)
f32 = jnp.float32
bf16 = jnp.bfloat16


def in_hbm(x):
    return pltpu.with_memory_space_constraint(x, pltpu.HBM)


def exchange(x, axis):
    return lax.all_to_all(x, axis, 0, 0, tiled=True)


def put_everywhere(half_pair, out_ref, copies):
    for copy in range(copies):
        for half in range(2):
            out_ref[copy, half] = half_pair[half]


def start_body(trace_ref, out_ref):
    halves = [trace_ref[:, h * TILE : (h + 1) * TILE].astype(bf16) for h in range(2)]
    put_everywhere(halves, out_ref, N_COL)


def spread_start(trace_start):
    return pl.pallas_call(
        start_body,
        out_shape=jax.ShapeDtypeStruct((N_COL, 2, RHS, TILE), bf16),
        in_specs=[VMEM],
        out_specs=VMEM,
        compiler_params=pltpu.CompilerParams(vmem_limit_bytes=6 * MIB),
        name="spread_start",
    )(trace_start)


def row_body(first_iteration, scal_ref, band_ref, *refs):
    out_ref = refs[-1]
    halves = [band_ref[scal_ref[SLOTS + 1]], band_ref[scal_ref[SLOTS + 2]]]
    put_everywhere(halves, out_ref, N_ROW)
    if first_iteration:

        @pl.when(scal_ref[SLOTS] == 1)
        def _():
            for peer in range(N_ROW):
                out_ref[peer, 0, :, LANES : 3 * LANES] = refs[0][...]


def spread_row(scal, band, edges):
    first_iteration = edges is not None
    args = [scal, band] + ([edges] if first_iteration else [])
    return pl.pallas_call(
        functools.partial(row_body, first_iteration),
        out_shape=jax.ShapeDtypeStruct((N_ROW, 2, RHS, TILE), bf16),
        in_specs=[SMEM] + [VMEM] * (len(args) - 1),
        out_specs=VMEM,
        compiler_params=pltpu.CompilerParams(vmem_limit_bytes=6 * MIB),
        name="spread_row",
    )(*args)


def for_slots(scal_ref, panel_ref, buffer_ref, sems, acc_ref, do_slot):
    def fetch(slot):
        return pltpu.make_async_copy(panel_ref.at[slot], buffer_ref.at[slot], sems.at[slot])

    def start(slot, carry):
        fetch(slot).start()
        return carry

    lax.fori_loop(0, SLOTS, start, 0)
    acc_ref[...] = jnp.zeros_like(acc_ref)

    def place(slot):
        ident = scal_ref[slot]
        named = ident >= 0
        safe = jnp.maximum(ident, 0)
        row_tile = lax.shift_right_logical(safe, 8)
        col_tile = jnp.bitwise_and(safe, 15)
        band_tile = lax.shift_right_logical(row_tile, 4) * 2 + jnp.bitwise_and(row_tile, 1)
        do_slot(slot, named, band_tile, col_tile)

    def group(index, carry):
        for extra in range(GROUP):
            fetch(index * GROUP + extra).wait()
        for extra in range(GROUP):
            place(index * GROUP + extra)
        return carry

    lax.fori_loop(0, SLOTS // GROUP, group, 0)
    for slot in range(SLOTS // GROUP * GROUP, SLOTS):
        fetch(slot).wait()
        place(slot)


def window_body(scal_ref, band_ref, panel_ref, win_out, win_acc, buffer_ref, sems):
    is_volume = scal_ref[SLOTS] == 1

    @pl.when(jnp.logical_not(is_volume))
    def _():
        def one_slot(slot, named, band_tile, col_tile):
            win_acc[jnp.where(named, col_tile, WIN_TILES)] += jnp.dot(
                band_ref[band_tile], buffer_ref[slot], preferred_element_type=f32
            )

        for_slots(scal_ref, panel_ref, buffer_ref, sems, win_acc, one_slot)

        win_out[...] = win_acc[:WIN_TILES].astype(bf16)

    @pl.when(is_volume)
    def _():
        win_out[...] = jnp.zeros_like(win_out)


def into_window(scal, band, panel):
    return pl.pallas_call(
        window_body,
        out_shape=jax.ShapeDtypeStruct((WIN_TILES, RHS, TILE), bf16),
        in_specs=[SMEM, VMEM, ANY],
        out_specs=VMEM,
        scratch_shapes=[
            pltpu.VMEM((WIN_TILES + 1, RHS, TILE), f32),
            pltpu.VMEM((SLOTS, TILE, TILE), bf16),
            pltpu.SemaphoreType.DMA((SLOTS,)),
        ],
        compiler_params=pltpu.CompilerParams(vmem_limit_bytes=44 * MIB),
        cost_estimate=pl.CostEstimate(flops=7 * 10**8, transcendentals=0, bytes_accessed=25 * 10**6),
        name="into_window",
    )(scal, band, panel)


def weigh(scal_ref, table_ref, cells_ref, win_ref, cell_ref, coef_ref):
    row = scal_ref[SLOTS + 4]
    before = jnp.maximum(row - 1, 0)
    after = jnp.minimum(row + 1, N_ROW - 1)
    layer = lax.broadcasted_iota(jnp.int32, (8, LANES), 0)
    lane = lax.broadcasted_iota(jnp.int32, (8, LANES), 1)
    nothing = jnp.zeros((8, LANES), f32)
    for chunk, source, start, here in (
        (0, 2 * before, 2 * LANES, row > 0),
        (EXT - 1, 2 * after, LANES, row < N_ROW - 1),
    ):
        sent = win_ref[source, :, start : start + LANES].astype(f32)
        k = nothing
        for level in range(COEFS):
            k = jnp.where(sent[0:8] == float(level), table_ref[level], k)
        cell_ref[chunk + 1, 0] = jnp.where((layer < LAYERS) & here, k, 0.0)
        cell_ref[chunk + 1, 1] = jnp.where(here, sent[8:16] + sent[16:24], 0.0)
    cell_ref[0, 0] = nothing
    cell_ref[EXT + 1, 0] = nothing

    for chunk in range(MID):
        cell_ref[chunk + 2] = cells_ref[chunk]

    def one_chunk(chunk, carry):
        k = cell_ref[chunk + 1, 0]
        left = pltpu.roll(jnp.where(lane == LANES - 1, cell_ref[chunk, 0], k), 1, 1)
        right = pltpu.roll(jnp.where(lane == 0, cell_ref[chunk + 2, 0], k), LANES - 1, 1)
        left = 0.5 * (k + left)
        right = 0.5 * (k + right)
        lower = jnp.where(layer < LAYERS - 1, 0.5 * (k + pltpu.roll(k, 7, 0)), 0.0)
        upper = jnp.where(layer == 0, k, pltpu.roll(lower, 1, 0))
        inside = ((chunk > 0) | (row > 0)) & ((chunk < EXT - 1) | (row < N_ROW - 1))
        scale = jnp.where(inside, JACOBI_WEIGHT / (left + right + upper + lower + CELL_MASS), 0.0)
        coef_ref[chunk, 0:8] = left * scale
        coef_ref[chunk, 8:16] = right * scale
        coef_ref[chunk, 16:24] = upper * scale
        coef_ref[chunk, 24:32] = lower * scale
        coef_ref[chunk, 32:40] = cell_ref[chunk + 1, 1] * scale
        coef_ref[chunk, 40:48] = k
        return carry

    lax.fori_loop(0, EXT, one_chunk, 0, unroll=2)


def relax(scal_ref, band_ref, win_ref, coef_ref, states, top_ref):
    first = scal_ref[SLOTS + 3]
    row = scal_ref[SLOTS + 4]
    before = jnp.maximum(row - 1, 0)
    after = jnp.minimum(row + 1, N_ROW - 1)
    top_ref[0] = win_ref[2 * before + 1, :, TILE - LANES :].astype(f32)
    top_ref[EXT - 1] = win_ref[2 * after, :, :LANES].astype(f32)
    for chunk in range(MID):
        start = chunk % 4 * LANES
        top = band_ref[first + chunk // 4, :, start : start + LANES]
        top_ref[chunk + 1] = top.astype(f32)
    lane = lax.broadcasted_iota(jnp.int32, (RHS, LANES), 1)
    is_first = lane == 0
    is_last = lane == LANES - 1

    def sweep(source_ref, target_ref):
        def one_chunk(chunk, carry):
            upper = top_ref[chunk]
            centre = source_ref[chunk + 1, 0]
            for l in range(LAYERS):
                left = pltpu.roll(jnp.where(is_last, source_ref[chunk, l], centre), 1, 1)
                right = pltpu.roll(jnp.where(is_first, source_ref[chunk + 2, l], centre), LANES - 1, 1)
                value = (
                    (1.0 - JACOBI_WEIGHT) * centre
                    + coef_ref[chunk, l : 1 + l, :] * left
                    + coef_ref[chunk, 8 + l : 9 + l, :] * right
                    + coef_ref[chunk, 16 + l : 17 + l, :] * upper
                    + coef_ref[chunk, 32 + l : 33 + l, :]
                )
                if l + 1 < LAYERS:
                    below = source_ref[chunk + 1, l + 1]
                    value = value + coef_ref[chunk, 24 + l : 25 + l, :] * below
                    upper, centre = centre, below
                target_ref[chunk + 1, l] = value
            return carry

        lax.fori_loop(0, EXT, one_chunk, 0, unroll=UNROLL)

    for step in range(SWEEPS):
        sweep(states[step % 2], states[1 - step % 2])


def rows_body(first_iteration, scal_ref, band_ref, win_ref, panel_ref, *refs):
    if first_iteration:
        table_ref, cells_ref, band_out, head_out, state_out, coef_out = refs[:6]
        refs = refs[6:]
    else:
        state_in, coef_in, band_out, head_out = refs[:4]
        refs = refs[4:]
    band_acc, state_a, state_b, coef_ref, cell_ref, top_ref, sems, buffer_ref, panel_sems = refs
    is_volume = scal_ref[SLOTS] == 1

    @pl.when(jnp.logical_not(is_volume))
    def _():
        def one_slot(slot, named, band_tile, col_tile):
            band_acc[jnp.where(named, band_tile, BAND_TILES)] += lax.dot_general(
                win_ref[col_tile],
                buffer_ref[slot],
                (((1,), (1,)), ((), ())),
                preferred_element_type=f32,
            )

        for_slots(scal_ref, panel_ref, buffer_ref, panel_sems, band_acc, one_slot)
        band_out[...] = band_acc[:BAND_TILES].astype(bf16)
        head_out[...] = band_acc[:2]

    @pl.when(is_volume)
    def _():
        guard = jnp.zeros((LAYERS, RHS, LANES), f32)
        state_b[0] = guard
        state_b[EXT + 1] = guard
        if first_iteration:
            state_a[...] = jnp.zeros_like(state_a)
            weigh(scal_ref, table_ref, cells_ref, win_ref, cell_ref, coef_ref)
        else:
            loads = [
                pltpu.make_async_copy(state_in, state_a, sems.at[0]),
                pltpu.make_async_copy(coef_in, coef_ref, sems.at[1]),
            ]
            for load in loads:
                load.start()
            for load in loads:
                load.wait()
        relax(scal_ref, band_ref, win_ref, coef_ref, (state_a, state_b), top_ref)
        if first_iteration:
            saves = [
                pltpu.make_async_copy(state_a, state_out, sems.at[0]),
                pltpu.make_async_copy(coef_ref, coef_out, sems.at[1]),
            ]
            for save in saves:
                save.start()
        band_out[...] = jnp.zeros_like(band_out)
        head_out[...] = jnp.zeros_like(head_out)
        first = scal_ref[SLOTS + 3]
        for chunk in range(MID):
            start = chunk % 4 * LANES
            flux = (top_ref[chunk + 1] - state_a[chunk + 2, 0])
            flux = coef_ref[chunk + 1, 40:41, :] * flux
            band_out[first + chunk // 4, :, start : start + LANES] = flux.astype(bf16)
            if chunk < 8:

                @pl.when(first == 0)
                def _():
                    head_out[chunk // 4, :, start : start + LANES] = flux

        if first_iteration:
            for save in saves:
                save.wait()


def into_rows(scal, band, win, panel, table, cells, saved):
    first_iteration = saved is None
    outs = [
        jax.ShapeDtypeStruct((BAND_TILES, RHS, TILE), bf16),
        jax.ShapeDtypeStruct((2, RHS, TILE), f32),
    ]
    out_specs = [VMEM, VMEM]
    in_specs = [SMEM, VMEM, VMEM, ANY]
    args = [scal, band, win, panel]
    state = (EXT + 2, LAYERS, RHS, LANES)
    coefs = (EXT, 48, LANES)
    if first_iteration:
        outs += [pltpu.HBM(state, f32), pltpu.HBM(coefs, f32)]
        out_specs += [ANY, ANY]
        in_specs += [SMEM, VMEM]
        args += [table, cells]
    else:
        in_specs += [ANY, ANY]
        args += [in_hbm(x) for x in saved]
    return pl.pallas_call(
        functools.partial(rows_body, first_iteration),
        out_shape=outs,
        in_specs=in_specs,
        out_specs=out_specs,
        scratch_shapes=[
            pltpu.VMEM((BAND_TILES + 1, RHS, TILE), f32),
            pltpu.VMEM(state, f32),
            pltpu.VMEM(state, f32),
            pltpu.VMEM(coefs, f32),
            pltpu.VMEM((EXT + 2, 2, 8, LANES), f32),
            pltpu.VMEM((EXT, RHS, LANES), f32),
            pltpu.SemaphoreType.DMA((2,)),
            pltpu.VMEM((SLOTS, TILE, TILE), bf16),
            pltpu.SemaphoreType.DMA((SLOTS,)),
        ],
        compiler_params=pltpu.CompilerParams(vmem_limit_bytes=44 * MIB),
        cost_estimate=pl.CostEstimate(flops=7 * 10**8, transcendentals=0, bytes_accessed=30 * 10**6),
        name="into_rows_first" if first_iteration else "into_rows_next",
    )(*args)


def head_body(parts_ref, head_ref, band_ref, out_ref):
    total = head_ref[...]
    for peer in range(N_ROW):
        total = total + parts_ref[peer].astype(f32)
    out_ref[0] = total.astype(bf16)


def add_head(parts, head, band):
    return pl.pallas_call(
        head_body,
        grid=(1,),
        out_shape=jax.ShapeDtypeStruct((N_COL, 2, RHS, TILE), bf16),
        in_specs=[
            pl.BlockSpec((N_ROW, 2, RHS, TILE), lambda i: (0, 0, 0, 0)),
            pl.BlockSpec((2, RHS, TILE), lambda i: (0, 0, 0)),
            ANY,
        ],
        out_specs=pl.BlockSpec((1, 2, RHS, TILE), lambda i: (0, 0, 0, 0)),
        input_output_aliases={2: 0},
        compiler_params=pltpu.CompilerParams(vmem_limit_bytes=6 * MIB),
        name="add_head",
    )(parts, head, band)


def update_body(last, parts_ref, trace_ref, load_ref, *outs):
    for half in range(2):
        lanes = slice(half * TILE, (half + 1) * TILE)
        total = parts_ref[0, half].astype(f32)
        for peer in range(1, N_COL):
            total = total + parts_ref[peer, half].astype(f32)
        trace = trace_ref[:, lanes]
        trace = trace + COUPLING_STEP * (load_ref[:, lanes] - trace - total)
        outs[0][:, lanes] = trace
        if last:
            outs[1][:, lanes] = total
        else:
            rounded = trace.astype(bf16)
            for copy in range(N_COL):
                outs[1][copy, half] = rounded


def update(parts, traces, load, last):
    whole = jax.ShapeDtypeStruct(traces.shape, f32)
    return pl.pallas_call(
        functools.partial(update_body, last),
        out_shape=[whole, whole if last else jax.ShapeDtypeStruct(parts.shape, bf16)],
        in_specs=[VMEM, VMEM, VMEM],
        out_specs=[VMEM, VMEM],
        compiler_params=pltpu.CompilerParams(vmem_limit_bytes=8 * MIB),
        name="update_last" if last else "update_next",
    )(parts, traces, load)


def lookup(indices, table):
    levels = jnp.arange(table.shape[0], dtype=jnp.int32)
    return jnp.sum(jnp.where(indices[..., None] == levels, table, 0.0), axis=-1)


def volume_cells(coef_index, coef_table, vol_source, volume_line):
    indices = lax.dynamic_index_in_dim(coef_index, volume_line, 0, keepdims=False)
    source = lax.dynamic_index_in_dim(vol_source, volume_line, 0, keepdims=False)
    spare = ((0, 0), (0, 8 - LAYERS), (0, 0), (0, 0))
    cells = jnp.stack([lookup(indices, coef_table), source]).reshape(2, LAYERS, MID, LANES)
    cells = jnp.pad(cells, spare).transpose(2, 0, 1, 3)

    def ends(x):
        return jnp.concatenate([x[:, :LANES], x[:, -LANES:]], 1)

    high = ends(source).astype(bf16)
    low = (ends(source) - high.astype(f32)).astype(bf16)
    edges = [jnp.pad(e, ((0, 4), (0, 0))) for e in (ends(indices).astype(bf16), high, low)]
    return cells, jnp.pad(jnp.concatenate(edges, 0), ((0, 8), (0, 0)))


def local(
    trace_start, surface_load, panel_tiles, tile_list, surf_map, coef_index, coef_table, vol_source
):
    col_index = lax.axis_index("col")
    row_index = lax.axis_index("row")
    volume_line = jnp.maximum(col_index - DENSE_COLS, 0)
    is_volume = col_index >= DENSE_COLS
    volume_tile = volume_line * N_ROW + row_index
    tile_numbers = jnp.arange(surf_map.shape[0], dtype=jnp.int32)
    quarter = jnp.sum(jnp.where(surf_map == volume_tile, tile_numbers, 0)) % 4
    first = quarter * 8
    own = [is_volume, jnp.where(is_volume, first, 0), jnp.where(is_volume, first + 7, 1), first, row_index]
    scal = jnp.concatenate([tile_list, jnp.stack([x.astype(jnp.int32) for x in own])])
    traces = trace_start
    spread = spread_start(traces)
    cells, edges = volume_cells(coef_index, coef_table, vol_source, volume_line)
    panel = in_hbm(panel_tiles)
    saved = None
    for iteration in range(ITERS):
        last = iteration == ITERS - 1
        band = exchange(spread, "col").reshape(BAND_TILES, RHS, TILE)
        row_spread = spread_row(scal, band, edges if iteration == 0 else None)
        win = exchange(row_spread, "row").reshape(WIN_TILES, RHS, TILE)
        win_part = into_window(scal, band, panel)
        win_parts = exchange(win_part.reshape(N_ROW, 2, RHS, TILE), "row")
        made = into_rows(scal, band, win, panel, coef_table, cells, saved)
        band_part, head = made[:2]
        saved = made[2:]
        band_part = add_head(win_parts, head, band_part.reshape(N_COL, 2, RHS, TILE))
        traces, spread = update(exchange(band_part, "col"), traces, surface_load, last)
    return (traces, spread)


def solution(mesh):
    return jax.shard_map(
        local,
        mesh=mesh,
        in_specs=(
            P(None, ("col", "row")),
            P(None, ("col", "row")),
            P(("col", "row"), None, None),
            P(("col", "row")),
            P(),
            P(None, None, "row"),
            P(),
            P(None, None, "row"),
        ),
        out_specs=(P(None, ("col", "row")), P(None, ("col", "row"))),
        check_vma=False,
    )
```

```python
import functools

import jax
import jax.numpy as jnp
from jax import lax
from jax.experimental import pallas as pl
from jax.experimental.pallas import tpu as pltpu
from jax.sharding import PartitionSpec as P

ITERS = 2
SWEEPS = 4
COUPLING_STEP = 0.3
JACOBI_WEIGHT = 0.8
CELL_MASS = 0.05

RHS = 32
TILE = 512
LANES = 128
N_COL = 16
N_ROW = 8
CORES = 2
CHIPS = N_COL // CORES
TILES = 2 * CHIPS
DENSE_COLS = 12
LAYERS = 4
SLOTS = 43
GROUP = 4
UNROLL = 17
COEFS = 16
BAND_TILES = 32
WIN_TILES = 16
MID = 32
EXT = MID + 2
MIB = 1 << 20

VMEM = pl.BlockSpec(memory_space=pltpu.VMEM)
SMEM = pl.BlockSpec(memory_space=pltpu.SMEM)
ANY = pl.BlockSpec(memory_space=pl.ANY)
f32 = jnp.float32
bf16 = jnp.bfloat16


def in_hbm(x):
    return pltpu.with_memory_space_constraint(x, pltpu.HBM)


def exchange(x, axis):
    return lax.all_to_all(x, axis, 0, 0, tiled=True)


def between_chips(x):
    groups = [list(range(core, N_COL, CORES)) for core in range(CORES)]
    return lax.all_to_all(x, "col", 0, 0, axis_index_groups=groups, tiled=True)


def from_mate(x):
    return lax.ppermute(x, "col", [(i, i ^ 1) for i in range(N_COL)])


def pick(near_ref, far_ref, is_far, index):
    return jnp.where(is_far == 0, near_ref[index], far_ref[index])


def put_everywhere(half_pair, out_ref, copies):
    for copy in range(copies):
        for half in range(2):
            out_ref[copy, half] = half_pair[half]


def start_body(trace_ref, out_ref):
    halves = [trace_ref[:, h * TILE : (h + 1) * TILE].astype(bf16) for h in range(2)]
    put_everywhere(halves, out_ref, CHIPS)


def spread_start(trace_start):
    return pl.pallas_call(
        start_body,
        out_shape=jax.ShapeDtypeStruct((CHIPS, 2, RHS, TILE), bf16),
        in_specs=[VMEM],
        out_specs=VMEM,
        compiler_params=pltpu.CompilerParams(vmem_limit_bytes=6 * MIB),
        name="spread_start",
    )(trace_start)


def row_body(first_iteration, scal_ref, near_ref, far_ref, *refs):
    out_ref = refs[-1]
    core = scal_ref[SLOTS + 6]
    halves = [
        pick(near_ref, far_ref, core, scal_ref[SLOTS + 1]),
        pick(near_ref, far_ref, scal_ref[SLOTS + 5], scal_ref[SLOTS + 2]),
    ]
    put_everywhere(halves, out_ref, N_ROW)
    if first_iteration:

        @pl.when(scal_ref[SLOTS] == 1)
        def _():
            for peer in range(N_ROW):
                out_ref[peer, 0, :, LANES : 3 * LANES] = refs[0][...]


def spread_row(scal, near, far, edges):
    first_iteration = edges is not None
    args = [scal, near, far] + ([edges] if first_iteration else [])
    return pl.pallas_call(
        functools.partial(row_body, first_iteration),
        out_shape=jax.ShapeDtypeStruct((N_ROW, 2, RHS, TILE), bf16),
        in_specs=[SMEM] + [VMEM] * (len(args) - 1),
        out_specs=VMEM,
        compiler_params=pltpu.CompilerParams(vmem_limit_bytes=6 * MIB),
        name="spread_row",
    )(*args)


def for_slots(scal_ref, panel_ref, buffer_ref, sems, acc_ref, do_slot):
    def fetch(slot):
        return pltpu.make_async_copy(panel_ref.at[slot], buffer_ref.at[slot], sems.at[slot])

    def start(slot, carry):
        fetch(slot).start()
        return carry

    lax.fori_loop(0, SLOTS, start, 0)
    acc_ref[...] = jnp.zeros_like(acc_ref)

    def place(slot):
        ident = scal_ref[slot]
        named = ident >= 0
        safe = jnp.maximum(ident, 0)
        row_tile = lax.shift_right_logical(safe, 8)
        col_tile = jnp.bitwise_and(safe, 15)
        shard = lax.shift_right_logical(row_tile, 4)
        do_slot(slot, named, shard, jnp.bitwise_and(row_tile, 1), col_tile)

    def group(index, carry):
        for extra in range(GROUP):
            fetch(index * GROUP + extra).wait()
        for extra in range(GROUP):
            place(index * GROUP + extra)
        return carry

    lax.fori_loop(0, SLOTS // GROUP, group, 0)
    for slot in range(SLOTS // GROUP * GROUP, SLOTS):
        fetch(slot).wait()
        place(slot)


def window_body(scal_ref, near_ref, far_ref, panel_ref, win_out, win_acc, buffer_ref, sems):
    is_volume = scal_ref[SLOTS] == 1

    @pl.when(jnp.logical_not(is_volume))
    def _():
        core = scal_ref[SLOTS + 6]

        def one_slot(slot, named, shard, half, col_tile):
            is_far = jnp.bitwise_xor(jnp.bitwise_and(shard, 1), core)
            index = lax.shift_right_logical(shard, 1) * 2 + half
            win_acc[jnp.where(named, col_tile, WIN_TILES)] += jnp.dot(
                pick(near_ref, far_ref, is_far, index),
                buffer_ref[slot],
                preferred_element_type=f32,
            )

        for_slots(scal_ref, panel_ref, buffer_ref, sems, win_acc, one_slot)

        win_out[...] = win_acc[:WIN_TILES].astype(bf16)

    @pl.when(is_volume)
    def _():
        win_out[...] = jnp.zeros_like(win_out)


def into_window(scal, near, far, panel):
    return pl.pallas_call(
        window_body,
        out_shape=jax.ShapeDtypeStruct((WIN_TILES, RHS, TILE), bf16),
        in_specs=[SMEM, VMEM, VMEM, ANY],
        out_specs=VMEM,
        scratch_shapes=[
            pltpu.VMEM((WIN_TILES + 1, RHS, TILE), f32),
            pltpu.VMEM((SLOTS, TILE, TILE), bf16),
            pltpu.SemaphoreType.DMA((SLOTS,)),
        ],
        compiler_params=pltpu.CompilerParams(vmem_limit_bytes=44 * MIB),
        cost_estimate=pl.CostEstimate(flops=7 * 10**8, transcendentals=0, bytes_accessed=25 * 10**6),
        name="into_window",
    )(scal, near, far, panel)


def weigh(scal_ref, table_ref, cells_ref, win_ref, cell_ref, coef_ref):
    row = scal_ref[SLOTS + 4]
    before = jnp.maximum(row - 1, 0)
    after = jnp.minimum(row + 1, N_ROW - 1)
    layer = lax.broadcasted_iota(jnp.int32, (8, LANES), 0)
    lane = lax.broadcasted_iota(jnp.int32, (8, LANES), 1)
    nothing = jnp.zeros((8, LANES), f32)
    for chunk, source, start, here in (
        (0, 2 * before, 2 * LANES, row > 0),
        (EXT - 1, 2 * after, LANES, row < N_ROW - 1),
    ):
        sent = win_ref[source, :, start : start + LANES].astype(f32)
        k = nothing
        for level in range(COEFS):
            k = jnp.where(sent[0:8] == float(level), table_ref[level], k)
        cell_ref[chunk + 1, 0] = jnp.where((layer < LAYERS) & here, k, 0.0)
        cell_ref[chunk + 1, 1] = jnp.where(here, sent[8:16] + sent[16:24], 0.0)
    cell_ref[0, 0] = nothing
    cell_ref[EXT + 1, 0] = nothing

    for chunk in range(MID):
        cell_ref[chunk + 2] = cells_ref[chunk]

    def one_chunk(chunk, carry):
        k = cell_ref[chunk + 1, 0]
        left = pltpu.roll(jnp.where(lane == LANES - 1, cell_ref[chunk, 0], k), 1, 1)
        right = pltpu.roll(jnp.where(lane == 0, cell_ref[chunk + 2, 0], k), LANES - 1, 1)
        left = 0.5 * (k + left)
        right = 0.5 * (k + right)
        lower = jnp.where(layer < LAYERS - 1, 0.5 * (k + pltpu.roll(k, 7, 0)), 0.0)
        upper = jnp.where(layer == 0, k, pltpu.roll(lower, 1, 0))
        inside = ((chunk > 0) | (row > 0)) & ((chunk < EXT - 1) | (row < N_ROW - 1))
        scale = jnp.where(inside, JACOBI_WEIGHT / (left + right + upper + lower + CELL_MASS), 0.0)
        coef_ref[chunk, 0:8] = left * scale
        coef_ref[chunk, 8:16] = right * scale
        coef_ref[chunk, 16:24] = upper * scale
        coef_ref[chunk, 24:32] = lower * scale
        coef_ref[chunk, 32:40] = cell_ref[chunk + 1, 1] * scale
        coef_ref[chunk, 40:48] = k
        return carry

    lax.fori_loop(0, EXT, one_chunk, 0, unroll=2)


def relax(scal_ref, near_ref, far_ref, win_ref, coef_ref, states, top_ref):
    quarter = scal_ref[SLOTS + 3]
    row = scal_ref[SLOTS + 4]
    core = scal_ref[SLOTS + 6]
    before = jnp.maximum(row - 1, 0)
    after = jnp.minimum(row + 1, N_ROW - 1)
    top_ref[0] = win_ref[2 * before + 1, :, TILE - LANES :].astype(f32)
    top_ref[EXT - 1] = win_ref[2 * after, :, :LANES].astype(f32)
    for tile in range(8):
        is_far = jnp.bitwise_xor(tile // 2 % 2, core)
        tops = pick(near_ref, far_ref, is_far, 4 * quarter + tile // 4 * 2 + tile % 2)
        for part in range(4):
            top_ref[4 * tile + part + 1] = tops[:, part * LANES : (part + 1) * LANES].astype(f32)
    lane = lax.broadcasted_iota(jnp.int32, (RHS, LANES), 1)
    is_first = lane == 0
    is_last = lane == LANES - 1

    def sweep(source_ref, target_ref):
        def one_chunk(chunk, carry):
            upper = top_ref[chunk]
            centre = source_ref[chunk + 1, 0]
            for l in range(LAYERS):
                left = pltpu.roll(jnp.where(is_last, source_ref[chunk, l], centre), 1, 1)
                right = pltpu.roll(jnp.where(is_first, source_ref[chunk + 2, l], centre), LANES - 1, 1)
                value = (
                    (1.0 - JACOBI_WEIGHT) * centre
                    + coef_ref[chunk, l : 1 + l, :] * left
                    + coef_ref[chunk, 8 + l : 9 + l, :] * right
                    + coef_ref[chunk, 16 + l : 17 + l, :] * upper
                    + coef_ref[chunk, 32 + l : 33 + l, :]
                )
                if l + 1 < LAYERS:
                    below = source_ref[chunk + 1, l + 1]
                    value = value + coef_ref[chunk, 24 + l : 25 + l, :] * below
                    upper, centre = centre, below
                target_ref[chunk + 1, l] = value
            return carry

        lax.fori_loop(0, EXT, one_chunk, 0, unroll=UNROLL)

    for step in range(SWEEPS):
        sweep(states[step % 2], states[1 - step % 2])


def rows_body(first_iteration, scal_ref, near_ref, far_ref, win_ref, panel_ref, *refs):
    if first_iteration:
        table_ref, cells_ref, own_out, mate_out, head_out, state_out, coef_out = refs[:7]
        refs = refs[7:]
    else:
        state_in, coef_in, own_out, mate_out, head_out = refs[:5]
        refs = refs[5:]
    band_acc, state_a, state_b, coef_ref, cell_ref, top_ref, sems, buffer_ref, panel_sems = refs
    is_volume = scal_ref[SLOTS] == 1

    @pl.when(jnp.logical_not(is_volume))
    def _():
        def one_slot(slot, named, shard, half, col_tile):
            band_acc[jnp.where(named, 2 * shard + half, BAND_TILES)] += lax.dot_general(
                win_ref[col_tile],
                buffer_ref[slot],
                (((1,), (1,)), ((), ())),
                preferred_element_type=f32,
            )

        for_slots(scal_ref, panel_ref, buffer_ref, panel_sems, band_acc, one_slot)

    @pl.when(is_volume)
    def _():
        guard = jnp.zeros((LAYERS, RHS, LANES), f32)
        state_b[0] = guard
        state_b[EXT + 1] = guard
        if first_iteration:
            state_a[...] = jnp.zeros_like(state_a)
            weigh(scal_ref, table_ref, cells_ref, win_ref, cell_ref, coef_ref)
        else:
            loads = [
                pltpu.make_async_copy(state_in, state_a, sems.at[0]),
                pltpu.make_async_copy(coef_in, coef_ref, sems.at[1]),
            ]
            for load in loads:
                load.start()
            for load in loads:
                load.wait()
        relax(scal_ref, near_ref, far_ref, win_ref, coef_ref, (state_a, state_b), top_ref)
        if first_iteration:
            saves = [
                pltpu.make_async_copy(state_a, state_out, sems.at[0]),
                pltpu.make_async_copy(coef_ref, coef_out, sems.at[1]),
            ]
            for save in saves:
                save.start()
        band_acc[...] = jnp.zeros_like(band_acc)
        first = 8 * scal_ref[SLOTS + 3]
        for chunk in range(MID):
            start = chunk % 4 * LANES
            flux = coef_ref[chunk + 1, 40:41, :] * (top_ref[chunk + 1] - state_a[chunk + 2, 0])
            band_acc[first + chunk // 4, :, start : start + LANES] = flux

        if first_iteration:
            for save in saves:
                save.wait()

    core = scal_ref[SLOTS + 6]
    for chip in range(CHIPS):
        own_out[chip] = band_acc[pl.ds(4 * chip + 2 * core, 2)]
        mate_out[chip] = band_acc[pl.ds(4 * chip + 2 - 2 * core, 2)].astype(bf16)
    head_out[...] = band_acc[:2]


def into_rows(scal, near, far, win, panel, table, cells, saved):
    first_iteration = saved is None
    outs = [
        jax.ShapeDtypeStruct((CHIPS, 2, RHS, TILE), f32),
        jax.ShapeDtypeStruct((CHIPS, 2, RHS, TILE), bf16),
        jax.ShapeDtypeStruct((2, RHS, TILE), f32),
    ]
    out_specs = [VMEM, VMEM, VMEM]
    in_specs = [SMEM, VMEM, VMEM, VMEM, ANY]
    args = [scal, near, far, win, panel]
    state = (EXT + 2, LAYERS, RHS, LANES)
    coefs = (EXT, 48, LANES)
    if first_iteration:
        outs += [pltpu.HBM(state, f32), pltpu.HBM(coefs, f32)]
        out_specs += [ANY, ANY]
        in_specs += [SMEM, VMEM]
        args += [table, cells]
    else:
        in_specs += [ANY, ANY]
        args += [in_hbm(x) for x in saved]
    return pl.pallas_call(
        functools.partial(rows_body, first_iteration),
        out_shape=outs,
        in_specs=in_specs,
        out_specs=out_specs,
        scratch_shapes=[
            pltpu.VMEM((BAND_TILES + 1, RHS, TILE), f32),
            pltpu.VMEM(state, f32),
            pltpu.VMEM(state, f32),
            pltpu.VMEM(coefs, f32),
            pltpu.VMEM((EXT + 2, 2, 8, LANES), f32),
            pltpu.VMEM((EXT, RHS, LANES), f32),
            pltpu.SemaphoreType.DMA((2,)),
            pltpu.VMEM((SLOTS, TILE, TILE), bf16),
            pltpu.SemaphoreType.DMA((SLOTS,)),
        ],
        compiler_params=pltpu.CompilerParams(vmem_limit_bytes=44 * MIB),
        cost_estimate=pl.CostEstimate(flops=7 * 10**8, transcendentals=0, bytes_accessed=30 * 10**6),
        name="into_rows_first" if first_iteration else "into_rows_next",
    )(*args)


def mate_body(scal_ref, parts_ref, head_ref, mate_ref, out_ref):
    out_ref[...] = mate_ref[...]

    @pl.when(scal_ref[SLOTS + 6] == 1)
    def _():
        total = head_ref[...]
        for peer in range(N_ROW):
            total = total + parts_ref[peer].astype(f32)
        out_ref[0] = total.astype(bf16)


def for_mate(scal, parts, head, mate):
    return pl.pallas_call(
        mate_body,
        out_shape=jax.ShapeDtypeStruct(mate.shape, bf16),
        in_specs=[SMEM, VMEM, VMEM, VMEM],
        out_specs=VMEM,
        compiler_params=pltpu.CompilerParams(vmem_limit_bytes=6 * MIB),
        name="for_mate",
    )(scal, parts, head, mate)


def pair_body(scal_ref, parts_ref, own_ref, got_ref, out_ref):
    for chip in range(1, CHIPS):
        out_ref[chip] = (own_ref[chip] + got_ref[chip].astype(f32)).astype(bf16)
    total = own_ref[0] + got_ref[0].astype(f32)
    share = parts_ref[0].astype(f32)
    for peer in range(1, N_ROW):
        share = share + parts_ref[peer].astype(f32)
    out_ref[0] = (total + jnp.where(scal_ref[SLOTS + 6] == 0, share, 0.0)).astype(bf16)


def pair_sum(scal, parts, own, got):
    return pl.pallas_call(
        pair_body,
        out_shape=jax.ShapeDtypeStruct(got.shape, bf16),
        in_specs=[SMEM, VMEM, VMEM, VMEM],
        out_specs=VMEM,
        compiler_params=pltpu.CompilerParams(vmem_limit_bytes=6 * MIB),
        name="pair_sum",
    )(scal, parts, own, got)


def update_body(last, parts_ref, trace_ref, load_ref, *outs):
    for half in range(2):
        lanes = slice(half * TILE, (half + 1) * TILE)
        total = parts_ref[0, half].astype(f32)
        for peer in range(1, CHIPS):
            total = total + parts_ref[peer, half].astype(f32)
        trace = trace_ref[:, lanes]
        trace = trace + COUPLING_STEP * (load_ref[:, lanes] - trace - total)
        outs[0][:, lanes] = trace
        if last:
            outs[1][:, lanes] = total
        else:
            rounded = trace.astype(bf16)
            for copy in range(CHIPS):
                outs[1][copy, half] = rounded


def update(parts, traces, load, last):
    whole = jax.ShapeDtypeStruct(traces.shape, f32)
    return pl.pallas_call(
        functools.partial(update_body, last),
        out_shape=[whole, whole if last else jax.ShapeDtypeStruct(parts.shape, bf16)],
        in_specs=[VMEM, VMEM, VMEM],
        out_specs=[VMEM, VMEM],
        compiler_params=pltpu.CompilerParams(vmem_limit_bytes=8 * MIB),
        name="update_last" if last else "update_next",
    )(parts, traces, load)


def lookup(indices, table):
    levels = jnp.arange(table.shape[0], dtype=jnp.int32)
    return jnp.sum(jnp.where(indices[..., None] == levels, table, 0.0), axis=-1)


def volume_cells(coef_index, coef_table, vol_source, volume_line):
    indices = lax.dynamic_index_in_dim(coef_index, volume_line, 0, keepdims=False)
    source = lax.dynamic_index_in_dim(vol_source, volume_line, 0, keepdims=False)
    spare = ((0, 0), (0, 8 - LAYERS), (0, 0), (0, 0))
    cells = jnp.stack([lookup(indices, coef_table), source]).reshape(2, LAYERS, MID, LANES)
    cells = jnp.pad(cells, spare).transpose(2, 0, 1, 3)

    def ends(x):
        return jnp.concatenate([x[:, :LANES], x[:, -LANES:]], 1)

    high = ends(source).astype(bf16)
    low = (ends(source) - high.astype(f32)).astype(bf16)
    edges = [jnp.pad(e, ((0, 4), (0, 0))) for e in (ends(indices).astype(bf16), high, low)]
    return cells, jnp.pad(jnp.concatenate(edges, 0), ((0, 8), (0, 0)))


def local(
    trace_start, surface_load, panel_tiles, tile_list, surf_map, coef_index, coef_table, vol_source
):
    col_index = lax.axis_index("col")
    row_index = lax.axis_index("row")
    volume_line = jnp.maximum(col_index - DENSE_COLS, 0)
    is_volume = col_index >= DENSE_COLS
    volume_tile = volume_line * N_ROW + row_index
    tile_numbers = jnp.arange(surf_map.shape[0], dtype=jnp.int32)
    quarter = jnp.sum(jnp.where(surf_map == volume_tile, tile_numbers, 0)) % 4
    core = col_index % CORES
    own = [
        is_volume,
        jnp.where(is_volume, 4 * quarter, 0),
        jnp.where(is_volume, 4 * quarter + 3, 1),
        quarter,
        row_index,
        jnp.where(is_volume, 1 - core, core),
        core,
    ]
    scal = jnp.concatenate([tile_list, jnp.stack([x.astype(jnp.int32) for x in own])])
    traces = trace_start
    spread = spread_start(traces)
    cells, edges = volume_cells(coef_index, coef_table, vol_source, volume_line)
    panel = in_hbm(panel_tiles)
    saved = None
    for iteration in range(ITERS):
        last = iteration == ITERS - 1
        near = between_chips(spread)
        far = from_mate(near)
        near, far = near.reshape(TILES, RHS, TILE), far.reshape(TILES, RHS, TILE)
        row_spread = spread_row(scal, near, far, edges if iteration == 0 else None)
        win = exchange(row_spread, "row").reshape(WIN_TILES, RHS, TILE)
        win_part = into_window(scal, near, far, panel)
        parts = exchange(win_part.reshape(N_ROW, 2, RHS, TILE), "row")
        own, mate, head, *saved = into_rows(
            scal, near, far, win, panel, coef_table, cells, saved
        )
        got = from_mate(for_mate(scal, parts, head, mate))
        summed = between_chips(pair_sum(scal, parts, own, got))
        traces, spread = update(summed, traces, surface_load, last)
    return (traces, spread)


def solution(mesh):
    return jax.shard_map(
        local,
        mesh=mesh,
        in_specs=(
            P(None, ("col", "row")),
            P(None, ("col", "row")),
            P(("col", "row"), None, None),
            P(("col", "row")),
            P(),
            P(None, None, "row"),
            P(),
            P(None, None, "row"),
        ),
        out_specs=(P(None, ("col", "row")), P(None, ("col", "row"))),
        check_vma=False,
    )
```

```python
import functools

import jax
import jax.numpy as jnp
from jax import lax
from jax.experimental import pallas as pl
from jax.experimental.pallas import tpu as pltpu
from jax.sharding import PartitionSpec as P

ITERS = 2
SWEEPS = 4
COUPLING_STEP = 0.3
JACOBI_WEIGHT = 0.8
CELL_MASS = 0.05

RHS = 32
TILE = 512
LANES = 128
N_COL = 16
N_ROW = 8
CORES = 2
CHIPS = N_COL // CORES
TILES = 2 * CHIPS
DENSE_COLS = 12
LAYERS = 4
SLOTS = 43
GROUP = 4
UNROLL = 17
COEFS = 16
BAND_TILES = 32
WIN_TILES = 16
MID = 32
EXT = MID + 2
MIB = 1 << 20

VMEM = pl.BlockSpec(memory_space=pltpu.VMEM)
SMEM = pl.BlockSpec(memory_space=pltpu.SMEM)
ANY = pl.BlockSpec(memory_space=pl.ANY)
f32 = jnp.float32
bf16 = jnp.bfloat16


def in_hbm(x):
    return pltpu.with_memory_space_constraint(x, pltpu.HBM)


def exchange(x, axis):
    return lax.all_to_all(x, axis, 0, 0, tiled=True)


def between_chips(x):
    groups = [list(range(core, N_COL, CORES)) for core in range(CORES)]
    return lax.all_to_all(x, "col", 0, 0, axis_index_groups=groups, tiled=True)


def from_mate(x):
    return lax.ppermute(x, "col", [(i, i ^ 1) for i in range(N_COL)])


def pick(near_ref, far_ref, is_far, index):
    return jnp.where(is_far == 0, near_ref[index], far_ref[index])


def start_body(trace_ref, out_ref):
    for half in range(2):
        rounded = trace_ref[:, half * TILE : (half + 1) * TILE].astype(bf16)
        for copy in range(CHIPS):
            out_ref[copy, half] = rounded


def spread_start(trace_start):
    return pl.pallas_call(
        start_body,
        out_shape=jax.ShapeDtypeStruct((CHIPS, 2, RHS, TILE), bf16),
        in_specs=[VMEM],
        out_specs=VMEM,
        compiler_params=pltpu.CompilerParams(vmem_limit_bytes=6 * MIB),
        name="spread_start",
    )(trace_start)


def row_body(first_iteration, scal_ref, near_ref, far_ref, *refs):
    out_ref = refs[-1]
    mine = pick(near_ref, far_ref, scal_ref[SLOTS + 5], scal_ref[SLOTS + 1])
    tail = pick(near_ref, far_ref, scal_ref[SLOTS + 7], scal_ref[SLOTS + 2])
    for peer in range(N_ROW):
        out_ref[peer, :, : 3 * LANES] = mine[:, : 3 * LANES]
        out_ref[peer, :, 3 * LANES :] = tail[:, 3 * LANES :]
    if first_iteration:

        @pl.when(scal_ref[SLOTS] == 1)
        def _():
            for peer in range(N_ROW):
                out_ref[peer, :, LANES : 3 * LANES] = refs[0][...]


def spread_row(scal, near, far, edges):
    first_iteration = edges is not None
    args = [scal, near, far] + ([edges] if first_iteration else [])
    return pl.pallas_call(
        functools.partial(row_body, first_iteration),
        out_shape=jax.ShapeDtypeStruct((N_ROW, RHS, TILE), bf16),
        in_specs=[SMEM] + [VMEM] * (len(args) - 1),
        out_specs=VMEM,
        compiler_params=pltpu.CompilerParams(vmem_limit_bytes=6 * MIB),
        name="spread_row",
    )(*args)


def for_slots(scal_ref, panel_ref, buffer_ref, sems, acc_ref, do_slot):
    def fetch(slot):
        return pltpu.make_async_copy(panel_ref.at[slot], buffer_ref.at[slot], sems.at[slot])

    def start(slot, carry):
        fetch(slot).start()
        return carry

    lax.fori_loop(0, SLOTS, start, 0)
    acc_ref[...] = jnp.zeros_like(acc_ref)

    def place(slot):
        ident = scal_ref[slot]
        named = ident >= 0
        safe = jnp.maximum(ident, 0)
        row_tile = lax.shift_right_logical(safe, 8)
        col_tile = jnp.bitwise_and(safe, 15)
        shard = lax.shift_right_logical(row_tile, 4)
        do_slot(slot, named, shard, jnp.bitwise_and(row_tile, 1), col_tile)

    def group(index, carry):
        for extra in range(GROUP):
            fetch(index * GROUP + extra).wait()
        for extra in range(GROUP):
            place(index * GROUP + extra)
        return carry

    lax.fori_loop(0, SLOTS // GROUP, group, 0)
    for slot in range(SLOTS // GROUP * GROUP, SLOTS):
        fetch(slot).wait()
        place(slot)


def window_body(scal_ref, near_ref, far_ref, panel_ref, win_out, win_acc, buffer_ref, sems):
    is_volume = scal_ref[SLOTS] == 1

    @pl.when(jnp.logical_not(is_volume))
    def _():
        core = scal_ref[SLOTS + 6]

        def one_slot(slot, named, shard, half, col_tile):
            is_far = jnp.bitwise_xor(jnp.bitwise_and(shard, 1), core)
            index = lax.shift_right_logical(shard, 1) * 2 + half
            win_acc[jnp.where(named, col_tile, WIN_TILES)] += jnp.dot(
                pick(near_ref, far_ref, is_far, index),
                buffer_ref[slot],
                preferred_element_type=f32,
            )

        for_slots(scal_ref, panel_ref, buffer_ref, sems, win_acc, one_slot)

        win_out[...] = win_acc[:WIN_TILES].astype(bf16)

    @pl.when(is_volume)
    def _():
        win_out[...] = jnp.zeros_like(win_out)


def into_window(scal, near, far, panel):
    return pl.pallas_call(
        window_body,
        out_shape=jax.ShapeDtypeStruct((WIN_TILES, RHS, TILE), bf16),
        in_specs=[SMEM, VMEM, VMEM, ANY],
        out_specs=VMEM,
        scratch_shapes=[
            pltpu.VMEM((WIN_TILES + 1, RHS, TILE), f32),
            pltpu.VMEM((SLOTS, TILE, TILE), bf16),
            pltpu.SemaphoreType.DMA((SLOTS,)),
        ],
        compiler_params=pltpu.CompilerParams(vmem_limit_bytes=44 * MIB),
        cost_estimate=pl.CostEstimate(flops=7 * 10**8, transcendentals=0, bytes_accessed=25 * 10**6),
        name="into_window",
    )(scal, near, far, panel)


def weigh(scal_ref, table_ref, cells_ref, win_ref, cell_ref, coef_ref):
    row = scal_ref[SLOTS + 4]
    before = jnp.maximum(row - 1, 0)
    after = jnp.minimum(row + 1, N_ROW - 1)
    layer = lax.broadcasted_iota(jnp.int32, (8, LANES), 0)
    lane = lax.broadcasted_iota(jnp.int32, (8, LANES), 1)
    nothing = jnp.zeros((8, LANES), f32)
    for chunk, source, start, here in (
        (0, before, 2 * LANES, row > 0),
        (EXT - 1, after, LANES, row < N_ROW - 1),
    ):
        sent = win_ref[source, :, start : start + LANES].astype(f32)
        k = nothing
        for level in range(COEFS):
            k = jnp.where(sent[0:8] == float(level), table_ref[level], k)
        cell_ref[chunk + 1, 0] = jnp.where((layer < LAYERS) & here, k, 0.0)
        cell_ref[chunk + 1, 1] = jnp.where(here, sent[8:16] + sent[16:24], 0.0)
    cell_ref[0, 0] = nothing
    cell_ref[EXT + 1, 0] = nothing

    for chunk in range(MID):
        cell_ref[chunk + 2] = cells_ref[chunk]

    def one_chunk(chunk, carry):
        k = cell_ref[chunk + 1, 0]
        left = pltpu.roll(jnp.where(lane == LANES - 1, cell_ref[chunk, 0], k), 1, 1)
        right = pltpu.roll(jnp.where(lane == 0, cell_ref[chunk + 2, 0], k), LANES - 1, 1)
        left = 0.5 * (k + left)
        right = 0.5 * (k + right)
        lower = jnp.where(layer < LAYERS - 1, 0.5 * (k + pltpu.roll(k, 7, 0)), 0.0)
        upper = jnp.where(layer == 0, k, pltpu.roll(lower, 1, 0))
        inside = ((chunk > 0) | (row > 0)) & ((chunk < EXT - 1) | (row < N_ROW - 1))
        scale = jnp.where(inside, JACOBI_WEIGHT / (left + right + upper + lower + CELL_MASS), 0.0)
        coef_ref[chunk, 0:8] = left * scale
        coef_ref[chunk, 8:16] = right * scale
        coef_ref[chunk, 16:24] = upper * scale
        coef_ref[chunk, 24:32] = lower * scale
        coef_ref[chunk, 32:40] = cell_ref[chunk + 1, 1] * scale
        coef_ref[chunk, 40:48] = k
        return carry

    lax.fori_loop(0, EXT, one_chunk, 0, unroll=2)


def relax(scal_ref, near_ref, far_ref, win_ref, coef_ref, states, top_ref):
    quarter = scal_ref[SLOTS + 3]
    row = scal_ref[SLOTS + 4]
    core = scal_ref[SLOTS + 6]
    before = jnp.maximum(row - 1, 0)
    after = jnp.minimum(row + 1, N_ROW - 1)
    top_ref[0] = win_ref[before, :, TILE - LANES :].astype(f32)
    top_ref[EXT - 1] = win_ref[after, :, :LANES].astype(f32)
    for tile in range(8):
        is_far = jnp.bitwise_xor(tile // 2 % 2, core)
        tops = pick(near_ref, far_ref, is_far, 4 * quarter + tile // 4 * 2 + tile % 2)
        for part in range(4):
            top_ref[4 * tile + part + 1] = tops[:, part * LANES : (part + 1) * LANES].astype(f32)
    lane = lax.broadcasted_iota(jnp.int32, (RHS, LANES), 1)
    is_first = lane == 0
    is_last = lane == LANES - 1

    def sweep(source_ref, target_ref):
        def one_chunk(chunk, carry):
            upper = top_ref[chunk]
            centre = source_ref[chunk + 1, 0]
            for l in range(LAYERS):
                left = pltpu.roll(jnp.where(is_last, source_ref[chunk, l], centre), 1, 1)
                right = pltpu.roll(jnp.where(is_first, source_ref[chunk + 2, l], centre), LANES - 1, 1)
                value = (
                    (1.0 - JACOBI_WEIGHT) * centre
                    + coef_ref[chunk, l : 1 + l, :] * left
                    + coef_ref[chunk, 8 + l : 9 + l, :] * right
                    + coef_ref[chunk, 16 + l : 17 + l, :] * upper
                    + coef_ref[chunk, 32 + l : 33 + l, :]
                )
                if l + 1 < LAYERS:
                    below = source_ref[chunk + 1, l + 1]
                    value = value + coef_ref[chunk, 24 + l : 25 + l, :] * below
                    upper, centre = centre, below
                target_ref[chunk + 1, l] = value
            return carry

        lax.fori_loop(0, EXT, one_chunk, 0, unroll=UNROLL)

    for step in range(SWEEPS):
        sweep(states[step % 2], states[1 - step % 2])


def rows_body(first_iteration, scal_ref, near_ref, far_ref, win_ref, mate_win_ref, panel_ref, *refs):
    if first_iteration:
        table_ref, cells_ref, own_out, mate_out, state_out, coef_out = refs[:6]
        refs = refs[6:]
    else:
        state_in, coef_in, own_out, mate_out = refs[:4]
        refs = refs[4:]
    band_acc, state_a, state_b, coef_ref, cell_ref, top_ref, sems, buffer_ref, panel_sems = refs
    is_volume = scal_ref[SLOTS] == 1
    core = scal_ref[SLOTS + 6]

    @pl.when(jnp.logical_not(is_volume))
    def _():
        def one_slot(slot, named, shard, half, col_tile):
            is_far = jnp.bitwise_xor(jnp.bitwise_and(col_tile, 1), core)
            band_acc[jnp.where(named, 2 * shard + half, BAND_TILES)] += lax.dot_general(
                pick(win_ref, mate_win_ref, is_far, lax.shift_right_logical(col_tile, 1)),
                buffer_ref[slot],
                (((1,), (1,)), ((), ())),
                preferred_element_type=f32,
            )

        for_slots(scal_ref, panel_ref, buffer_ref, panel_sems, band_acc, one_slot)

    @pl.when(is_volume)
    def _():
        guard = jnp.zeros((LAYERS, RHS, LANES), f32)
        state_b[0] = guard
        state_b[EXT + 1] = guard
        if first_iteration:
            state_a[...] = jnp.zeros_like(state_a)
            weigh(scal_ref, table_ref, cells_ref, win_ref, cell_ref, coef_ref)
        else:
            loads = [
                pltpu.make_async_copy(state_in, state_a, sems.at[0]),
                pltpu.make_async_copy(coef_in, coef_ref, sems.at[1]),
            ]
            for load in loads:
                load.start()
            for load in loads:
                load.wait()
        relax(scal_ref, near_ref, far_ref, win_ref, coef_ref, (state_a, state_b), top_ref)
        if first_iteration:
            saves = [
                pltpu.make_async_copy(state_a, state_out, sems.at[0]),
                pltpu.make_async_copy(coef_ref, coef_out, sems.at[1]),
            ]
            for save in saves:
                save.start()
        band_acc[...] = jnp.zeros_like(band_acc)
        first = 8 * scal_ref[SLOTS + 3]
        for chunk in range(MID):
            start = chunk % 4 * LANES
            flux = coef_ref[chunk + 1, 40:41, :] * (top_ref[chunk + 1] - state_a[chunk + 2, 0])
            band_acc[first + chunk // 4, :, start : start + LANES] = flux

        if first_iteration:
            for save in saves:
                save.wait()

    for chip in range(CHIPS):
        own_out[chip] = band_acc[pl.ds(4 * chip + 2 * core, 2)]
        mate_out[chip] = band_acc[pl.ds(4 * chip + 2 - 2 * core, 2)].astype(bf16)


def into_rows(scal, near, far, win, mate_win, panel, table, cells, saved):
    first_iteration = saved is None
    outs = [
        jax.ShapeDtypeStruct((CHIPS, 2, RHS, TILE), f32),
        jax.ShapeDtypeStruct((CHIPS, 2, RHS, TILE), bf16),
    ]
    out_specs = [VMEM, VMEM]
    in_specs = [SMEM, VMEM, VMEM, VMEM, VMEM, ANY]
    args = [scal, near, far, win, mate_win, panel]
    state = (EXT + 2, LAYERS, RHS, LANES)
    coefs = (EXT, 48, LANES)
    if first_iteration:
        outs += [pltpu.HBM(state, f32), pltpu.HBM(coefs, f32)]
        out_specs += [ANY, ANY]
        in_specs += [SMEM, VMEM]
        args += [table, cells]
    else:
        in_specs += [ANY, ANY]
        args += [in_hbm(x) for x in saved]
    return pl.pallas_call(
        functools.partial(rows_body, first_iteration),
        out_shape=outs,
        in_specs=in_specs,
        out_specs=out_specs,
        scratch_shapes=[
            pltpu.VMEM((BAND_TILES + 1, RHS, TILE), f32),
            pltpu.VMEM(state, f32),
            pltpu.VMEM(state, f32),
            pltpu.VMEM(coefs, f32),
            pltpu.VMEM((EXT + 2, 2, 8, LANES), f32),
            pltpu.VMEM((EXT, RHS, LANES), f32),
            pltpu.SemaphoreType.DMA((2,)),
            pltpu.VMEM((SLOTS, TILE, TILE), bf16),
            pltpu.SemaphoreType.DMA((SLOTS,)),
        ],
        compiler_params=pltpu.CompilerParams(vmem_limit_bytes=44 * MIB),
        cost_estimate=pl.CostEstimate(flops=7 * 10**8, transcendentals=0, bytes_accessed=30 * 10**6),
        name="into_rows_first" if first_iteration else "into_rows_next",
    )(*args)


def share_body(parts_ref, out_ref):
    share = parts_ref[0].astype(f32)
    for peer in range(1, N_ROW):
        share = share + parts_ref[peer].astype(f32)
    out_ref[...] = share


def window_share(parts):
    return pl.pallas_call(
        share_body,
        out_shape=jax.ShapeDtypeStruct(parts.shape[1:], f32),
        in_specs=[VMEM],
        out_specs=VMEM,
        compiler_params=pltpu.CompilerParams(vmem_limit_bytes=6 * MIB),
        name="window_share",
    )(parts)


def pair_body(scal_ref, own_ref, got_ref, share_ref, got_share_ref, out_ref):
    for chip in range(1, CHIPS):
        out_ref[chip] = (own_ref[chip] + got_ref[chip].astype(f32)).astype(bf16)
    total = own_ref[0] + got_ref[0].astype(f32)
    share = share_ref[...] + got_share_ref[...]
    out_ref[0] = (total + jnp.where(scal_ref[SLOTS + 6] == 0, share, 0.0)).astype(bf16)


def pair_sum(scal, own, got, share, got_share):
    return pl.pallas_call(
        pair_body,
        out_shape=jax.ShapeDtypeStruct(got.shape, bf16),
        in_specs=[SMEM, VMEM, VMEM, VMEM, VMEM],
        out_specs=VMEM,
        compiler_params=pltpu.CompilerParams(vmem_limit_bytes=6 * MIB),
        name="pair_sum",
    )(scal, own, got, share, got_share)


def update_body(last, parts_ref, trace_ref, load_ref, *outs):
    for half in range(2):
        lanes = slice(half * TILE, (half + 1) * TILE)
        total = parts_ref[0, half].astype(f32)
        for peer in range(1, CHIPS):
            total = total + parts_ref[peer, half].astype(f32)
        trace = trace_ref[:, lanes]
        trace = trace + COUPLING_STEP * (load_ref[:, lanes] - trace - total)
        outs[0][:, lanes] = trace
        if last:
            outs[1][:, lanes] = total
        else:
            rounded = trace.astype(bf16)
            for copy in range(CHIPS):
                outs[1][copy, half] = rounded


def update(parts, traces, load, last):
    whole = jax.ShapeDtypeStruct(traces.shape, f32)
    return pl.pallas_call(
        functools.partial(update_body, last),
        out_shape=[whole, whole if last else jax.ShapeDtypeStruct(parts.shape, bf16)],
        in_specs=[VMEM, VMEM, VMEM],
        out_specs=[VMEM, VMEM],
        compiler_params=pltpu.CompilerParams(vmem_limit_bytes=8 * MIB),
        name="update_last" if last else "update_next",
    )(parts, traces, load)


def lookup(indices, table):
    levels = jnp.arange(table.shape[0], dtype=jnp.int32)
    return jnp.sum(jnp.where(indices[..., None] == levels, table, 0.0), axis=-1)


def volume_cells(coef_index, coef_table, vol_source, volume_line):
    indices = lax.dynamic_index_in_dim(coef_index, volume_line, 0, keepdims=False)
    source = lax.dynamic_index_in_dim(vol_source, volume_line, 0, keepdims=False)
    spare = ((0, 0), (0, 8 - LAYERS), (0, 0), (0, 0))
    cells = jnp.stack([lookup(indices, coef_table), source]).reshape(2, LAYERS, MID, LANES)
    cells = jnp.pad(cells, spare).transpose(2, 0, 1, 3)

    def ends(x):
        return jnp.concatenate([x[:, :LANES], x[:, -LANES:]], 1)

    high = ends(source).astype(bf16)
    low = (ends(source) - high.astype(f32)).astype(bf16)
    edges = [jnp.pad(e, ((0, 4), (0, 0))) for e in (ends(indices).astype(bf16), high, low)]
    return cells, jnp.pad(jnp.concatenate(edges, 0), ((0, 8), (0, 0)))


def local(
    trace_start, surface_load, panel_tiles, tile_list, surf_map, coef_index, coef_table, vol_source
):
    col_index = lax.axis_index("col")
    row_index = lax.axis_index("row")
    volume_line = jnp.maximum(col_index - DENSE_COLS, 0)
    is_volume = col_index >= DENSE_COLS
    volume_tile = volume_line * N_ROW + row_index
    tile_numbers = jnp.arange(surf_map.shape[0], dtype=jnp.int32)
    quarter = jnp.sum(jnp.where(surf_map == volume_tile, tile_numbers, 0)) % 4
    core = col_index % CORES
    own = [
        is_volume,
        jnp.where(is_volume, 4 * quarter, core),
        jnp.where(is_volume, 4 * quarter + 3, core),
        quarter,
        row_index,
        core,
        core,
        jnp.where(is_volume, 1 - core, core),
    ]
    scal = jnp.concatenate([tile_list, jnp.stack([x.astype(jnp.int32) for x in own])])
    traces = trace_start
    spread = spread_start(traces)
    cells, edges = volume_cells(coef_index, coef_table, vol_source, volume_line)
    panel = in_hbm(panel_tiles)
    cells, edges = lax.optimization_barrier((cells, edges))
    saved = None
    for iteration in range(ITERS):
        last = iteration == ITERS - 1
        near = between_chips(spread)
        far = from_mate(near)
        near, far = near.reshape(TILES, RHS, TILE), far.reshape(TILES, RHS, TILE)
        row_spread = spread_row(scal, near, far, edges if iteration == 0 else None)
        win = exchange(row_spread, "row")
        win_part = into_window(scal, near, far, panel)
        win, _ = lax.optimization_barrier((win, win_part))
        mate_win = from_mate(win)
        parts = exchange(win_part.reshape(N_ROW, 2, RHS, TILE), "row")
        own, mate, *saved = into_rows(
            scal, near, far, win, mate_win, panel, coef_table, cells, saved
        )
        got = from_mate(mate)
        share = window_share(parts)
        summed = between_chips(pair_sum(scal, own, got, share, from_mate(share)))
        traces, spread = update(summed, traces, surface_load, last)
    return (traces, spread)


def solution(mesh):
    return jax.shard_map(
        local,
        mesh=mesh,
        in_specs=(
            P(None, ("col", "row")),
            P(None, ("col", "row")),
            P(("col", "row"), None, None),
            P(("col", "row")),
            P(),
            P(None, None, "row"),
            P(),
            P(None, None, "row"),
        ),
        out_specs=(P(None, ("col", "row")), P(None, ("col", "row"))),
        check_vma=False,
    )
```

```python
import functools

import jax
import jax.numpy as jnp
from jax import lax
from jax.experimental import pallas as pl
from jax.experimental.pallas import tpu as pltpu
from jax.sharding import PartitionSpec as P

ITERS = 2
SWEEPS = 4
COUPLING_STEP = 0.3
JACOBI_WEIGHT = 0.8
CELL_MASS = 0.05

RHS = 32
TILE = 512
LANES = 128
N_COL = 16
N_ROW = 8
CORES = 2
CHIPS = N_COL // CORES
TILES = 2 * CHIPS
DENSE_COLS = 12
LAYERS = 4
SLOTS = 43
GROUP = 4
UNROLL = 17
COEFS = 16
BAND_TILES = 32
WIN_TILES = 16
MID = 32
EXT = MID + 2
MIB = 1 << 20

VMEM = pl.BlockSpec(memory_space=pltpu.VMEM)
SMEM = pl.BlockSpec(memory_space=pltpu.SMEM)
ANY = pl.BlockSpec(memory_space=pl.ANY)
f32 = jnp.float32
bf16 = jnp.bfloat16


def in_hbm(x):
    return pltpu.with_memory_space_constraint(x, pltpu.HBM)


def exchange(x, axis):
    return lax.all_to_all(x, axis, 0, 0, tiled=True)


def between_chips(x):
    groups = [list(range(core, N_COL, CORES)) for core in range(CORES)]
    return lax.all_to_all(x, "col", 0, 0, axis_index_groups=groups, tiled=True)


def from_mate(x):
    return lax.ppermute(x, "col", [(i, i ^ 1) for i in range(N_COL)])


def pick(near_ref, far_ref, is_far, index):
    return jnp.where(is_far == 0, near_ref[index], far_ref[index])


def start_body(trace_ref, out_ref):
    for half in range(2):
        rounded = trace_ref[:, half * TILE : (half + 1) * TILE].astype(bf16)
        for copy in range(CHIPS):
            out_ref[copy, half] = rounded


def spread_start(trace_start):
    return pl.pallas_call(
        start_body,
        out_shape=jax.ShapeDtypeStruct((CHIPS, 2, RHS, TILE), bf16),
        in_specs=[VMEM],
        out_specs=VMEM,
        compiler_params=pltpu.CompilerParams(vmem_limit_bytes=6 * MIB),
        name="spread_start",
    )(trace_start)


def row_body(first_iteration, scal_ref, near_ref, far_ref, *refs):
    out_ref = refs[-1]
    mine = pick(near_ref, far_ref, scal_ref[SLOTS + 5], scal_ref[SLOTS + 1])
    tail = pick(near_ref, far_ref, scal_ref[SLOTS + 7], scal_ref[SLOTS + 2])
    for peer in range(N_ROW):
        out_ref[peer, :, : 3 * LANES] = mine[:, : 3 * LANES]
        out_ref[peer, :, 3 * LANES :] = tail[:, 3 * LANES :]
    if first_iteration:

        @pl.when(scal_ref[SLOTS] == 1)
        def _():
            for peer in range(N_ROW):
                out_ref[peer, :, LANES : 3 * LANES] = refs[0][...]


def spread_row(scal, near, far, edges):
    first_iteration = edges is not None
    args = [scal, near, far] + ([edges] if first_iteration else [])
    return pl.pallas_call(
        functools.partial(row_body, first_iteration),
        out_shape=jax.ShapeDtypeStruct((N_ROW, RHS, TILE), bf16),
        in_specs=[SMEM] + [VMEM] * (len(args) - 1),
        out_specs=VMEM,
        compiler_params=pltpu.CompilerParams(vmem_limit_bytes=6 * MIB),
        name="spread_row",
    )(*args)


def interleave(near_ref, far_ref, core, run, out_ref):
    for index in range(near_ref.shape[0]):
        block, part = index // run, index % run
        out_ref[(2 * block + core) * run + part] = near_ref[index]
        out_ref[(2 * block + 1 - core) * run + part] = far_ref[index]


def for_slots(scal_ref, panel_ref, buffer_ref, sems, acc_ref, prepare, do_slot):
    def fetch(slot):
        return pltpu.make_async_copy(panel_ref.at[slot], buffer_ref.at[slot], sems.at[slot])

    def start(slot, carry):
        fetch(slot).start()
        return carry

    lax.fori_loop(0, SLOTS, start, 0)
    acc_ref[...] = jnp.zeros_like(acc_ref)
    prepare()

    def place(slot):
        ident = scal_ref[slot]
        named = ident >= 0
        safe = jnp.maximum(ident, 0)
        row_tile = lax.shift_right_logical(safe, 8)
        col_tile = jnp.bitwise_and(safe, 15)
        shard = lax.shift_right_logical(row_tile, 4)
        do_slot(slot, named, shard, jnp.bitwise_and(row_tile, 1), col_tile)

    def group(index, carry):
        for extra in range(GROUP):
            fetch(index * GROUP + extra).wait()
        for extra in range(GROUP):
            place(index * GROUP + extra)
        return carry

    lax.fori_loop(0, SLOTS // GROUP, group, 0)
    for slot in range(SLOTS // GROUP * GROUP, SLOTS):
        fetch(slot).wait()
        place(slot)


def window_body(scal_ref, near_ref, far_ref, panel_ref, win_out, win_acc, buffer_ref, sems, traces_ref):
    is_volume = scal_ref[SLOTS] == 1

    @pl.when(jnp.logical_not(is_volume))
    def _():
        core = scal_ref[SLOTS + 6]

        def one_slot(slot, named, shard, half, col_tile):
            win_acc[jnp.where(named, col_tile, WIN_TILES)] += jnp.dot(
                traces_ref[2 * shard + half], buffer_ref[slot], preferred_element_type=f32
            )

        prepare = functools.partial(interleave, near_ref, far_ref, core, 2, traces_ref)
        for_slots(scal_ref, panel_ref, buffer_ref, sems, win_acc, prepare, one_slot)

        win_out[...] = win_acc[:WIN_TILES].astype(bf16)

    @pl.when(is_volume)
    def _():
        win_out[...] = jnp.zeros_like(win_out)


def into_window(scal, near, far, panel):
    return pl.pallas_call(
        window_body,
        out_shape=jax.ShapeDtypeStruct((WIN_TILES, RHS, TILE), bf16),
        in_specs=[SMEM, VMEM, VMEM, ANY],
        out_specs=VMEM,
        scratch_shapes=[
            pltpu.VMEM((WIN_TILES + 1, RHS, TILE), f32),
            pltpu.VMEM((SLOTS, TILE, TILE), bf16),
            pltpu.SemaphoreType.DMA((SLOTS,)),
            pltpu.VMEM((BAND_TILES, RHS, TILE), bf16),
        ],
        compiler_params=pltpu.CompilerParams(vmem_limit_bytes=44 * MIB),
        cost_estimate=pl.CostEstimate(flops=7 * 10**8, transcendentals=0, bytes_accessed=25 * 10**6),
        name="into_window",
    )(scal, near, far, panel)


def weigh(scal_ref, table_ref, index_ref, source_ref, win_ref, cell_ref, coef_ref):
    row = scal_ref[SLOTS + 4]
    before = jnp.maximum(row - 1, 0)
    after = jnp.minimum(row + 1, N_ROW - 1)
    layer = lax.broadcasted_iota(jnp.int32, (8, LANES), 0)
    lane = lax.broadcasted_iota(jnp.int32, (8, LANES), 1)
    nothing = jnp.zeros((8, LANES), f32)
    cell_ref[...] = jnp.zeros_like(cell_ref)
    for chunk, source, start, here in (
        (0, before, 2 * LANES, row > 0),
        (EXT - 1, after, LANES, row < N_ROW - 1),
    ):
        sent = win_ref[source, :, start : start + LANES].astype(f32)
        k = nothing
        for level in range(COEFS):
            k = jnp.where(sent[0:8] == float(level), table_ref[level], k)
        cell_ref[chunk + 1, 0] = jnp.where((layer < LAYERS) & here, k, 0.0)
        cell_ref[chunk + 1, 1] = jnp.where(here, sent[8:16] + sent[16:24], 0.0)

    for chunk in range(MID):
        lanes = slice(chunk * LANES, (chunk + 1) * LANES)
        indices = index_ref[:, lanes]
        k = jnp.zeros((LAYERS, LANES), f32)
        for level in range(COEFS):
            k = jnp.where(indices == level, table_ref[level], k)
        cell_ref[chunk + 2, 0, :LAYERS] = k
        cell_ref[chunk + 2, 1, :LAYERS] = source_ref[:, lanes]

    def one_chunk(chunk, carry):
        k = cell_ref[chunk + 1, 0]
        left = pltpu.roll(jnp.where(lane == LANES - 1, cell_ref[chunk, 0], k), 1, 1)
        right = pltpu.roll(jnp.where(lane == 0, cell_ref[chunk + 2, 0], k), LANES - 1, 1)
        left = 0.5 * (k + left)
        right = 0.5 * (k + right)
        lower = jnp.where(layer < LAYERS - 1, 0.5 * (k + pltpu.roll(k, 7, 0)), 0.0)
        upper = jnp.where(layer == 0, k, pltpu.roll(lower, 1, 0))
        inside = ((chunk > 0) | (row > 0)) & ((chunk < EXT - 1) | (row < N_ROW - 1))
        scale = jnp.where(inside, JACOBI_WEIGHT / (left + right + upper + lower + CELL_MASS), 0.0)
        coef_ref[chunk, 0:8] = left * scale
        coef_ref[chunk, 8:16] = right * scale
        coef_ref[chunk, 16:24] = upper * scale
        coef_ref[chunk, 24:32] = lower * scale
        coef_ref[chunk, 32:40] = cell_ref[chunk + 1, 1] * scale
        coef_ref[chunk, 40:48] = k
        return carry

    lax.fori_loop(0, EXT, one_chunk, 0, unroll=2)


def relax(scal_ref, near_ref, far_ref, win_ref, coef_ref, states, top_ref):
    quarter = scal_ref[SLOTS + 3]
    row = scal_ref[SLOTS + 4]
    core = scal_ref[SLOTS + 6]
    before = jnp.maximum(row - 1, 0)
    after = jnp.minimum(row + 1, N_ROW - 1)
    top_ref[0] = win_ref[before, :, TILE - LANES :].astype(f32)
    top_ref[EXT - 1] = win_ref[after, :, :LANES].astype(f32)
    for tile in range(8):
        is_far = jnp.bitwise_xor(tile // 2 % 2, core)
        tops = pick(near_ref, far_ref, is_far, 4 * quarter + tile // 4 * 2 + tile % 2)
        for part in range(4):
            top_ref[4 * tile + part + 1] = tops[:, part * LANES : (part + 1) * LANES].astype(f32)
    lane = lax.broadcasted_iota(jnp.int32, (RHS, LANES), 1)
    is_first = lane == 0
    is_last = lane == LANES - 1

    def sweep(source_ref, target_ref):
        def one_chunk(chunk, carry):
            upper = top_ref[chunk]
            centre = source_ref[chunk + 1, 0]
            for l in range(LAYERS):
                left = pltpu.roll(jnp.where(is_last, source_ref[chunk, l], centre), 1, 1)
                right = pltpu.roll(jnp.where(is_first, source_ref[chunk + 2, l], centre), LANES - 1, 1)
                value = (
                    (1.0 - JACOBI_WEIGHT) * centre
                    + coef_ref[chunk, l : 1 + l, :] * left
                    + coef_ref[chunk, 8 + l : 9 + l, :] * right
                    + coef_ref[chunk, 16 + l : 17 + l, :] * upper
                    + coef_ref[chunk, 32 + l : 33 + l, :]
                )
                if l + 1 < LAYERS:
                    below = source_ref[chunk + 1, l + 1]
                    value = value + coef_ref[chunk, 24 + l : 25 + l, :] * below
                    upper, centre = centre, below
                target_ref[chunk + 1, l] = value
            return carry

        lax.fori_loop(0, EXT, one_chunk, 0, unroll=UNROLL)

    for step in range(SWEEPS):
        sweep(states[step % 2], states[1 - step % 2])


def rows_body(first_iteration, scal_ref, near_ref, far_ref, win_ref, mate_win_ref, panel_ref, *refs):
    if first_iteration:
        table_ref, all_index_ref, all_source_ref, own_out, mate_out, state_out, coef_out = refs[:7]
        refs = refs[7:]
    else:
        state_in, coef_in, own_out, mate_out = refs[:4]
        refs = refs[4:]
    band_acc, state_a, state_b, coef_ref, cell_ref, top_ref, sems, buffer_ref, panel_sems, traces_ref = refs[:10]
    if first_iteration:
        index_ref, source_ref = refs[10:]
    is_volume = scal_ref[SLOTS] == 1
    core = scal_ref[SLOTS + 6]

    @pl.when(jnp.logical_not(is_volume))
    def _():
        def one_slot(slot, named, shard, half, col_tile):
            band_acc[jnp.where(named, 2 * shard + half, BAND_TILES)] += lax.dot_general(
                traces_ref[col_tile],
                buffer_ref[slot],
                (((1,), (1,)), ((), ())),
                preferred_element_type=f32,
            )

        prepare = functools.partial(interleave, win_ref, mate_win_ref, core, 1, traces_ref)
        for_slots(scal_ref, panel_ref, buffer_ref, panel_sems, band_acc, prepare, one_slot)

    @pl.when(is_volume)
    def _():
        guard = jnp.zeros((LAYERS, RHS, LANES), f32)
        state_b[0] = guard
        state_b[EXT + 1] = guard
        if first_iteration:
            line = scal_ref[SLOTS + 8]
            loads = [
                pltpu.make_async_copy(all_index_ref.at[line], index_ref, sems.at[0]),
                pltpu.make_async_copy(all_source_ref.at[line], source_ref, sems.at[1]),
            ]
            for load in loads:
                load.start()
            state_a[...] = jnp.zeros_like(state_a)
            for load in loads:
                load.wait()
            weigh(scal_ref, table_ref, index_ref, source_ref, win_ref, cell_ref, coef_ref)
        else:
            loads = [
                pltpu.make_async_copy(state_in, state_a, sems.at[0]),
                pltpu.make_async_copy(coef_in, coef_ref, sems.at[1]),
            ]
            for load in loads:
                load.start()
            for load in loads:
                load.wait()
        relax(scal_ref, near_ref, far_ref, win_ref, coef_ref, (state_a, state_b), top_ref)
        if first_iteration:
            saves = [
                pltpu.make_async_copy(state_a, state_out, sems.at[0]),
                pltpu.make_async_copy(coef_ref, coef_out, sems.at[1]),
            ]
            for save in saves:
                save.start()
        band_acc[...] = jnp.zeros_like(band_acc)
        first = 8 * scal_ref[SLOTS + 3]
        for chunk in range(MID):
            start = chunk % 4 * LANES
            flux = coef_ref[chunk + 1, 40:41, :] * (top_ref[chunk + 1] - state_a[chunk + 2, 0])
            band_acc[first + chunk // 4, :, start : start + LANES] = flux

        if first_iteration:
            for save in saves:
                save.wait()

    for chip in range(CHIPS):
        own_out[chip] = band_acc[pl.ds(4 * chip + 2 * core, 2)]
        mate_out[chip] = band_acc[pl.ds(4 * chip + 2 - 2 * core, 2)].astype(bf16)


def into_rows(scal, near, far, win, mate_win, panel, table, indices, sources, saved):
    first_iteration = saved is None
    outs = [
        jax.ShapeDtypeStruct((CHIPS, 2, RHS, TILE), f32),
        jax.ShapeDtypeStruct((CHIPS, 2, RHS, TILE), bf16),
    ]
    out_specs = [VMEM, VMEM]
    in_specs = [SMEM, VMEM, VMEM, VMEM, VMEM, ANY]
    args = [scal, near, far, win, mate_win, panel]
    state = (EXT + 2, LAYERS, RHS, LANES)
    coefs = (EXT, 48, LANES)
    if first_iteration:
        outs += [pltpu.HBM(state, f32), pltpu.HBM(coefs, f32)]
        out_specs += [ANY, ANY]
        in_specs += [SMEM, ANY, ANY]
        args += [table, in_hbm(indices), in_hbm(sources)]
    else:
        in_specs += [ANY, ANY]
        args += [in_hbm(x) for x in saved]
    cells = (LAYERS, MID * LANES)
    lines = [pltpu.VMEM(cells, jnp.int32), pltpu.VMEM(cells, f32)] if first_iteration else []
    return pl.pallas_call(
        functools.partial(rows_body, first_iteration),
        out_shape=outs,
        in_specs=in_specs,
        out_specs=out_specs,
        scratch_shapes=[
            pltpu.VMEM((BAND_TILES + 1, RHS, TILE), f32),
            pltpu.VMEM(state, f32),
            pltpu.VMEM(state, f32),
            pltpu.VMEM(coefs, f32),
            pltpu.VMEM((EXT + 2, 2, 8, LANES), f32),
            pltpu.VMEM((EXT, RHS, LANES), f32),
            pltpu.SemaphoreType.DMA((2,)),
            pltpu.VMEM((SLOTS, TILE, TILE), bf16),
            pltpu.SemaphoreType.DMA((SLOTS,)),
            pltpu.VMEM((WIN_TILES, RHS, TILE), bf16),
            *lines,
        ],
        compiler_params=pltpu.CompilerParams(vmem_limit_bytes=44 * MIB),
        cost_estimate=pl.CostEstimate(flops=7 * 10**8, transcendentals=0, bytes_accessed=30 * 10**6),
        name="into_rows_first" if first_iteration else "into_rows_next",
    )(*args)


def share_body(parts_ref, out_ref):
    share = parts_ref[0].astype(f32)
    for peer in range(1, N_ROW):
        share = share + parts_ref[peer].astype(f32)
    out_ref[...] = share


def window_share(parts):
    return pl.pallas_call(
        share_body,
        out_shape=jax.ShapeDtypeStruct(parts.shape[1:], f32),
        in_specs=[VMEM],
        out_specs=VMEM,
        compiler_params=pltpu.CompilerParams(vmem_limit_bytes=6 * MIB),
        name="window_share",
    )(parts)


def pair_body(scal_ref, own_ref, got_ref, share_ref, got_share_ref, out_ref):
    for chip in range(1, CHIPS):
        out_ref[chip] = (own_ref[chip] + got_ref[chip].astype(f32)).astype(bf16)
    total = own_ref[0] + got_ref[0].astype(f32)
    share = share_ref[...] + got_share_ref[...]
    out_ref[0] = (total + jnp.where(scal_ref[SLOTS + 6] == 0, share, 0.0)).astype(bf16)


def pair_sum(scal, own, got, share, got_share):
    return pl.pallas_call(
        pair_body,
        out_shape=jax.ShapeDtypeStruct(got.shape, bf16),
        in_specs=[SMEM, VMEM, VMEM, VMEM, VMEM],
        out_specs=VMEM,
        compiler_params=pltpu.CompilerParams(vmem_limit_bytes=6 * MIB),
        name="pair_sum",
    )(scal, own, got, share, got_share)


def update_body(last, parts_ref, trace_ref, load_ref, *outs):
    for half in range(2):
        lanes = slice(half * TILE, (half + 1) * TILE)
        total = parts_ref[0, half].astype(f32)
        for peer in range(1, CHIPS):
            total = total + parts_ref[peer, half].astype(f32)
        trace = trace_ref[:, lanes]
        trace = trace + COUPLING_STEP * (load_ref[:, lanes] - trace - total)
        outs[0][:, lanes] = trace
        if last:
            outs[1][:, lanes] = total
        else:
            rounded = trace.astype(bf16)
            for copy in range(CHIPS):
                outs[1][copy, half] = rounded


def update(parts, traces, load, last):
    whole = jax.ShapeDtypeStruct(traces.shape, f32)
    return pl.pallas_call(
        functools.partial(update_body, last),
        out_shape=[whole, whole if last else jax.ShapeDtypeStruct(parts.shape, bf16)],
        in_specs=[VMEM, VMEM, VMEM],
        out_specs=[VMEM, VMEM],
        compiler_params=pltpu.CompilerParams(vmem_limit_bytes=8 * MIB),
        name="update_last" if last else "update_next",
    )(parts, traces, load)


def volume_edges(coef_index, vol_source, volume_line):
    indices = lax.dynamic_index_in_dim(coef_index, volume_line, 0, keepdims=False)
    source = lax.dynamic_index_in_dim(vol_source, volume_line, 0, keepdims=False)

    def ends(x):
        return jnp.concatenate([x[:, :LANES], x[:, -LANES:]], 1)

    high = ends(source).astype(bf16)
    low = (ends(source) - high.astype(f32)).astype(bf16)
    edges = [jnp.pad(e, ((0, 4), (0, 0))) for e in (ends(indices).astype(bf16), high, low)]
    return jnp.pad(jnp.concatenate(edges, 0), ((0, 8), (0, 0)))


def local(
    trace_start, surface_load, panel_tiles, tile_list, surf_map, coef_index, coef_table, vol_source
):
    col_index = lax.axis_index("col")
    row_index = lax.axis_index("row")
    volume_line = jnp.maximum(col_index - DENSE_COLS, 0)
    is_volume = col_index >= DENSE_COLS
    volume_tile = volume_line * N_ROW + row_index
    tile_numbers = jnp.arange(surf_map.shape[0], dtype=jnp.int32)
    quarter = jnp.sum(jnp.where(surf_map == volume_tile, tile_numbers, 0)) % 4
    core = col_index % CORES
    own = [
        is_volume,
        jnp.where(is_volume, 4 * quarter, core),
        jnp.where(is_volume, 4 * quarter + 3, core),
        quarter,
        row_index,
        core,
        core,
        jnp.where(is_volume, 1 - core, core),
        volume_line,
    ]
    scal = jnp.concatenate([tile_list, jnp.stack([x.astype(jnp.int32) for x in own])])
    traces = trace_start
    spread = spread_start(traces)
    edges = volume_edges(coef_index, vol_source, volume_line)
    panel = in_hbm(panel_tiles)
    saved = None
    for iteration in range(ITERS):
        last = iteration == ITERS - 1
        near = between_chips(spread)
        far = from_mate(near)
        near, far = near.reshape(TILES, RHS, TILE), far.reshape(TILES, RHS, TILE)
        row_spread = spread_row(scal, near, far, edges if iteration == 0 else None)
        win = exchange(row_spread, "row")
        win_part = into_window(scal, near, far, panel)
        win, _ = lax.optimization_barrier((win, win_part))
        mate_win = from_mate(win)
        parts = exchange(win_part.reshape(N_ROW, 2, RHS, TILE), "row")
        own, mate, *saved = into_rows(
            scal, near, far, win, mate_win, panel, coef_table, coef_index, vol_source, saved
        )
        got = from_mate(mate)
        share = window_share(parts)
        summed = between_chips(pair_sum(scal, own, got, share, from_mate(share)))
        traces, spread = update(summed, traces, surface_load, last)
    return (traces, spread)


def solution(mesh):
    return jax.shard_map(
        local,
        mesh=mesh,
        in_specs=(
            P(None, ("col", "row")),
            P(None, ("col", "row")),
            P(("col", "row"), None, None),
            P(("col", "row")),
            P(),
            P(None, None, "row"),
            P(),
            P(None, None, "row"),
        ),
        out_specs=(P(None, ("col", "row")), P(None, ("col", "row"))),
        check_vma=False,
    )
```

```python
import functools

import jax
import jax.numpy as jnp
from jax import lax
from jax.experimental import pallas as pl
from jax.experimental.pallas import tpu as pltpu
from jax.sharding import PartitionSpec as P

ITERS = 2
SWEEPS = 4
COUPLING_STEP = 0.3
JACOBI_WEIGHT = 0.8
CELL_MASS = 0.05

RHS = 32
TILE = 512
LANES = 128
N_COL = 16
N_ROW = 8
CORES = 2
CHIPS = N_COL // CORES
TILES = 2 * CHIPS
DENSE_COLS = 12
LAYERS = 4
SLOTS = 43
GROUP = 6
UNROLL = 17
COEFS = 16
BAND_TILES = 32
WIN_TILES = 16
MID = 32
EXT = MID + 2
MIB = 1 << 20

VMEM = pl.BlockSpec(memory_space=pltpu.VMEM)
SMEM = pl.BlockSpec(memory_space=pltpu.SMEM)
ANY = pl.BlockSpec(memory_space=pl.ANY)
f32 = jnp.float32
bf16 = jnp.bfloat16


def in_hbm(x):
    return pltpu.with_memory_space_constraint(x, pltpu.HBM)


def exchange(x, axis):
    return lax.all_to_all(x, axis, 0, 0, tiled=True)


def between_chips(x):
    groups = [list(range(core, N_COL, CORES)) for core in range(CORES)]
    return lax.all_to_all(x, "col", 0, 0, axis_index_groups=groups, tiled=True)


def from_mate(x):
    return lax.ppermute(x, "col", [(i, i ^ 1) for i in range(N_COL)])


def pick(near_ref, far_ref, is_far, index):
    return jnp.where(is_far == 0, near_ref[index], far_ref[index])


def send_copies(block_ref, out_ref, sems):
    copies = [
        pltpu.make_async_copy(block_ref, out_ref.at[peer], sems.at[peer])
        for peer in range(out_ref.shape[0])
    ]
    for copy in copies:
        copy.start()
    for copy in copies:
        copy.wait()


def start_body(trace_ref, out_ref, block_ref, sems):
    for half in range(2):
        block_ref[half] = trace_ref[:, half * TILE : (half + 1) * TILE].astype(bf16)
    send_copies(block_ref, out_ref, sems)


def spread_start(trace_start):
    return pl.pallas_call(
        start_body,
        out_shape=pltpu.HBM((CHIPS, 2, RHS, TILE), bf16),
        in_specs=[VMEM],
        out_specs=ANY,
        scratch_shapes=[pltpu.VMEM((2, RHS, TILE), bf16), pltpu.SemaphoreType.DMA((CHIPS,))],
        compiler_params=pltpu.CompilerParams(vmem_limit_bytes=6 * MIB),
        name="spread_start",
    )(trace_start)


def row_body(first_iteration, scal_ref, near_ref, far_ref, *refs):
    out_ref, block_ref, sems = refs[-3:]
    mine = pick(near_ref, far_ref, scal_ref[SLOTS + 5], scal_ref[SLOTS + 1])
    tail = pick(near_ref, far_ref, scal_ref[SLOTS + 7], scal_ref[SLOTS + 2])
    block_ref[:, : 3 * LANES] = mine[:, : 3 * LANES]
    block_ref[:, 3 * LANES :] = tail[:, 3 * LANES :]
    if first_iteration:

        @pl.when(scal_ref[SLOTS] == 1)
        def _():
            block_ref[:, LANES : 3 * LANES] = refs[0][...]

    send_copies(block_ref, out_ref, sems)


def spread_row(scal, near, far, edges):
    first_iteration = edges is not None
    args = [scal, near, far] + ([edges] if first_iteration else [])
    return pl.pallas_call(
        functools.partial(row_body, first_iteration),
        out_shape=pltpu.HBM((N_ROW, RHS, TILE), bf16),
        in_specs=[SMEM] + [VMEM] * (len(args) - 1),
        out_specs=ANY,
        scratch_shapes=[pltpu.VMEM((RHS, TILE), bf16), pltpu.SemaphoreType.DMA((N_ROW,))],
        compiler_params=pltpu.CompilerParams(vmem_limit_bytes=6 * MIB),
        name="spread_row",
    )(*args)


def interleave(near_ref, far_ref, core, run, out_ref):
    for index in range(near_ref.shape[0]):
        block, part = index // run, index % run
        out_ref[(2 * block + core) * run + part] = near_ref[index]
        out_ref[(2 * block + 1 - core) * run + part] = far_ref[index]


def for_slots(scal_ref, panel_ref, buffer_ref, sems, acc_ref, prepare, do_slot):
    def fetch(slot):
        return pltpu.make_async_copy(panel_ref.at[slot], buffer_ref.at[slot], sems.at[slot])

    def start(slot, carry):
        fetch(slot).start()
        return carry

    lax.fori_loop(0, SLOTS, start, 0)
    acc_ref[...] = jnp.zeros_like(acc_ref)
    prepare()

    def place(slot):
        ident = scal_ref[slot]
        named = ident >= 0
        safe = jnp.maximum(ident, 0)
        row_tile = lax.shift_right_logical(safe, 8)
        col_tile = jnp.bitwise_and(safe, 15)
        shard = lax.shift_right_logical(row_tile, 4)
        do_slot(slot, named, shard, jnp.bitwise_and(row_tile, 1), col_tile)

    def group(index, carry):
        for extra in range(GROUP):
            fetch(index * GROUP + extra).wait()
        for extra in range(GROUP):
            place(index * GROUP + extra)
        return carry

    lax.fori_loop(0, SLOTS // GROUP, group, 0)
    for slot in range(SLOTS // GROUP * GROUP, SLOTS):
        fetch(slot).wait()
        place(slot)


def window_body(scal_ref, near_ref, far_ref, panel_ref, win_out, win_acc, buffer_ref, sems, traces_ref):
    is_volume = scal_ref[SLOTS] == 1

    @pl.when(jnp.logical_not(is_volume))
    def _():
        core = scal_ref[SLOTS + 6]

        def one_slot(slot, named, shard, half, col_tile):
            win_acc[jnp.where(named, col_tile, WIN_TILES)] += jnp.dot(
                traces_ref[2 * shard + half], buffer_ref[slot], preferred_element_type=f32
            )

        prepare = functools.partial(interleave, near_ref, far_ref, core, 2, traces_ref)
        for_slots(scal_ref, panel_ref, buffer_ref, sems, win_acc, prepare, one_slot)

        win_out[...] = win_acc[:WIN_TILES].astype(bf16)

    @pl.when(is_volume)
    def _():
        win_out[...] = jnp.zeros_like(win_out)


def into_window(scal, near, far, panel):
    return pl.pallas_call(
        window_body,
        out_shape=jax.ShapeDtypeStruct((WIN_TILES, RHS, TILE), bf16),
        in_specs=[SMEM, VMEM, VMEM, ANY],
        out_specs=VMEM,
        scratch_shapes=[
            pltpu.VMEM((WIN_TILES + 1, RHS, TILE), f32),
            pltpu.VMEM((SLOTS, TILE, TILE), bf16),
            pltpu.SemaphoreType.DMA((SLOTS,)),
            pltpu.VMEM((BAND_TILES, RHS, TILE), bf16),
        ],
        compiler_params=pltpu.CompilerParams(vmem_limit_bytes=44 * MIB),
        cost_estimate=pl.CostEstimate(flops=7 * 10**8, transcendentals=0, bytes_accessed=25 * 10**6),
        name="into_window",
    )(scal, near, far, panel)


def weigh(scal_ref, table_ref, index_ref, source_ref, win_ref, cell_ref, coef_ref):
    row = scal_ref[SLOTS + 4]
    before = jnp.maximum(row - 1, 0)
    after = jnp.minimum(row + 1, N_ROW - 1)
    layer = lax.broadcasted_iota(jnp.int32, (8, LANES), 0)
    lane = lax.broadcasted_iota(jnp.int32, (8, LANES), 1)
    nothing = jnp.zeros((8, LANES), f32)
    cell_ref[...] = jnp.zeros_like(cell_ref)
    for chunk, source, start, here in (
        (0, before, 2 * LANES, row > 0),
        (EXT - 1, after, LANES, row < N_ROW - 1),
    ):
        sent = win_ref[source, :, start : start + LANES].astype(f32)
        k = nothing
        for level in range(COEFS):
            k = jnp.where(sent[0:8] == float(level), table_ref[level], k)
        cell_ref[chunk + 1, 0] = jnp.where((layer < LAYERS) & here, k, 0.0)
        cell_ref[chunk + 1, 1] = jnp.where(here, sent[8:16] + sent[16:24], 0.0)

    for chunk in range(MID):
        lanes = slice(chunk * LANES, (chunk + 1) * LANES)
        indices = index_ref[:, lanes]
        k = jnp.zeros((LAYERS, LANES), f32)
        for level in range(COEFS):
            k = jnp.where(indices == level, table_ref[level], k)
        cell_ref[chunk + 2, 0, :LAYERS] = k
        cell_ref[chunk + 2, 1, :LAYERS] = source_ref[:, lanes]

    def one_chunk(chunk, carry):
        k = cell_ref[chunk + 1, 0]
        left = pltpu.roll(jnp.where(lane == LANES - 1, cell_ref[chunk, 0], k), 1, 1)
        right = pltpu.roll(jnp.where(lane == 0, cell_ref[chunk + 2, 0], k), LANES - 1, 1)
        left = 0.5 * (k + left)
        right = 0.5 * (k + right)
        lower = jnp.where(layer < LAYERS - 1, 0.5 * (k + pltpu.roll(k, 7, 0)), 0.0)
        upper = jnp.where(layer == 0, k, pltpu.roll(lower, 1, 0))
        inside = ((chunk > 0) | (row > 0)) & ((chunk < EXT - 1) | (row < N_ROW - 1))
        scale = jnp.where(inside, JACOBI_WEIGHT / (left + right + upper + lower + CELL_MASS), 0.0)
        coef_ref[chunk, 0:8] = left * scale
        coef_ref[chunk, 8:16] = right * scale
        coef_ref[chunk, 16:24] = upper * scale
        coef_ref[chunk, 24:32] = lower * scale
        coef_ref[chunk, 32:40] = cell_ref[chunk + 1, 1] * scale
        coef_ref[chunk, 40:48] = k
        return carry

    lax.fori_loop(0, EXT, one_chunk, 0, unroll=2)


def relax(scal_ref, near_ref, far_ref, win_ref, coef_ref, states, top_ref):
    quarter = scal_ref[SLOTS + 3]
    row = scal_ref[SLOTS + 4]
    core = scal_ref[SLOTS + 6]
    before = jnp.maximum(row - 1, 0)
    after = jnp.minimum(row + 1, N_ROW - 1)
    top_ref[0] = win_ref[before, :, TILE - LANES :].astype(f32)
    top_ref[EXT - 1] = win_ref[after, :, :LANES].astype(f32)
    for tile in range(8):
        is_far = jnp.bitwise_xor(tile // 2 % 2, core)
        tops = pick(near_ref, far_ref, is_far, 4 * quarter + tile // 4 * 2 + tile % 2)
        for part in range(4):
            top_ref[4 * tile + part + 1] = tops[:, part * LANES : (part + 1) * LANES].astype(f32)
    lane = lax.broadcasted_iota(jnp.int32, (RHS, LANES), 1)
    is_first = lane == 0
    is_last = lane == LANES - 1

    def sweep(source_ref, target_ref):
        def one_chunk(chunk, carry):
            upper = top_ref[chunk]
            centre = source_ref[chunk + 1, 0]
            for l in range(LAYERS):
                left = pltpu.roll(jnp.where(is_last, source_ref[chunk, l], centre), 1, 1)
                right = pltpu.roll(jnp.where(is_first, source_ref[chunk + 2, l], centre), LANES - 1, 1)
                value = (
                    (1.0 - JACOBI_WEIGHT) * centre
                    + coef_ref[chunk, l : 1 + l, :] * left
                    + coef_ref[chunk, 8 + l : 9 + l, :] * right
                    + coef_ref[chunk, 16 + l : 17 + l, :] * upper
                    + coef_ref[chunk, 32 + l : 33 + l, :]
                )
                if l + 1 < LAYERS:
                    below = source_ref[chunk + 1, l + 1]
                    value = value + coef_ref[chunk, 24 + l : 25 + l, :] * below
                    upper, centre = centre, below
                target_ref[chunk + 1, l] = value
            return carry

        lax.fori_loop(0, EXT, one_chunk, 0, unroll=UNROLL)

    for step in range(SWEEPS):
        sweep(states[step % 2], states[1 - step % 2])


def rows_body(first_iteration, scal_ref, near_ref, far_ref, win_ref, mate_win_ref, panel_ref, *refs):
    if first_iteration:
        table_ref, all_index_ref, all_source_ref, own_out, mate_out, state_out, coef_out = refs[:7]
        refs = refs[7:]
    else:
        state_in, coef_in, own_out, mate_out = refs[:4]
        refs = refs[4:]
    band_acc, state_a, state_b, coef_ref, cell_ref, top_ref, sems, buffer_ref, panel_sems = refs[:9]
    traces_ref, mate_ref, mate_sems = refs[9:12]
    if first_iteration:
        index_ref, source_ref = refs[12:]
    is_volume = scal_ref[SLOTS] == 1
    core = scal_ref[SLOTS + 6]

    @pl.when(jnp.logical_not(is_volume))
    def _():
        def one_slot(slot, named, shard, half, col_tile):
            band_acc[jnp.where(named, 2 * shard + half, BAND_TILES)] += lax.dot_general(
                traces_ref[col_tile],
                buffer_ref[slot],
                (((1,), (1,)), ((), ())),
                preferred_element_type=f32,
            )

        prepare = functools.partial(interleave, win_ref, mate_win_ref, core, 1, traces_ref)
        for_slots(scal_ref, panel_ref, buffer_ref, panel_sems, band_acc, prepare, one_slot)

    @pl.when(is_volume)
    def _():
        guard = jnp.zeros((LAYERS, RHS, LANES), f32)
        state_b[0] = guard
        state_b[EXT + 1] = guard
        if first_iteration:
            line = scal_ref[SLOTS + 8]
            loads = [
                pltpu.make_async_copy(all_index_ref.at[line], index_ref, sems.at[0]),
                pltpu.make_async_copy(all_source_ref.at[line], source_ref, sems.at[1]),
            ]
            for load in loads:
                load.start()
            state_a[...] = jnp.zeros_like(state_a)
            for load in loads:
                load.wait()
            weigh(scal_ref, table_ref, index_ref, source_ref, win_ref, cell_ref, coef_ref)
        else:
            loads = [
                pltpu.make_async_copy(state_in, state_a, sems.at[0]),
                pltpu.make_async_copy(coef_in, coef_ref, sems.at[1]),
            ]
            for load in loads:
                load.start()
            for load in loads:
                load.wait()
        relax(scal_ref, near_ref, far_ref, win_ref, coef_ref, (state_a, state_b), top_ref)
        if first_iteration:
            saves = [
                pltpu.make_async_copy(state_a, state_out, sems.at[0]),
                pltpu.make_async_copy(coef_ref, coef_out, sems.at[1]),
            ]
            for save in saves:
                save.start()
        band_acc[...] = jnp.zeros_like(band_acc)
        first = 8 * scal_ref[SLOTS + 3]
        for chunk in range(MID):
            start = chunk % 4 * LANES
            flux = coef_ref[chunk + 1, 40:41, :] * (top_ref[chunk + 1] - state_a[chunk + 2, 0])
            band_acc[first + chunk // 4, :, start : start + LANES] = flux

        if first_iteration:
            for save in saves:
                save.wait()

    def leave(chip):
        return pltpu.make_async_copy(mate_ref.at[chip], mate_out.at[chip], mate_sems.at[chip])

    for chip in range(CHIPS):
        mate_ref[chip] = band_acc[pl.ds(4 * chip + 2 - 2 * core, 2)].astype(bf16)
        leave(chip).start()
    for chip in range(CHIPS):
        own_out[chip] = band_acc[pl.ds(4 * chip + 2 * core, 2)]
    for chip in range(CHIPS):
        leave(chip).wait()


def into_rows(scal, near, far, win, mate_win, panel, table, indices, sources, saved):
    first_iteration = saved is None
    outs = [
        jax.ShapeDtypeStruct((CHIPS, 2, RHS, TILE), f32),
        pltpu.HBM((CHIPS, 2, RHS, TILE), bf16),
    ]
    out_specs = [VMEM, ANY]
    in_specs = [SMEM, VMEM, VMEM, VMEM, VMEM, ANY]
    args = [scal, near, far, win, mate_win, panel]
    state = (EXT + 2, LAYERS, RHS, LANES)
    coefs = (EXT, 48, LANES)
    if first_iteration:
        outs += [pltpu.HBM(state, f32), pltpu.HBM(coefs, f32)]
        out_specs += [ANY, ANY]
        in_specs += [SMEM, ANY, ANY]
        args += [table, in_hbm(indices), in_hbm(sources)]
    else:
        in_specs += [ANY, ANY]
        args += [in_hbm(x) for x in saved]
    cells = (LAYERS, MID * LANES)
    lines = [pltpu.VMEM(cells, jnp.int32), pltpu.VMEM(cells, f32)] if first_iteration else []
    return pl.pallas_call(
        functools.partial(rows_body, first_iteration),
        out_shape=outs,
        in_specs=in_specs,
        out_specs=out_specs,
        scratch_shapes=[
            pltpu.VMEM((BAND_TILES + 1, RHS, TILE), f32),
            pltpu.VMEM(state, f32),
            pltpu.VMEM(state, f32),
            pltpu.VMEM(coefs, f32),
            pltpu.VMEM((EXT + 2, 2, 8, LANES), f32),
            pltpu.VMEM((EXT, RHS, LANES), f32),
            pltpu.SemaphoreType.DMA((2,)),
            pltpu.VMEM((SLOTS, TILE, TILE), bf16),
            pltpu.SemaphoreType.DMA((SLOTS,)),
            pltpu.VMEM((WIN_TILES, RHS, TILE), bf16),
            pltpu.VMEM((CHIPS, 2, RHS, TILE), bf16),
            pltpu.SemaphoreType.DMA((CHIPS,)),
            *lines,
        ],
        compiler_params=pltpu.CompilerParams(vmem_limit_bytes=44 * MIB),
        cost_estimate=pl.CostEstimate(flops=7 * 10**8, transcendentals=0, bytes_accessed=30 * 10**6),
        name="into_rows_first" if first_iteration else "into_rows_next",
    )(*args)


def share_body(parts_ref, out_ref):
    share = parts_ref[0].astype(f32)
    for peer in range(1, N_ROW):
        share = share + parts_ref[peer].astype(f32)
    out_ref[...] = share


def window_share(parts):
    return pl.pallas_call(
        share_body,
        out_shape=jax.ShapeDtypeStruct(parts.shape[1:], f32),
        in_specs=[VMEM],
        out_specs=VMEM,
        compiler_params=pltpu.CompilerParams(vmem_limit_bytes=6 * MIB),
        name="window_share",
    )(parts)


def pair_body(scal_ref, own_ref, got_ref, share_ref, got_share_ref, out_ref):
    for chip in range(1, CHIPS):
        out_ref[chip] = (own_ref[chip] + got_ref[chip].astype(f32)).astype(bf16)
    total = own_ref[0] + got_ref[0].astype(f32)
    share = share_ref[...] + got_share_ref[...]
    out_ref[0] = (total + jnp.where(scal_ref[SLOTS + 6] == 0, share, 0.0)).astype(bf16)


def pair_sum(scal, own, got, share, got_share):
    return pl.pallas_call(
        pair_body,
        out_shape=jax.ShapeDtypeStruct(got.shape, bf16),
        in_specs=[SMEM, VMEM, VMEM, VMEM, VMEM],
        out_specs=VMEM,
        compiler_params=pltpu.CompilerParams(vmem_limit_bytes=6 * MIB),
        name="pair_sum",
    )(scal, own, got, share, got_share)


def update_body(last, parts_ref, trace_ref, load_ref, *outs):
    for half in range(2):
        lanes = slice(half * TILE, (half + 1) * TILE)
        total = parts_ref[0, half].astype(f32)
        for peer in range(1, CHIPS):
            total = total + parts_ref[peer, half].astype(f32)
        trace = trace_ref[:, lanes]
        trace = trace + COUPLING_STEP * (load_ref[:, lanes] - trace - total)
        outs[0][:, lanes] = trace
        if last:
            outs[1][:, lanes] = total
        else:
            rounded = trace.astype(bf16)
            for copy in range(CHIPS):
                outs[1][copy, half] = rounded


def update(parts, traces, load, last):
    whole = jax.ShapeDtypeStruct(traces.shape, f32)
    return pl.pallas_call(
        functools.partial(update_body, last),
        out_shape=[whole, whole if last else jax.ShapeDtypeStruct(parts.shape, bf16)],
        in_specs=[VMEM, VMEM, VMEM],
        out_specs=[VMEM, VMEM],
        compiler_params=pltpu.CompilerParams(vmem_limit_bytes=8 * MIB),
        name="update_last" if last else "update_next",
    )(parts, traces, load)


def volume_edges(coef_index, vol_source, volume_line):
    indices = lax.dynamic_index_in_dim(coef_index, volume_line, 0, keepdims=False)
    source = lax.dynamic_index_in_dim(vol_source, volume_line, 0, keepdims=False)

    def ends(x):
        return jnp.concatenate([x[:, :LANES], x[:, -LANES:]], 1)

    high = ends(source).astype(bf16)
    low = (ends(source) - high.astype(f32)).astype(bf16)
    edges = [jnp.pad(e, ((0, 4), (0, 0))) for e in (ends(indices).astype(bf16), high, low)]
    return jnp.pad(jnp.concatenate(edges, 0), ((0, 8), (0, 0)))


def local(
    trace_start, surface_load, panel_tiles, tile_list, surf_map, coef_index, coef_table, vol_source
):
    col_index = lax.axis_index("col")
    row_index = lax.axis_index("row")
    volume_line = jnp.maximum(col_index - DENSE_COLS, 0)
    is_volume = col_index >= DENSE_COLS
    volume_tile = volume_line * N_ROW + row_index
    tile_numbers = jnp.arange(surf_map.shape[0], dtype=jnp.int32)
    quarter = jnp.sum(jnp.where(surf_map == volume_tile, tile_numbers, 0)) % 4
    core = col_index % CORES
    own = [
        is_volume,
        jnp.where(is_volume, 4 * quarter, core),
        jnp.where(is_volume, 4 * quarter + 3, core),
        quarter,
        row_index,
        core,
        core,
        jnp.where(is_volume, 1 - core, core),
        volume_line,
    ]
    scal = jnp.concatenate([tile_list, jnp.stack([x.astype(jnp.int32) for x in own])])
    traces = trace_start
    spread = spread_start(traces)
    edges = volume_edges(coef_index, vol_source, volume_line)
    panel = in_hbm(panel_tiles)
    saved = None
    for iteration in range(ITERS):
        last = iteration == ITERS - 1
        near = between_chips(spread)
        far = from_mate(near)
        near, far = near.reshape(TILES, RHS, TILE), far.reshape(TILES, RHS, TILE)
        row_spread = spread_row(scal, near, far, edges if iteration == 0 else None)
        win = exchange(row_spread, "row")
        win_part = into_window(scal, near, far, panel)
        win, _ = lax.optimization_barrier((win, win_part))
        mate_win = from_mate(win)
        parts = exchange(win_part.reshape(N_ROW, 2, RHS, TILE), "row")
        own, mate, *saved = into_rows(
            scal, near, far, win, mate_win, panel, coef_table, coef_index, vol_source, saved
        )
        got = from_mate(mate)
        share = window_share(parts)
        summed = between_chips(pair_sum(scal, own, got, share, from_mate(share)))
        traces, spread = update(summed, traces, surface_load, last)
    return (traces, spread)


def solution(mesh):
    return jax.shard_map(
        local,
        mesh=mesh,
        in_specs=(
            P(None, ("col", "row")),
            P(None, ("col", "row")),
            P(("col", "row"), None, None),
            P(("col", "row")),
            P(),
            P(None, None, "row"),
            P(),
            P(None, None, "row"),
        ),
        out_specs=(P(None, ("col", "row")), P(None, ("col", "row"))),
        check_vma=False,
    )
```

```python
import functools

import jax
import jax.numpy as jnp
from jax import lax
from jax.experimental import pallas as pl
from jax.experimental.pallas import tpu as pltpu
from jax.sharding import PartitionSpec as P

ITERS = 2
SWEEPS = 4
COUPLING_STEP = 0.3
JACOBI_WEIGHT = 0.8
CELL_MASS = 0.05

RHS = 32
TILE = 512
LANES = 128
N_COL = 16
N_ROW = 8
CORES = 2
CHIPS = N_COL // CORES
TILES = 2 * CHIPS
DENSE_COLS = 12
LAYERS = 4
SLOTS = 43
WINDOW_GROUPS = (6, 6, 6, 6, 6, 5, 4, 2, 2)
ROW_GROUPS = (2, 3, 4, 6, 7, 7, 7, 7)
UNROLL = 17
COEFS = 16
BAND_TILES = 32
WIN_TILES = 16
MID = 32
EXT = MID + 2
MIB = 1 << 20

VMEM = pl.BlockSpec(memory_space=pltpu.VMEM)
SMEM = pl.BlockSpec(memory_space=pltpu.SMEM)
ANY = pl.BlockSpec(memory_space=pl.ANY)
f32 = jnp.float32
bf16 = jnp.bfloat16


def in_hbm(x):
    return pltpu.with_memory_space_constraint(x, pltpu.HBM)


def exchange(x, axis):
    return lax.all_to_all(x, axis, 0, 0, tiled=True)


def between_chips(x):
    groups = [list(range(core, N_COL, CORES)) for core in range(CORES)]
    return lax.all_to_all(x, "col", 0, 0, axis_index_groups=groups, tiled=True)


def from_mate(x):
    return lax.ppermute(x, "col", [(i, i ^ 1) for i in range(N_COL)])


def pick(near_ref, far_ref, is_far, index):
    return jnp.where(is_far == 0, near_ref[index], far_ref[index])


def send_copies(block_ref, out_ref, sems):
    copies = [
        pltpu.make_async_copy(block_ref, out_ref.at[peer], sems.at[peer])
        for peer in range(out_ref.shape[0])
    ]
    for copy in copies:
        copy.start()
    for copy in copies:
        copy.wait()


def start_body(trace_ref, out_ref, trace_vmem, block_ref, load_sem, sems):
    load = pltpu.make_async_copy(trace_ref, trace_vmem, load_sem)
    load.start()
    load.wait()
    for half in range(2):
        block_ref[half] = trace_vmem[:, half * TILE : (half + 1) * TILE].astype(bf16)
    send_copies(block_ref, out_ref, sems)


def spread_start(trace_start):
    return pl.pallas_call(
        start_body,
        out_shape=pltpu.HBM((CHIPS, 2, RHS, TILE), bf16),
        in_specs=[ANY],
        out_specs=ANY,
        scratch_shapes=[
            pltpu.VMEM(trace_start.shape, f32),
            pltpu.VMEM((2, RHS, TILE), bf16),
            pltpu.SemaphoreType.DMA(()),
            pltpu.SemaphoreType.DMA((CHIPS,)),
        ],
        compiler_params=pltpu.CompilerParams(vmem_limit_bytes=6 * MIB),
        name="spread_start",
    )(in_hbm(trace_start))


def row_body(first_iteration, scal_ref, near_ref, far_ref, *refs):
    out_ref, block_ref, sems = refs[-3:]
    mine = pick(near_ref, far_ref, scal_ref[SLOTS + 5], scal_ref[SLOTS + 1])
    tail = pick(near_ref, far_ref, scal_ref[SLOTS + 7], scal_ref[SLOTS + 2])
    block_ref[:, : 3 * LANES] = mine[:, : 3 * LANES]
    block_ref[:, 3 * LANES :] = tail[:, 3 * LANES :]
    if first_iteration:

        @pl.when(scal_ref[SLOTS] == 1)
        def _():
            block_ref[:, LANES : 3 * LANES] = refs[0][...]

    send_copies(block_ref, out_ref, sems)


def spread_row(scal, near, far, edges):
    first_iteration = edges is not None
    args = [scal, near, far] + ([edges] if first_iteration else [])
    return pl.pallas_call(
        functools.partial(row_body, first_iteration),
        out_shape=pltpu.HBM((N_ROW, RHS, TILE), bf16),
        in_specs=[SMEM] + [VMEM] * (len(args) - 1),
        out_specs=ANY,
        scratch_shapes=[pltpu.VMEM((RHS, TILE), bf16), pltpu.SemaphoreType.DMA((N_ROW,))],
        compiler_params=pltpu.CompilerParams(vmem_limit_bytes=6 * MIB),
        name="spread_row",
    )(*args)


def interleave(near_ref, far_ref, core, run, out_ref):
    for index in range(near_ref.shape[0]):
        block, part = index // run, index % run
        out_ref[(2 * block + core) * run + part] = near_ref[index]
        out_ref[(2 * block + 1 - core) * run + part] = far_ref[index]


def for_slots(groups, scal_ref, panel_ref, buffer_ref, sems, acc_ref, prepare, do_slot):
    def fetch(slot):
        return pltpu.make_async_copy(panel_ref.at[slot], buffer_ref.at[slot], sems.at[slot])

    def start(slot, carry):
        fetch(slot).start()
        return carry

    lax.fori_loop(0, SLOTS, start, 0)
    acc_ref[...] = jnp.zeros_like(acc_ref)
    prepare()

    def place(slot):
        ident = scal_ref[slot]
        named = ident >= 0
        safe = jnp.maximum(ident, 0)
        row_tile = lax.shift_right_logical(safe, 8)
        col_tile = jnp.bitwise_and(safe, 15)
        shard = lax.shift_right_logical(row_tile, 4)
        do_slot(slot, named, shard, jnp.bitwise_and(row_tile, 1), col_tile)

    begin = 0
    for size in groups:
        for slot in range(begin, begin + size):
            fetch(slot).wait()
        for slot in range(begin, begin + size):
            place(slot)
        begin += size


def window_body(scal_ref, near_ref, far_ref, panel_ref, win_out, win_acc, buffer_ref, sems, traces_ref):
    is_volume = scal_ref[SLOTS] == 1

    @pl.when(jnp.logical_not(is_volume))
    def _():
        core = scal_ref[SLOTS + 6]

        def one_slot(slot, named, shard, half, col_tile):
            win_acc[jnp.where(named, col_tile, WIN_TILES)] += jnp.dot(
                traces_ref[2 * shard + half], buffer_ref[slot], preferred_element_type=f32
            )

        prepare = functools.partial(interleave, near_ref, far_ref, core, 2, traces_ref)
        for_slots(WINDOW_GROUPS, scal_ref, panel_ref, buffer_ref, sems, win_acc, prepare, one_slot)

        win_out[...] = win_acc[:WIN_TILES].astype(bf16)

    @pl.when(is_volume)
    def _():
        win_out[...] = jnp.zeros_like(win_out)


def into_window(scal, near, far, panel):
    return pl.pallas_call(
        window_body,
        out_shape=jax.ShapeDtypeStruct((WIN_TILES, RHS, TILE), bf16),
        in_specs=[SMEM, VMEM, VMEM, ANY],
        out_specs=VMEM,
        scratch_shapes=[
            pltpu.VMEM((WIN_TILES + 1, RHS, TILE), f32),
            pltpu.VMEM((SLOTS, TILE, TILE), bf16),
            pltpu.SemaphoreType.DMA((SLOTS,)),
            pltpu.VMEM((BAND_TILES, RHS, TILE), bf16),
        ],
        compiler_params=pltpu.CompilerParams(vmem_limit_bytes=44 * MIB),
        cost_estimate=pl.CostEstimate(flops=7 * 10**8, transcendentals=0, bytes_accessed=25 * 10**6),
        name="into_window",
    )(scal, near, far, panel)


def weigh(scal_ref, table_ref, index_ref, source_ref, win_ref, cell_ref, coef_ref):
    row = scal_ref[SLOTS + 4]
    before = jnp.maximum(row - 1, 0)
    after = jnp.minimum(row + 1, N_ROW - 1)
    layer = lax.broadcasted_iota(jnp.int32, (8, LANES), 0)
    lane = lax.broadcasted_iota(jnp.int32, (8, LANES), 1)
    nothing = jnp.zeros((8, LANES), f32)
    cell_ref[...] = jnp.zeros_like(cell_ref)
    for chunk, source, start, here in (
        (0, before, 2 * LANES, row > 0),
        (EXT - 1, after, LANES, row < N_ROW - 1),
    ):
        sent = win_ref[source, :, start : start + LANES].astype(f32)
        k = nothing
        for level in range(COEFS):
            k = jnp.where(sent[0:8] == float(level), table_ref[level], k)
        cell_ref[chunk + 1, 0] = jnp.where((layer < LAYERS) & here, k, 0.0)
        cell_ref[chunk + 1, 1] = jnp.where(here, sent[8:16] + sent[16:24], 0.0)

    for chunk in range(MID):
        lanes = slice(chunk * LANES, (chunk + 1) * LANES)
        indices = index_ref[:, lanes]
        k = jnp.zeros((LAYERS, LANES), f32)
        for level in range(COEFS):
            k = jnp.where(indices == level, table_ref[level], k)
        cell_ref[chunk + 2, 0, :LAYERS] = k
        cell_ref[chunk + 2, 1, :LAYERS] = source_ref[:, lanes]

    def one_chunk(chunk, carry):
        k = cell_ref[chunk + 1, 0]
        left = pltpu.roll(jnp.where(lane == LANES - 1, cell_ref[chunk, 0], k), 1, 1)
        right = pltpu.roll(jnp.where(lane == 0, cell_ref[chunk + 2, 0], k), LANES - 1, 1)
        left = 0.5 * (k + left)
        right = 0.5 * (k + right)
        lower = jnp.where(layer < LAYERS - 1, 0.5 * (k + pltpu.roll(k, 7, 0)), 0.0)
        upper = jnp.where(layer == 0, k, pltpu.roll(lower, 1, 0))
        inside = ((chunk > 0) | (row > 0)) & ((chunk < EXT - 1) | (row < N_ROW - 1))
        scale = jnp.where(inside, JACOBI_WEIGHT / (left + right + upper + lower + CELL_MASS), 0.0)
        coef_ref[chunk, 0:8] = left * scale
        coef_ref[chunk, 8:16] = right * scale
        coef_ref[chunk, 16:24] = upper * scale
        coef_ref[chunk, 24:32] = lower * scale
        coef_ref[chunk, 32:40] = cell_ref[chunk + 1, 1] * scale
        coef_ref[chunk, 40:48] = k
        return carry

    lax.fori_loop(0, EXT, one_chunk, 0, unroll=2)


def relax(scal_ref, near_ref, far_ref, win_ref, coef_ref, states, top_ref):
    quarter = scal_ref[SLOTS + 3]
    row = scal_ref[SLOTS + 4]
    core = scal_ref[SLOTS + 6]
    before = jnp.maximum(row - 1, 0)
    after = jnp.minimum(row + 1, N_ROW - 1)
    top_ref[0] = win_ref[before, :, TILE - LANES :].astype(f32)
    top_ref[EXT - 1] = win_ref[after, :, :LANES].astype(f32)
    for tile in range(8):
        is_far = jnp.bitwise_xor(tile // 2 % 2, core)
        tops = pick(near_ref, far_ref, is_far, 4 * quarter + tile // 4 * 2 + tile % 2)
        for part in range(4):
            top_ref[4 * tile + part + 1] = tops[:, part * LANES : (part + 1) * LANES].astype(f32)
    lane = lax.broadcasted_iota(jnp.int32, (RHS, LANES), 1)
    is_first = lane == 0
    is_last = lane == LANES - 1

    def sweep(source_ref, target_ref):
        def one_chunk(chunk, carry):
            upper = top_ref[chunk]
            centre = source_ref[chunk + 1, 0]
            for l in range(LAYERS):
                left = pltpu.roll(jnp.where(is_last, source_ref[chunk, l], centre), 1, 1)
                right = pltpu.roll(jnp.where(is_first, source_ref[chunk + 2, l], centre), LANES - 1, 1)
                value = (
                    (1.0 - JACOBI_WEIGHT) * centre
                    + coef_ref[chunk, l : 1 + l, :] * left
                    + coef_ref[chunk, 8 + l : 9 + l, :] * right
                    + coef_ref[chunk, 16 + l : 17 + l, :] * upper
                    + coef_ref[chunk, 32 + l : 33 + l, :]
                )
                if l + 1 < LAYERS:
                    below = source_ref[chunk + 1, l + 1]
                    value = value + coef_ref[chunk, 24 + l : 25 + l, :] * below
                    upper, centre = centre, below
                target_ref[chunk + 1, l] = value
            return carry

        lax.fori_loop(0, EXT, one_chunk, 0, unroll=UNROLL)

    for step in range(SWEEPS):
        sweep(states[step % 2], states[1 - step % 2])


def rows_body(first_iteration, scal_ref, near_ref, far_ref, win_ref, mate_win_ref, panel_ref, *refs):
    if first_iteration:
        table_ref, all_index_ref, all_source_ref, own_out, mate_out, state_out, coef_out = refs[:7]
        refs = refs[7:]
    else:
        state_in, coef_in, own_out, mate_out = refs[:4]
        refs = refs[4:]
    band_acc, state_a, state_b, coef_ref, cell_ref, top_ref, sems, buffer_ref, panel_sems = refs[:9]
    traces_ref, mate_ref, mate_sems = refs[9:12]
    if first_iteration:
        index_ref, source_ref = refs[12:]
    is_volume = scal_ref[SLOTS] == 1
    core = scal_ref[SLOTS + 6]

    @pl.when(jnp.logical_not(is_volume))
    def _():
        def one_slot(slot, named, shard, half, col_tile):
            band_acc[jnp.where(named, 2 * shard + half, BAND_TILES)] += lax.dot_general(
                traces_ref[col_tile],
                buffer_ref[slot],
                (((1,), (1,)), ((), ())),
                preferred_element_type=f32,
            )

        prepare = functools.partial(interleave, win_ref, mate_win_ref, core, 1, traces_ref)
        for_slots(ROW_GROUPS, scal_ref, panel_ref, buffer_ref, panel_sems, band_acc, prepare, one_slot)

    @pl.when(is_volume)
    def _():
        guard = jnp.zeros((LAYERS, RHS, LANES), f32)
        state_b[0] = guard
        state_b[EXT + 1] = guard
        if first_iteration:
            line = scal_ref[SLOTS + 8]
            loads = [
                pltpu.make_async_copy(all_index_ref.at[line], index_ref, sems.at[0]),
                pltpu.make_async_copy(all_source_ref.at[line], source_ref, sems.at[1]),
            ]
            for load in loads:
                load.start()
            state_a[...] = jnp.zeros_like(state_a)
            for load in loads:
                load.wait()
            weigh(scal_ref, table_ref, index_ref, source_ref, win_ref, cell_ref, coef_ref)
        else:
            loads = [
                pltpu.make_async_copy(state_in, state_a, sems.at[0]),
                pltpu.make_async_copy(coef_in, coef_ref, sems.at[1]),
            ]
            for load in loads:
                load.start()
            for load in loads:
                load.wait()
        relax(scal_ref, near_ref, far_ref, win_ref, coef_ref, (state_a, state_b), top_ref)
        if first_iteration:
            saves = [
                pltpu.make_async_copy(state_a, state_out, sems.at[0]),
                pltpu.make_async_copy(coef_ref, coef_out, sems.at[1]),
            ]
            for save in saves:
                save.start()
        band_acc[...] = jnp.zeros_like(band_acc)
        first = 8 * scal_ref[SLOTS + 3]
        for chunk in range(MID):
            start = chunk % 4 * LANES
            flux = coef_ref[chunk + 1, 40:41, :] * (top_ref[chunk + 1] - state_a[chunk + 2, 0])
            band_acc[first + chunk // 4, :, start : start + LANES] = flux

        if first_iteration:
            for save in saves:
                save.wait()

    def leave(chip):
        return pltpu.make_async_copy(mate_ref.at[chip], mate_out.at[chip], mate_sems.at[chip])

    for chip in range(CHIPS):
        mate_ref[chip] = band_acc[pl.ds(4 * chip + 2 - 2 * core, 2)].astype(bf16)
        leave(chip).start()
    for chip in range(CHIPS):
        own_out[chip] = band_acc[pl.ds(4 * chip + 2 * core, 2)]
    for chip in range(CHIPS):
        leave(chip).wait()


def into_rows(scal, near, far, win, mate_win, panel, table, indices, sources, saved):
    first_iteration = saved is None
    outs = [
        jax.ShapeDtypeStruct((CHIPS, 2, RHS, TILE), f32),
        pltpu.HBM((CHIPS, 2, RHS, TILE), bf16),
    ]
    out_specs = [VMEM, ANY]
    in_specs = [SMEM, VMEM, VMEM, VMEM, VMEM, ANY]
    args = [scal, near, far, win, mate_win, panel]
    state = (EXT + 2, LAYERS, RHS, LANES)
    coefs = (EXT, 48, LANES)
    if first_iteration:
        outs += [pltpu.HBM(state, f32), pltpu.HBM(coefs, f32)]
        out_specs += [ANY, ANY]
        in_specs += [SMEM, ANY, ANY]
        args += [table, in_hbm(indices), in_hbm(sources)]
    else:
        in_specs += [ANY, ANY]
        args += [in_hbm(x) for x in saved]
    cells = (LAYERS, MID * LANES)
    lines = [pltpu.VMEM(cells, jnp.int32), pltpu.VMEM(cells, f32)] if first_iteration else []
    return pl.pallas_call(
        functools.partial(rows_body, first_iteration),
        out_shape=outs,
        in_specs=in_specs,
        out_specs=out_specs,
        scratch_shapes=[
            pltpu.VMEM((BAND_TILES + 1, RHS, TILE), f32),
            pltpu.VMEM(state, f32),
            pltpu.VMEM(state, f32),
            pltpu.VMEM(coefs, f32),
            pltpu.VMEM((EXT + 2, 2, 8, LANES), f32),
            pltpu.VMEM((EXT, RHS, LANES), f32),
            pltpu.SemaphoreType.DMA((2,)),
            pltpu.VMEM((SLOTS, TILE, TILE), bf16),
            pltpu.SemaphoreType.DMA((SLOTS,)),
            pltpu.VMEM((WIN_TILES, RHS, TILE), bf16),
            pltpu.VMEM((CHIPS, 2, RHS, TILE), bf16),
            pltpu.SemaphoreType.DMA((CHIPS,)),
            *lines,
        ],
        compiler_params=pltpu.CompilerParams(vmem_limit_bytes=44 * MIB),
        cost_estimate=pl.CostEstimate(flops=7 * 10**8, transcendentals=0, bytes_accessed=30 * 10**6),
        name="into_rows_first" if first_iteration else "into_rows_next",
    )(*args)


def share_body(parts_ref, out_ref):
    share = parts_ref[0].astype(f32)
    for peer in range(1, N_ROW):
        share = share + parts_ref[peer].astype(f32)
    out_ref[...] = share


def window_share(parts):
    return pl.pallas_call(
        share_body,
        out_shape=jax.ShapeDtypeStruct(parts.shape[1:], f32),
        in_specs=[VMEM],
        out_specs=VMEM,
        compiler_params=pltpu.CompilerParams(vmem_limit_bytes=6 * MIB),
        name="window_share",
    )(parts)


def pair_body(scal_ref, own_ref, got_ref, share_ref, got_share_ref, out_ref):
    for chip in range(1, CHIPS):
        out_ref[chip] = (own_ref[chip] + got_ref[chip].astype(f32)).astype(bf16)
    total = own_ref[0] + got_ref[0].astype(f32)
    share = share_ref[...] + got_share_ref[...]
    out_ref[0] = (total + jnp.where(scal_ref[SLOTS + 6] == 0, share, 0.0)).astype(bf16)


def pair_sum(scal, own, got, share, got_share):
    return pl.pallas_call(
        pair_body,
        out_shape=jax.ShapeDtypeStruct(got.shape, bf16),
        in_specs=[SMEM, VMEM, VMEM, VMEM, VMEM],
        out_specs=VMEM,
        compiler_params=pltpu.CompilerParams(vmem_limit_bytes=6 * MIB),
        name="pair_sum",
    )(scal, own, got, share, got_share)


def update_body(last, parts_ref, trace_ref, load_ref, *outs):
    for half in range(2):
        lanes = slice(half * TILE, (half + 1) * TILE)
        total = parts_ref[0, half].astype(f32)
        for peer in range(1, CHIPS):
            total = total + parts_ref[peer, half].astype(f32)
        trace = trace_ref[:, lanes]
        trace = trace + COUPLING_STEP * (load_ref[:, lanes] - trace - total)
        outs[0][:, lanes] = trace
        if last:
            outs[1][:, lanes] = total
        else:
            rounded = trace.astype(bf16)
            for copy in range(CHIPS):
                outs[1][copy, half] = rounded


def update(parts, traces, load, last):
    whole = jax.ShapeDtypeStruct(traces.shape, f32)
    return pl.pallas_call(
        functools.partial(update_body, last),
        out_shape=[whole, whole if last else jax.ShapeDtypeStruct(parts.shape, bf16)],
        in_specs=[VMEM, VMEM, VMEM],
        out_specs=[VMEM, VMEM],
        compiler_params=pltpu.CompilerParams(vmem_limit_bytes=8 * MIB),
        name="update_last" if last else "update_next",
    )(parts, traces, load)


def volume_edges(coef_index, vol_source, volume_line):
    indices = lax.dynamic_index_in_dim(coef_index, volume_line, 0, keepdims=False)
    source = lax.dynamic_index_in_dim(vol_source, volume_line, 0, keepdims=False)

    def ends(x):
        return jnp.concatenate([x[:, :LANES], x[:, -LANES:]], 1)

    high = ends(source).astype(bf16)
    low = (ends(source) - high.astype(f32)).astype(bf16)
    edges = [jnp.pad(e, ((0, 4), (0, 0))) for e in (ends(indices).astype(bf16), high, low)]
    return jnp.pad(jnp.concatenate(edges, 0), ((0, 8), (0, 0)))


def local(
    trace_start, surface_load, panel_tiles, tile_list, surf_map, coef_index, coef_table, vol_source
):
    col_index = lax.axis_index("col")
    row_index = lax.axis_index("row")
    volume_line = jnp.maximum(col_index - DENSE_COLS, 0)
    is_volume = col_index >= DENSE_COLS
    volume_tile = volume_line * N_ROW + row_index
    tile_numbers = jnp.arange(surf_map.shape[0], dtype=jnp.int32)
    quarter = jnp.sum(jnp.where(surf_map == volume_tile, tile_numbers, 0)) % 4
    core = col_index % CORES
    own = [
        is_volume,
        jnp.where(is_volume, 4 * quarter, core),
        jnp.where(is_volume, 4 * quarter + 3, core),
        quarter,
        row_index,
        core,
        core,
        jnp.where(is_volume, 1 - core, core),
        volume_line,
    ]
    scal = jnp.concatenate([tile_list, jnp.stack([x.astype(jnp.int32) for x in own])])
    traces = trace_start
    spread = spread_start(traces)
    edges = volume_edges(coef_index, vol_source, volume_line)
    panel = in_hbm(panel_tiles)
    saved = None
    for iteration in range(ITERS):
        last = iteration == ITERS - 1
        near = between_chips(spread)
        far = from_mate(near)
        near, far = near.reshape(TILES, RHS, TILE), far.reshape(TILES, RHS, TILE)
        row_spread = spread_row(scal, near, far, edges if iteration == 0 else None)
        win = exchange(row_spread, "row")
        win_part = into_window(scal, near, far, panel)
        win, _ = lax.optimization_barrier((win, win_part))
        mate_win = from_mate(win)
        parts = exchange(win_part.reshape(N_ROW, 2, RHS, TILE), "row")
        own, mate, *saved = into_rows(
            scal, near, far, win, mate_win, panel, coef_table, coef_index, vol_source, saved
        )
        got = from_mate(mate)
        share = window_share(parts)
        summed = between_chips(pair_sum(scal, own, got, share, from_mate(share)))
        traces, spread = update(summed, traces, surface_load, last)
    return (traces, spread)


def solution(mesh):
    return jax.shard_map(
        local,
        mesh=mesh,
        in_specs=(
            P(None, ("col", "row")),
            P(None, ("col", "row")),
            P(("col", "row"), None, None),
            P(("col", "row")),
            P(),
            P(None, None, "row"),
            P(),
            P(None, None, "row"),
        ),
        out_specs=(P(None, ("col", "row")), P(None, ("col", "row"))),
        check_vma=False,
    )
```

```python
import functools

import jax
import jax.numpy as jnp
from jax import lax
from jax.experimental import pallas as pl
from jax.experimental.pallas import tpu as pltpu
from jax.sharding import PartitionSpec as P

ITERS = 2
SWEEPS = 4
COUPLING_STEP = 0.3
JACOBI_WEIGHT = 0.8
CELL_MASS = 0.05

RHS = 32
TILE = 512
LANES = 128
N_COL = 16
N_ROW = 8
CORES = 2
CHIPS = N_COL // CORES
TILES = 2 * CHIPS
DENSE_COLS = 12
LAYERS = 4
SLOTS = 43
WINDOW_GROUPS = (6, 6, 6, 6, 6, 5, 4, 2, 2)
ROW_GROUPS = (2, 3, 4, 6, 7, 7, 7, 7)
UNROLL = 17
COEFS = 16
BAND_TILES = 32
WIN_TILES = 16
MID = 32
EXT = MID + 2
MIB = 1 << 20

VMEM = pl.BlockSpec(memory_space=pltpu.VMEM)
SMEM = pl.BlockSpec(memory_space=pltpu.SMEM)
ANY = pl.BlockSpec(memory_space=pl.ANY)
f32 = jnp.float32
bf16 = jnp.bfloat16


def in_hbm(x):
    return pltpu.with_memory_space_constraint(x, pltpu.HBM)


def exchange(x, axis):
    return lax.all_to_all(x, axis, 0, 0, tiled=True)


def between_chips(x):
    groups = [list(range(core, N_COL, CORES)) for core in range(CORES)]
    return lax.all_to_all(x, "col", 0, 0, axis_index_groups=groups, tiled=True)


def from_mate(x):
    return lax.ppermute(x, "col", [(i, i ^ 1) for i in range(N_COL)])


def pick(near_ref, far_ref, is_far, index):
    return jnp.where(is_far == 0, near_ref[index], far_ref[index])


def send_copies(block_ref, out_ref, sems):
    copies = [
        pltpu.make_async_copy(block_ref, out_ref.at[peer], sems.at[peer])
        for peer in range(out_ref.shape[0])
    ]
    for copy in copies:
        copy.start()
    for copy in copies:
        copy.wait()


def start_body(trace_ref, out_ref, trace_vmem, block_ref, load_sem, sems):
    load = pltpu.make_async_copy(trace_ref, trace_vmem, load_sem)
    load.start()
    load.wait()
    for half in range(2):
        block_ref[half] = trace_vmem[:, half * TILE : (half + 1) * TILE].astype(bf16)
    send_copies(block_ref, out_ref, sems)


def spread_start(trace_start):
    return pl.pallas_call(
        start_body,
        out_shape=pltpu.HBM((CHIPS, 2, RHS, TILE), bf16),
        in_specs=[ANY],
        out_specs=ANY,
        scratch_shapes=[
            pltpu.VMEM(trace_start.shape, f32),
            pltpu.VMEM((2, RHS, TILE), bf16),
            pltpu.SemaphoreType.DMA(()),
            pltpu.SemaphoreType.DMA((CHIPS,)),
        ],
        compiler_params=pltpu.CompilerParams(vmem_limit_bytes=6 * MIB),
        name="spread_start",
    )(in_hbm(trace_start))


def row_body(first_iteration, scal_ref, near_ref, far_ref, *refs):
    out_ref, block_ref, sems = refs[-3:]
    mine = pick(near_ref, far_ref, scal_ref[SLOTS + 5], scal_ref[SLOTS + 1])
    tail = pick(near_ref, far_ref, scal_ref[SLOTS + 7], scal_ref[SLOTS + 2])
    block_ref[:, : 3 * LANES] = mine[:, : 3 * LANES]
    block_ref[:, 3 * LANES :] = tail[:, 3 * LANES :]
    if first_iteration:

        @pl.when(scal_ref[SLOTS] == 1)
        def _():
            block_ref[:, LANES : 3 * LANES] = refs[0][...]

    send_copies(block_ref, out_ref, sems)


def spread_row(scal, near, far, edges):
    first_iteration = edges is not None
    args = [scal, near, far] + ([edges] if first_iteration else [])
    return pl.pallas_call(
        functools.partial(row_body, first_iteration),
        out_shape=pltpu.HBM((N_ROW, RHS, TILE), bf16),
        in_specs=[SMEM] + [VMEM] * (len(args) - 1),
        out_specs=ANY,
        scratch_shapes=[pltpu.VMEM((RHS, TILE), bf16), pltpu.SemaphoreType.DMA((N_ROW,))],
        compiler_params=pltpu.CompilerParams(vmem_limit_bytes=6 * MIB),
        name="spread_row",
    )(*args)


def interleave(near_ref, far_ref, core, run, out_ref):
    for index in range(near_ref.shape[0]):
        block, part = index // run, index % run
        out_ref[(2 * block + core) * run + part] = near_ref[index]
        out_ref[(2 * block + 1 - core) * run + part] = far_ref[index]


def for_slots(groups, scal_ref, panel_ref, buffer_ref, sems, acc_ref, prepare, do_slot):
    def fetch(slot):
        return pltpu.make_async_copy(panel_ref.at[slot], buffer_ref.at[slot], sems.at[slot])

    def start(slot, carry):
        fetch(slot).start()
        return carry

    lax.fori_loop(0, SLOTS, start, 0)
    acc_ref[...] = jnp.zeros_like(acc_ref)
    prepare()

    def place(slot):
        ident = scal_ref[slot]
        named = ident >= 0
        safe = jnp.maximum(ident, 0)
        row_tile = lax.shift_right_logical(safe, 8)
        col_tile = jnp.bitwise_and(safe, 15)
        shard = lax.shift_right_logical(row_tile, 4)
        do_slot(slot, named, shard, jnp.bitwise_and(row_tile, 1), col_tile)

    begin = 0
    for size in groups:
        for slot in range(begin, begin + size):
            fetch(slot).wait()
        for slot in range(begin, begin + size):
            place(slot)
        begin += size


def window_body(scal_ref, near_ref, far_ref, panel_ref, win_out, win_acc, buffer_ref, sems, traces_ref, sum_ref, out_sems):
    is_volume = scal_ref[SLOTS] == 1

    @pl.when(jnp.logical_not(is_volume))
    def _():
        core = scal_ref[SLOTS + 6]

        def one_slot(slot, named, shard, half, col_tile):
            win_acc[jnp.where(named, col_tile, WIN_TILES)] += jnp.dot(
                traces_ref[2 * shard + half], buffer_ref[slot], preferred_element_type=f32
            )

        prepare = functools.partial(interleave, near_ref, far_ref, core, 2, traces_ref)
        for_slots(WINDOW_GROUPS, scal_ref, panel_ref, buffer_ref, sems, win_acc, prepare, one_slot)


    @pl.when(is_volume)
    def _():
        win_acc[...] = jnp.zeros_like(win_acc)

    def leave(peer):
        return pltpu.make_async_copy(sum_ref.at[peer], win_out.at[peer], out_sems.at[peer])

    for peer in range(N_ROW):
        sum_ref[peer] = win_acc[2 * peer : 2 * peer + 2].astype(bf16)
        leave(peer).start()
    for peer in range(N_ROW):
        leave(peer).wait()


def into_window(scal, near, far, panel):
    return pl.pallas_call(
        window_body,
        out_shape=pltpu.HBM((N_ROW, 2, RHS, TILE), bf16),
        in_specs=[SMEM, VMEM, VMEM, ANY],
        out_specs=ANY,
        scratch_shapes=[
            pltpu.VMEM((WIN_TILES + 1, RHS, TILE), f32),
            pltpu.VMEM((SLOTS, TILE, TILE), bf16),
            pltpu.SemaphoreType.DMA((SLOTS,)),
            pltpu.VMEM((BAND_TILES, RHS, TILE), bf16),
            pltpu.VMEM((N_ROW, 2, RHS, TILE), bf16),
            pltpu.SemaphoreType.DMA((N_ROW,)),
        ],
        compiler_params=pltpu.CompilerParams(vmem_limit_bytes=44 * MIB),
        cost_estimate=pl.CostEstimate(flops=7 * 10**8, transcendentals=0, bytes_accessed=25 * 10**6),
        name="into_window",
    )(scal, near, far, panel)


def weigh(scal_ref, table_ref, index_ref, source_ref, win_ref, cell_ref, coef_ref):
    row = scal_ref[SLOTS + 4]
    before = jnp.maximum(row - 1, 0)
    after = jnp.minimum(row + 1, N_ROW - 1)
    layer = lax.broadcasted_iota(jnp.int32, (8, LANES), 0)
    lane = lax.broadcasted_iota(jnp.int32, (8, LANES), 1)
    nothing = jnp.zeros((8, LANES), f32)
    cell_ref[...] = jnp.zeros_like(cell_ref)
    for chunk, source, start, here in (
        (0, before, 2 * LANES, row > 0),
        (EXT - 1, after, LANES, row < N_ROW - 1),
    ):
        sent = win_ref[source, :, start : start + LANES].astype(f32)
        k = nothing
        for level in range(COEFS):
            k = jnp.where(sent[0:8] == float(level), table_ref[level], k)
        cell_ref[chunk + 1, 0] = jnp.where((layer < LAYERS) & here, k, 0.0)
        cell_ref[chunk + 1, 1] = jnp.where(here, sent[8:16] + sent[16:24], 0.0)

    for chunk in range(MID):
        lanes = slice(chunk * LANES, (chunk + 1) * LANES)
        indices = index_ref[:, lanes]
        k = jnp.zeros((LAYERS, LANES), f32)
        for level in range(COEFS):
            k = jnp.where(indices == level, table_ref[level], k)
        cell_ref[chunk + 2, 0, :LAYERS] = k
        cell_ref[chunk + 2, 1, :LAYERS] = source_ref[:, lanes]

    def one_chunk(chunk, carry):
        k = cell_ref[chunk + 1, 0]
        left = pltpu.roll(jnp.where(lane == LANES - 1, cell_ref[chunk, 0], k), 1, 1)
        right = pltpu.roll(jnp.where(lane == 0, cell_ref[chunk + 2, 0], k), LANES - 1, 1)
        left = 0.5 * (k + left)
        right = 0.5 * (k + right)
        lower = jnp.where(layer < LAYERS - 1, 0.5 * (k + pltpu.roll(k, 7, 0)), 0.0)
        upper = jnp.where(layer == 0, k, pltpu.roll(lower, 1, 0))
        inside = ((chunk > 0) | (row > 0)) & ((chunk < EXT - 1) | (row < N_ROW - 1))
        scale = jnp.where(inside, JACOBI_WEIGHT / (left + right + upper + lower + CELL_MASS), 0.0)
        coef_ref[chunk, 0:8] = left * scale
        coef_ref[chunk, 8:16] = right * scale
        coef_ref[chunk, 16:24] = upper * scale
        coef_ref[chunk, 24:32] = lower * scale
        coef_ref[chunk, 32:40] = cell_ref[chunk + 1, 1] * scale
        coef_ref[chunk, 40:48] = k
        return carry

    lax.fori_loop(0, EXT, one_chunk, 0, unroll=2)


def relax(scal_ref, near_ref, far_ref, win_ref, coef_ref, states, top_ref):
    quarter = scal_ref[SLOTS + 3]
    row = scal_ref[SLOTS + 4]
    core = scal_ref[SLOTS + 6]
    before = jnp.maximum(row - 1, 0)
    after = jnp.minimum(row + 1, N_ROW - 1)
    top_ref[0] = win_ref[before, :, TILE - LANES :].astype(f32)
    top_ref[EXT - 1] = win_ref[after, :, :LANES].astype(f32)
    for tile in range(8):
        is_far = jnp.bitwise_xor(tile // 2 % 2, core)
        tops = pick(near_ref, far_ref, is_far, 4 * quarter + tile // 4 * 2 + tile % 2)
        for part in range(4):
            top_ref[4 * tile + part + 1] = tops[:, part * LANES : (part + 1) * LANES].astype(f32)
    lane = lax.broadcasted_iota(jnp.int32, (RHS, LANES), 1)
    is_first = lane == 0
    is_last = lane == LANES - 1

    def sweep(source_ref, target_ref):
        def one_chunk(chunk, carry):
            upper = top_ref[chunk]
            centre = source_ref[chunk + 1, 0]
            for l in range(LAYERS):
                left = pltpu.roll(jnp.where(is_last, source_ref[chunk, l], centre), 1, 1)
                right = pltpu.roll(jnp.where(is_first, source_ref[chunk + 2, l], centre), LANES - 1, 1)
                value = (
                    (1.0 - JACOBI_WEIGHT) * centre
                    + coef_ref[chunk, l : 1 + l, :] * left
                    + coef_ref[chunk, 8 + l : 9 + l, :] * right
                    + coef_ref[chunk, 16 + l : 17 + l, :] * upper
                    + coef_ref[chunk, 32 + l : 33 + l, :]
                )
                if l + 1 < LAYERS:
                    below = source_ref[chunk + 1, l + 1]
                    value = value + coef_ref[chunk, 24 + l : 25 + l, :] * below
                    upper, centre = centre, below
                target_ref[chunk + 1, l] = value
            return carry

        lax.fori_loop(0, EXT, one_chunk, 0, unroll=UNROLL)

    for step in range(SWEEPS):
        sweep(states[step % 2], states[1 - step % 2])


def rows_body(first_iteration, scal_ref, near_ref, far_ref, win_ref, mate_win_ref, panel_ref, *refs):
    if first_iteration:
        table_ref, all_index_ref, all_source_ref, own_out, mate_out, state_out, coef_out = refs[:7]
        refs = refs[7:]
    else:
        state_in, coef_in, own_out, mate_out = refs[:4]
        refs = refs[4:]
    band_acc, state_a, state_b, coef_ref, cell_ref, top_ref, sems, buffer_ref, panel_sems = refs[:9]
    traces_ref, mate_ref, mate_sems = refs[9:12]
    if first_iteration:
        index_ref, source_ref = refs[12:]
    is_volume = scal_ref[SLOTS] == 1
    core = scal_ref[SLOTS + 6]

    @pl.when(jnp.logical_not(is_volume))
    def _():
        def one_slot(slot, named, shard, half, col_tile):
            band_acc[jnp.where(named, 2 * shard + half, BAND_TILES)] += lax.dot_general(
                traces_ref[col_tile],
                buffer_ref[slot],
                (((1,), (1,)), ((), ())),
                preferred_element_type=f32,
            )

        prepare = functools.partial(interleave, win_ref, mate_win_ref, core, 1, traces_ref)
        for_slots(ROW_GROUPS, scal_ref, panel_ref, buffer_ref, panel_sems, band_acc, prepare, one_slot)

    @pl.when(is_volume)
    def _():
        guard = jnp.zeros((LAYERS, RHS, LANES), f32)
        state_b[0] = guard
        state_b[EXT + 1] = guard
        if first_iteration:
            line = scal_ref[SLOTS + 8]
            loads = [
                pltpu.make_async_copy(all_index_ref.at[line], index_ref, sems.at[0]),
                pltpu.make_async_copy(all_source_ref.at[line], source_ref, sems.at[1]),
            ]
            for load in loads:
                load.start()
            state_a[...] = jnp.zeros_like(state_a)
            for load in loads:
                load.wait()
            weigh(scal_ref, table_ref, index_ref, source_ref, win_ref, cell_ref, coef_ref)
        else:
            loads = [
                pltpu.make_async_copy(state_in, state_a, sems.at[0]),
                pltpu.make_async_copy(coef_in, coef_ref, sems.at[1]),
            ]
            for load in loads:
                load.start()
            for load in loads:
                load.wait()
        relax(scal_ref, near_ref, far_ref, win_ref, coef_ref, (state_a, state_b), top_ref)
        if first_iteration:
            saves = [
                pltpu.make_async_copy(state_a, state_out, sems.at[0]),
                pltpu.make_async_copy(coef_ref, coef_out, sems.at[1]),
            ]
            for save in saves:
                save.start()
        band_acc[...] = jnp.zeros_like(band_acc)
        first = 8 * scal_ref[SLOTS + 3]
        for chunk in range(MID):
            start = chunk % 4 * LANES
            flux = coef_ref[chunk + 1, 40:41, :] * (top_ref[chunk + 1] - state_a[chunk + 2, 0])
            band_acc[first + chunk // 4, :, start : start + LANES] = flux

        if first_iteration:
            for save in saves:
                save.wait()

    def leave(chip):
        return pltpu.make_async_copy(mate_ref.at[chip], mate_out.at[chip], mate_sems.at[chip])

    for chip in range(CHIPS):
        mate_ref[chip] = band_acc[pl.ds(4 * chip + 2 - 2 * core, 2)].astype(bf16)
        leave(chip).start()
    for chip in range(CHIPS):
        own_out[chip] = band_acc[pl.ds(4 * chip + 2 * core, 2)]
    for chip in range(CHIPS):
        leave(chip).wait()


def into_rows(scal, near, far, win, mate_win, panel, table, indices, sources, saved):
    first_iteration = saved is None
    outs = [
        jax.ShapeDtypeStruct((CHIPS, 2, RHS, TILE), f32),
        pltpu.HBM((CHIPS, 2, RHS, TILE), bf16),
    ]
    out_specs = [VMEM, ANY]
    in_specs = [SMEM, VMEM, VMEM, VMEM, VMEM, ANY]
    args = [scal, near, far, win, mate_win, panel]
    state = (EXT + 2, LAYERS, RHS, LANES)
    coefs = (EXT, 48, LANES)
    if first_iteration:
        outs += [pltpu.HBM(state, f32), pltpu.HBM(coefs, f32)]
        out_specs += [ANY, ANY]
        in_specs += [SMEM, ANY, ANY]
        args += [table, in_hbm(indices), in_hbm(sources)]
    else:
        in_specs += [ANY, ANY]
        args += [in_hbm(x) for x in saved]
    cells = (LAYERS, MID * LANES)
    lines = [pltpu.VMEM(cells, jnp.int32), pltpu.VMEM(cells, f32)] if first_iteration else []
    return pl.pallas_call(
        functools.partial(rows_body, first_iteration),
        out_shape=outs,
        in_specs=in_specs,
        out_specs=out_specs,
        scratch_shapes=[
            pltpu.VMEM((BAND_TILES + 1, RHS, TILE), f32),
            pltpu.VMEM(state, f32),
            pltpu.VMEM(state, f32),
            pltpu.VMEM(coefs, f32),
            pltpu.VMEM((EXT + 2, 2, 8, LANES), f32),
            pltpu.VMEM((EXT, RHS, LANES), f32),
            pltpu.SemaphoreType.DMA((2,)),
            pltpu.VMEM((SLOTS, TILE, TILE), bf16),
            pltpu.SemaphoreType.DMA((SLOTS,)),
            pltpu.VMEM((WIN_TILES, RHS, TILE), bf16),
            pltpu.VMEM((CHIPS, 2, RHS, TILE), bf16),
            pltpu.SemaphoreType.DMA((CHIPS,)),
            *lines,
        ],
        compiler_params=pltpu.CompilerParams(vmem_limit_bytes=44 * MIB),
        cost_estimate=pl.CostEstimate(flops=7 * 10**8, transcendentals=0, bytes_accessed=30 * 10**6),
        name="into_rows_first" if first_iteration else "into_rows_next",
    )(*args)


def share_body(parts_ref, out_ref):
    share = parts_ref[0].astype(f32)
    for peer in range(1, N_ROW):
        share = share + parts_ref[peer].astype(f32)
    out_ref[...] = share


def window_share(parts):
    return pl.pallas_call(
        share_body,
        out_shape=jax.ShapeDtypeStruct(parts.shape[1:], f32),
        in_specs=[VMEM],
        out_specs=VMEM,
        compiler_params=pltpu.CompilerParams(vmem_limit_bytes=6 * MIB),
        name="window_share",
    )(parts)


def pair_body(scal_ref, own_ref, got_ref, share_ref, got_share_ref, out_ref):
    for chip in range(1, CHIPS):
        out_ref[chip] = (own_ref[chip] + got_ref[chip].astype(f32)).astype(bf16)
    total = own_ref[0] + got_ref[0].astype(f32)
    share = share_ref[...] + got_share_ref[...]
    out_ref[0] = (total + jnp.where(scal_ref[SLOTS + 6] == 0, share, 0.0)).astype(bf16)


def pair_sum(scal, own, got, share, got_share):
    return pl.pallas_call(
        pair_body,
        out_shape=jax.ShapeDtypeStruct(got.shape, bf16),
        in_specs=[SMEM, VMEM, VMEM, VMEM, VMEM],
        out_specs=VMEM,
        compiler_params=pltpu.CompilerParams(vmem_limit_bytes=6 * MIB),
        name="pair_sum",
    )(scal, own, got, share, got_share)


def update_body(last, parts_ref, trace_ref, load_ref, *outs):
    for half in range(2):
        lanes = slice(half * TILE, (half + 1) * TILE)
        total = parts_ref[0, half].astype(f32)
        for peer in range(1, CHIPS):
            total = total + parts_ref[peer, half].astype(f32)
        trace = trace_ref[:, lanes]
        trace = trace + COUPLING_STEP * (load_ref[:, lanes] - trace - total)
        outs[0][:, lanes] = trace
        if last:
            outs[1][:, lanes] = total
        else:
            rounded = trace.astype(bf16)
            for copy in range(CHIPS):
                outs[1][copy, half] = rounded


def update(parts, traces, load, last):
    whole = jax.ShapeDtypeStruct(traces.shape, f32)
    return pl.pallas_call(
        functools.partial(update_body, last),
        out_shape=[whole, whole if last else jax.ShapeDtypeStruct(parts.shape, bf16)],
        in_specs=[VMEM, VMEM, VMEM],
        out_specs=[VMEM, VMEM],
        compiler_params=pltpu.CompilerParams(vmem_limit_bytes=8 * MIB),
        name="update_last" if last else "update_next",
    )(parts, traces, load)


def volume_edges(coef_index, vol_source, volume_line):
    indices = lax.dynamic_index_in_dim(coef_index, volume_line, 0, keepdims=False)
    source = lax.dynamic_index_in_dim(vol_source, volume_line, 0, keepdims=False)

    def ends(x):
        return jnp.concatenate([x[:, :LANES], x[:, -LANES:]], 1)

    high = ends(source).astype(bf16)
    low = (ends(source) - high.astype(f32)).astype(bf16)
    edges = [jnp.pad(e, ((0, 4), (0, 0))) for e in (ends(indices).astype(bf16), high, low)]
    return jnp.pad(jnp.concatenate(edges, 0), ((0, 8), (0, 0)))


def local(
    trace_start, surface_load, panel_tiles, tile_list, surf_map, coef_index, coef_table, vol_source
):
    col_index = lax.axis_index("col")
    row_index = lax.axis_index("row")
    volume_line = jnp.maximum(col_index - DENSE_COLS, 0)
    is_volume = col_index >= DENSE_COLS
    volume_tile = volume_line * N_ROW + row_index
    tile_numbers = jnp.arange(surf_map.shape[0], dtype=jnp.int32)
    quarter = jnp.sum(jnp.where(surf_map == volume_tile, tile_numbers, 0)) % 4
    core = col_index % CORES
    own = [
        is_volume,
        jnp.where(is_volume, 4 * quarter, core),
        jnp.where(is_volume, 4 * quarter + 3, core),
        quarter,
        row_index,
        core,
        core,
        jnp.where(is_volume, 1 - core, core),
        volume_line,
    ]
    scal = jnp.concatenate([tile_list, jnp.stack([x.astype(jnp.int32) for x in own])])
    traces = trace_start
    spread = spread_start(traces)
    edges = volume_edges(coef_index, vol_source, volume_line)
    panel = in_hbm(panel_tiles)
    saved = None
    for iteration in range(ITERS):
        last = iteration == ITERS - 1
        near = between_chips(spread)
        far = from_mate(near)
        near, far = near.reshape(TILES, RHS, TILE), far.reshape(TILES, RHS, TILE)
        row_spread = spread_row(scal, near, far, edges if iteration == 0 else None)
        win = exchange(row_spread, "row")
        win_part = into_window(scal, near, far, panel)
        win, _ = lax.optimization_barrier((win, win_part))
        mate_win = from_mate(win)
        parts = exchange(win_part, "row")
        own, mate, *saved = into_rows(
            scal, near, far, win, mate_win, panel, coef_table, coef_index, vol_source, saved
        )
        got = from_mate(mate)
        share = window_share(parts)
        summed = between_chips(pair_sum(scal, own, got, share, from_mate(share)))
        traces, spread = update(summed, traces, surface_load, last)
    return (traces, spread)


def solution(mesh):
    return jax.shard_map(
        local,
        mesh=mesh,
        in_specs=(
            P(None, ("col", "row")),
            P(None, ("col", "row")),
            P(("col", "row"), None, None),
            P(("col", "row")),
            P(),
            P(None, None, "row"),
            P(),
            P(None, None, "row"),
        ),
        out_specs=(P(None, ("col", "row")), P(None, ("col", "row"))),
        check_vma=False,
    )
```
